32 devices in a mesh: dp: 8 (over y, x, core), tensor: 4 (over z).
Axes of the slice: x: 2, y: 2, z: 4, core: 2. Of those that a mesh axis runs over, the one named last changes fastest.
Arguments:
- tokens: bfloat16 [8, 1024, 2048], P('dp', 'tensor'), may hold values from -6 to 6
- lengths: int32 [8], P('dp'), may hold values from 512 to 1024, as said below
- routes: int32 [8, 1024, 8], P('dp'), may hold values from 0 to 31, all different within a row; in each aligned block of 256 rows (0 to 255, 256 to 511, ..., all dimensions but the last counted through in order) at most 80 rows name the same one
- attn_gain: float32 [2048], replicated, may hold values from 0.5 to 1.5
- w_query: bfloat16 [2048, 2048], P(None, 'tensor'), may hold values from -0.125 to 0.125
- w_key: bfloat16 [2048, 2048], P(None, 'tensor'), may hold values from -0.125 to 0.125
- w_value: bfloat16 [2048, 2048], P(None, 'tensor'), may hold values from -0.125 to 0.125
- w_out: bfloat16 [2048, 2048], P(None, 'tensor'), may hold values from -2 to 2
- q_gain: float32 [128], replicated, may hold values from 0.5 to 1.5
- k_gain: float32 [128], replicated, may hold values from 0.5 to 1.5
- ffn_gain: float32 [2048], replicated, may hold values from 0.5 to 1.5
- router_weight: bfloat16 [2048, 32], replicated, may hold values from -0.0625 to 0.0625
- w_gate: bfloat16 [32, 2048, 1024], P('dp', None, 'tensor'), may hold values from -0.125 to 0.125
- w_up: bfloat16 [32, 2048, 1024], P('dp', None, 'tensor'), may hold values from -0.125 to 0.125
- w_down: bfloat16 [32, 1024, 2048], P('dp', 'tensor'), may hold values from -6 to 6
- cotangent: bfloat16 [8, 1024, 2048], P('dp'), may hold values from -6 to 6
Outputs:
- output: bfloat16 [8, 1024, 2048], P('dp', 'tensor')
- grad_tokens: bfloat16 [8, 1024, 2048], P('dp', 'tensor')
- grad_attn_gain: float32 [2048], P('dp')
- grad_query: float32 [2048, 2048], P('dp', 'tensor')
- grad_key: float32 [2048, 2048], P('dp', 'tensor')
- grad_value: float32 [2048, 2048], P('dp', 'tensor')
- grad_out: float32 [2048, 2048], P('dp', 'tensor')
- grad_q_gain: float32 [128], P('dp')
- grad_k_gain: float32 [128], P('dp')
- grad_ffn_gain: float32 [2048], P('dp')
- grad_router: float32 [2048, 32], P('dp')
- grad_gate: float32 [32, 2048, 1024], P('dp', None, 'tensor')
- grad_up: float32 [32, 2048, 1024], P('dp', None, 'tensor')
- grad_down: float32 [32, 1024, 2048], P('dp', 'tensor')
The draws below stay inside these ranges and needn't reach their ends.
Inputs may be any that keep to these rules, and one draw needn't show every extreme that they name: `lengths`: at least one sequence has all 1024 positions valid. `routes`: in each aligned block of 256 positions (one sequence's positions on one index of tensor) an expert is named by at most 80 rows, and by exactly 80 in some blocks.
All inputs are finite; a program needn't handle non-finite values.
Results may differ from the reference program's by a relative error of at most 0.029.
Values may be sent and summed in bfloat16 or wider, within the bound.
A program may use at most 320 MiB of HBM per device.

```python
import math
import jax
import jax.numpy as jnp
import numpy as np
from jax import lax

D = 2048
HEADS = 16
HEAD_DIM = 128
FF = 1024
TOPK = 8
SEQ_LEN = 1024
EXPERTS = 32
NSEQ = 8
ROWS_DEV = 256
CAPACITY = 80
N_TENSOR = 4


def draw_lengths(key, part):
    base = jax.random.randint(jax.random.fold_in(key, 11), (NSEQ,), SEQ_LEN // 2, SEQ_LEN + 1)
    chosen = jax.random.randint(jax.random.fold_in(key, 12), (), 0, NSEQ)
    return jnp.where(jnp.arange(NSEQ) == chosen, SEQ_LEN, base).astype(jnp.int32)


def shard_levels(key, extent, cuts, least, top_value):
    def one(axis_at, shards_of):
        steps = jax.random.uniform(jax.random.fold_in(jax.random.fold_in(key, 6), axis_at), (shards_of,), jnp.float32, least / len(cuts), top_value / len(cuts))
        return jnp.repeat(jnp.exp(steps), extent[axis_at] // shards_of).reshape((-1,) + (1,) * (len(extent) - axis_at - 1))

    level = one(*cuts[0])
    for cut in cuts[1:]:
        level = level * one(*cut)
    return level


def assign_block(key, own, number, rows, number_of, top, limit, skew):
    order = jax.random.permutation(key, number_of)
    heavy_load, ordinary = load_shares(number_of, rows * top, limit, skew, True), load_shares(number_of, rows * top, limit, skew, False)
    places = jnp.arange(number_of)

    def named(tallies, offset_by):
        used = int((tallies > 0).sum())
        fixed = max(1, used // 4)
        shifted = fixed + (places - fixed + offset_by * (used - fixed)) % max(1, number_of - fixed)
        return jnp.zeros((number_of,), jnp.int32).at[order[jnp.where(places < fixed, places, shifted)]].set(jnp.asarray(tallies, jnp.int32))

    tallies = jnp.where(number % 4 == 0, named(heavy_load, number // 4), named(ordinary, number - number // 4 - 1))
    mixed = jax.random.permutation(jax.random.fold_in(own, 3), number_of)
    donor, sink = mixed[0:number_of // 2 * 2:2], mixed[1:number_of // 2 * 2:2]
    room = jnp.minimum(tallies[donor] - 1, limit - tallies[sink]) // 2
    room = jnp.where((donor == order[0]) | (sink == order[0]) | (tallies[sink] == 0), 0, jnp.maximum(room, 0))
    shifted = jax.random.randint(jax.random.fold_in(own, 4), (number_of // 2,), 0, 1 << 20) % (room + 1)
    tallies = tallies.at[donor].add(-shifted).at[sink].add(shifted)
    labels = jnp.searchsorted(jnp.cumsum(tallies), jnp.arange(rows * top), side="right").astype(jnp.int32)
    listing = labels.reshape(top, rows).T
    listing = listing[jax.random.permutation(jax.random.fold_in(own, 1), rows)]
    offset_by = jax.random.randint(jax.random.fold_in(own, 2), (rows, 1), 0, top)
    return jnp.take_along_axis(listing, (jnp.arange(top)[None, :] + offset_by) % top, axis=1)


def load_shares(number_of, total, limit, skew, full):
    portions = [(1 << 20) // math.isqrt(standing ** skew) + 1 for standing in range(1, number_of + 1)]
    largest = limit if full else min(limit, max(-(-total // number_of), total * portions[0] // sum(portions)))
    least = 1 if total - largest >= number_of - 1 else 0
    holding, surplus = [largest] + [least] * (number_of - 1), total - largest - least * (number_of - 1)
    while surplus > 0:
        movable = [i for i in range(1, number_of) if holding[i] < largest] or [i for i in range(1, number_of) if holding[i] < limit]
        pool, budget = sum([portions[i] for i in movable]), surplus
        for i in movable:
            addition = min(limit - holding[i], max(1, budget * portions[i] // pool), surplus)
            holding[i] = holding[i] + addition
            surplus = surplus - addition
    return np.array(holding)


def scatter_about(key, shape, deviation, bound, shards=(), kind=jnp.bfloat16):
    array = jax.random.normal(key, shape, jnp.float32) * deviation
    if len(shards) > 0:
        array = shard_levels(key, shape, shards, -0.22, 0.18) * array
    return jnp.clip(array, min=-bound, max=bound).astype(kind)


def setup_inputs(seed: int = 0) -> dict:
    arg_keys = jax.random.split(jax.random.key(seed), 17)
    tokens = scatter_about(arg_keys[0], (NSEQ, SEQ_LEN, D), 1.0, 6.0, ((0, 8), (1, 4)))
    lengths = draw_lengths(jax.random.fold_in(arg_keys[16], 71), 0)
    routes_keys = jax.random.split(jax.random.fold_in(arg_keys[2], 1), NSEQ * SEQ_LEN // ROWS_DEV)
    routes_turns = jax.random.permutation(jax.random.fold_in(arg_keys[2], 3), NSEQ * SEQ_LEN // ROWS_DEV)
    routes = jax.vmap(lambda own, number: assign_block(jax.random.fold_in(arg_keys[2], 2), own, number, ROWS_DEV, EXPERTS, TOPK, CAPACITY, 1))(routes_keys, routes_turns).reshape((NSEQ, SEQ_LEN, TOPK))
    attn_gain = jnp.clip(1.0 + 0.1 * jax.random.normal(arg_keys[3], (D,), jnp.float32), 0.5, 1.5)
    w_query = scatter_about(arg_keys[4], (D, HEADS * HEAD_DIM), D ** -0.5, 0.125, ((1, 4),))
    w_key = scatter_about(arg_keys[5], (D, HEADS * HEAD_DIM), D ** -0.5, 0.125, ((1, 4),))
    w_value = scatter_about(arg_keys[6], (D, HEADS * HEAD_DIM), D ** -0.5, 0.125, ((1, 4),))
    w_out = scatter_about(arg_keys[7], (D, HEADS * HEAD_DIM), (max(1, HEADS * HEAD_DIM // 256)) ** -0.5, 2.0, ((1, 4),))
    q_gain = jnp.clip(1.0 + 0.1 * jax.random.normal(arg_keys[8], (HEAD_DIM,), jnp.float32), 0.5, 1.5)
    k_gain = jnp.clip(1.0 + 0.1 * jax.random.normal(arg_keys[9], (HEAD_DIM,), jnp.float32), 0.5, 1.5)
    ffn_gain = jnp.clip(1.0 + 0.1 * jax.random.normal(arg_keys[10], (D,), jnp.float32), 0.5, 1.5)
    router_weight = scatter_about(arg_keys[11], (D, EXPERTS), (4 * D) ** -0.5, 0.0625)
    w_gate = scatter_about(arg_keys[12], (EXPERTS, D, FF), D ** -0.5, 0.125, ((0, 8), (2, 4)))
    w_up = scatter_about(arg_keys[13], (EXPERTS, D, FF), D ** -0.5, 0.125, ((0, 8), (2, 4)))
    w_down = scatter_about(arg_keys[14], (EXPERTS, FF, D), 1.0, 6.0, ((0, 8), (1, 4)))
    cotangent = scatter_about(arg_keys[15], (NSEQ, SEQ_LEN, D), 1.0, 6.0, ((0, 8),))
    return {"tokens": tokens, "lengths": lengths, "routes": routes, "attn_gain": attn_gain, "w_query": w_query, "w_key": w_key, "w_value": w_value, "w_out": w_out, "q_gain": q_gain, "k_gain": k_gain, "ffn_gain": ffn_gain, "router_weight": router_weight, "w_gate": w_gate, "w_up": w_up, "w_down": w_down, "cotangent": cotangent}


EPS = 1e-06
THETA = 50000.0
NEG = -1e+30
BEST_PRECISION = lax.Precision.HIGHEST

@jax.custom_vjp
def low(v):
    return lax.optimization_barrier(v.astype(jnp.bfloat16)).astype(jnp.float32)

@jax.custom_vjp
def lowered_pullback(v):
    return v

def low_keep(v):
    return (low(v), None)

def lowered_forward(kept, grad):
    return (grad,)

def back_keep(v):
    return (v, None)

def back_low(kept, grad):
    return (low(grad),)
low.defvjp(low_keep, lowered_forward)
lowered_pullback.defvjp(back_keep, back_low)

def rms_scale(values, gain):
    return values * lax.rsqrt(lax.optimization_barrier(jnp.mean(values * values, axis=-1, keepdims=True)) + EPS) * gain

def rotate(values):
    length = values.shape[-3]
    half_dim = values.shape[-1] // 2
    positions = jnp.arange(length).astype(jnp.float32)
    rates = THETA ** (-jnp.arange(half_dim).astype(jnp.float32) / half_dim)
    angles = positions[:, None] * rates[None, :]
    cosine = jnp.cos(angles)[:, None, :]
    sine = jnp.sin(angles)[:, None, :]
    first = values[..., :half_dim]
    second = values[..., half_dim:]
    return jnp.concatenate([first * cosine - second * sine, second * cosine + first * sine], axis=-1)

def prepare(raw, gain):
    shaped = raw.reshape(raw.shape[0], -1, gain.shape[0])
    return rotate(rms_scale(shaped, gain))

def dispatch_tables(routes):
    blocks = NSEQ * N_TENSOR
    pairs = ROWS_DEV * TOPK
    pair_expert = routes.reshape(blocks, pairs).astype(jnp.int32)
    onehot = (pair_expert[:, :, None] == jnp.arange(EXPERTS).astype(jnp.int32)[None, None, :]).astype(jnp.int32)
    slots = lax.optimization_barrier(jnp.sum((jnp.cumsum(onehot, axis=1) - 1) * onehot, axis=2)).astype(jnp.int32)
    block_ids = jnp.broadcast_to(jnp.arange(blocks).astype(jnp.int32)[:, None], (blocks, pairs))
    pair_ids = jnp.broadcast_to(jnp.arange(pairs).astype(jnp.int32)[None, :], (blocks, pairs))
    table = jnp.full((EXPERTS, blocks, CAPACITY), pairs, jnp.int32)
    table = table.at[pair_expert, block_ids, slots].set(pair_ids)
    block_base = jnp.arange(blocks).astype(jnp.int32)[None, :, None]
    token_rows = jnp.where(table < pairs, block_base * ROWS_DEV + table // TOPK, blocks * ROWS_DEV)
    route_index = pair_expert * (blocks * CAPACITY) + block_ids * CAPACITY + slots
    return (token_rows.reshape(EXPERTS, blocks * CAPACITY).astype(jnp.int32), route_index.reshape(NSEQ, SEQ_LEN, TOPK).astype(jnp.int32))

def reference(tokens, lengths, routes, attn_gain, w_query, w_key, w_value, w_out, q_gain, k_gain, ffn_gain, router_weight, w_gate, w_up, w_down, cotangent):
    token_rows, route_index = dispatch_tables(routes)
    valid = (jnp.arange(SEQ_LEN).astype(jnp.int32)[None, :] < lengths[:, None]).astype(jnp.float32)
    scale = HEAD_DIM ** (-0.5)

    def forward(token_values, attn_gain, w_query, w_key, w_value, w_out, q_gain, k_gain, ffn_gain, router_weight, w_gate, w_up, w_down):
        normed = low(rms_scale(token_values, attn_gain))

        def attend(inputs):
            sequence, length = inputs
            query_unrotated = lowered_pullback(jnp.einsum('ld,dh->lh', sequence, w_query, precision=BEST_PRECISION))
            key_raw = lowered_pullback(jnp.einsum('ld,dh->lh', sequence, w_key, precision=BEST_PRECISION))
            value_raw = lowered_pullback(jnp.einsum('ld,dh->lh', sequence, w_value, precision=BEST_PRECISION))
            query = low(prepare(query_unrotated, q_gain))
            keys = low(prepare(key_raw, k_gain))
            values = low(value_raw).reshape(SEQ_LEN, HEADS, HEAD_DIM)
            key_mask = jnp.arange(SEQ_LEN).astype(jnp.int32) < length
            scores = lowered_pullback(jnp.einsum('qhd,khd->hqk', query, keys, precision=BEST_PRECISION) * scale)
            scores = jnp.where(key_mask[None, None, :], scores, NEG)
            probs = low(jax.nn.softmax(scores, axis=-1))
            mixed = low(lowered_pullback(jnp.einsum('hqk,khd->qhd', probs, values, precision=BEST_PRECISION)))
            mixed = mixed.reshape(SEQ_LEN, HEADS * HEAD_DIM)
            return lowered_pullback(jnp.einsum('lh,dh->ld', mixed, w_out, precision=BEST_PRECISION))
        attended = lax.map(jax.checkpoint(attend), (normed, lengths))
        hidden = token_values + valid[:, :, None] * attended
        expert_layer_input = low(rms_scale(hidden, ffn_gain))
        router_logits = lowered_pullback(jnp.einsum('iwr,rf->iwf', expert_layer_input, router_weight, precision=BEST_PRECISION))
        router_probs = jax.nn.softmax(router_logits, axis=-1)
        picked = jnp.take_along_axis(router_probs, routes, axis=-1) * valid[:, :, None]
        padded = jnp.concatenate([expert_layer_input.reshape(NSEQ * SEQ_LEN, D), jnp.zeros((1, D), jnp.float32)], axis=0)

        def expert(inputs):
            rows_index, gate_matrix, up_matrix, down_matrix = inputs
            rows = lowered_pullback(padded[rows_index])
            gate = lowered_pullback(jnp.einsum('rd,df->rf', rows, gate_matrix, precision=BEST_PRECISION))
            up_value = lowered_pullback(jnp.einsum('rd,df->rf', rows, up_matrix, precision=BEST_PRECISION))
            activation = low(jax.nn.silu(gate) * up_value)
            return low(lowered_pullback(jnp.einsum('rf,fd->rd', activation, down_matrix, precision=BEST_PRECISION)))
        results = lax.map(jax.checkpoint(expert), (token_rows, w_gate, w_up, w_down))
        results = results.reshape(EXPERTS * NSEQ * N_TENSOR * CAPACITY, D)

        def combine(inputs):
            index, weight = inputs
            return jnp.einsum('lk,lkd->ld', weight, results[index], precision=BEST_PRECISION)
        mixed_experts = lax.map(jax.checkpoint(combine), (route_index, picked))
        return hidden + mixed_experts
    output, pullback = jax.vjp(forward, tokens.astype(jnp.float32), attn_gain, w_query.astype(jnp.float32), w_key.astype(jnp.float32), w_value.astype(jnp.float32), w_out.astype(jnp.float32), q_gain, k_gain, ffn_gain, router_weight.astype(jnp.float32), w_gate.astype(jnp.float32), w_up.astype(jnp.float32), w_down.astype(jnp.float32))
    grads = pullback(cotangent.astype(jnp.float32))
    return (output.astype(jnp.bfloat16), grads[0].astype(jnp.bfloat16), grads[1], grads[2], grads[3], grads[4], grads[5], grads[6], grads[7], grads[8], grads[9], grads[10], grads[11], grads[12])
```

```python
import functools

import jax
import jax.numpy as jnp
from jax import lax
from jax.experimental import pallas as pl
from jax.experimental.pallas import tpu as pltpu
from jax.sharding import PartitionSpec as P

EPS = 1e-06
THETA = 50000.0
NEG = -1e30


def rms_scale(values, gain):
    return values * lax.rsqrt(jnp.mean(values * values, axis=-1, keepdims=True) + EPS) * gain


def rotate(values):
    length = values.shape[-3]
    half_dim = values.shape[-1] // 2
    positions = jnp.arange(length).astype(jnp.float32)
    rates = THETA ** (-jnp.arange(half_dim).astype(jnp.float32) / half_dim)
    angles = positions[:, None] * rates[None, :]
    cosine = jnp.cos(angles)[:, None, :]
    sine = jnp.sin(angles)[:, None, :]
    first = values[..., :half_dim]
    second = values[..., half_dim:]
    return jnp.concatenate(
        [first * cosine - second * sine, second * cosine + first * sine], axis=-1
    )


def prepare(raw, gain):
    shaped = raw.reshape(raw.shape[0], -1, gain.shape[0])
    return rotate(rms_scale(shaped, gain))


def dot_nt(a, b):
    return lax.dot_general(a, b, (((1,), (1,)), ((), ())), preferred_element_type=jnp.float32)


def dot_nn(a, b):
    return jnp.dot(a, b, preferred_element_type=jnp.float32)


def largest_tile(total, limit, unit):
    best = unit
    for tile in range(unit, limit + 1, unit):
        if total % tile == 0:
            best = tile
    return best


def expert_kernel(
    sizes,
    first,
    table_ref,
    x_ref,
    c_ref,
    pick_ref,
    wg_ref,
    wu_ref,
    wd_ref,
    *rest,
):
    blocks, experts, slots, rows, width, extra, hidden, all_experts = sizes
    if first:
        acc_in = None
        y0_ref, y1_ref, g0_ref, g1_ref, acc_out = rest[:5]
        scratch = rest[5:]
    else:
        acc_in, y0_ref, y1_ref, g0_ref, g1_ref, acc_out = rest[:6]
        scratch = rest[6:]
    rows_s, crow_s, mrow_s, meta_s, aw_s, gg_s, gu_s, turn_s, acc_s, load_sem, store_sem = scratch
    step = pl.program_id(0)
    total = blocks * slots
    half = blocks // 2

    def load(e, slot):
        return pltpu.make_async_copy(acc_in.at[e], acc_s.at[slot], load_sem.at[slot])

    def store(e, slot):
        return pltpu.make_async_copy(acc_s.at[slot], acc_out.at[e], store_sem.at[slot])

    if not first:

        @pl.when(step == 0)
        def _():
            load(0, 0).start()

    @pl.when(step < blocks)
    def _():
        meta = x_ref[0, :, width:]
        picks = (dot_nt(pick_ref[...], meta) == 0.0).astype(jnp.bfloat16)
        at = pl.multiple_of(step * slots, slots)
        got = dot_nn(picks, x_ref[0]).astype(jnp.bfloat16)
        cot = dot_nn(picks, c_ref[0]).astype(jnp.bfloat16)
        for e in range(experts):
            part = slice(e * slots, (e + 1) * slots)
            rows_s[e, pl.ds(at, slots), :] = got[part, :width]
            mrow_s[e, pl.ds(at, slots), :] = got[part, width:]
            crow_s[e, pl.ds(at, slots), :] = cot[part]
        meta_s[step] = meta

    @pl.when((step >= blocks) & (step < blocks + experts))
    def _():
        e = step - blocks
        slot = lax.rem(e, 2)
        tile = largest_tile(total, 320, 16)
        expert = table_ref[0] + e
        wg = wg_ref[0]
        wu = wu_ref[0]
        wd = wd_ref[0]

        @pl.loop(0, total // tile)
        def _(m):
            ds = pl.ds(pl.multiple_of(m * tile, tile), tile)
            picked_rows = rows_s[e, ds, :]
            gate = dot_nn(picked_rows, wg)
            up = dot_nn(picked_rows, wu)
            grad_act = dot_nt(crow_s[e, ds, :], wd)
            meta = mrow_s[e, ds, :].astype(jnp.float32)
            column = lax.broadcasted_iota(jnp.int32, meta.shape, 1)
            wanted = (column == expert) | (column == expert + all_experts)
            weight = jnp.sum(jnp.where(wanted, meta, 0.0), axis=1, keepdims=True)
            sig = jax.nn.sigmoid(gate)
            silu = gate * sig
            act = silu * up
            g_pick = jnp.sum(act * grad_act, axis=1, keepdims=True)
            scaled = weight * grad_act
            aw_s[ds, :] = (weight * act).astype(jnp.bfloat16)
            gg_s[ds, :] = (scaled * up * sig * (1.0 + gate * (1.0 - sig))).astype(jnp.bfloat16)
            gu_s[ds, :] = (scaled * silu).astype(jnp.bfloat16)
            mrow_s[e, ds, :] = jnp.where(column == expert, g_pick, 0.0).astype(jnp.bfloat16)

        if not first:
            load(e, slot).wait()

            @pl.when(e >= 1)
            def _():
                store(e - 1, 1 - slot).wait()

            @pl.when(e + 1 < experts)
            def _():
                load(e + 1, 1 - slot).start()

        else:

            @pl.when(e >= 2)
            def _():
                store(e - 2, slot).wait()

        cols = largest_tile(width, 512, 128)
        for which, (left, right) in enumerate(((gg_s, rows_s), (gu_s, rows_s), (aw_s, crow_s))):
            turn_s[...] = left[...].T

            @pl.loop(0, width // cols)
            def _(n):
                ds = pl.ds(pl.multiple_of(n * cols, cols), cols)
                add = dot_nn(turn_s[...], right[e, :, ds])
                if first:
                    acc_s[slot, which, :, ds] = add
                else:
                    acc_s[slot, which, :, ds] = acc_s[slot, which, :, ds] + add

        store(e, slot).start()

        @pl.loop(0, total // tile)
        def _(m):
            ds = pl.ds(pl.multiple_of(m * tile, tile), tile)
            crow_s[e, ds, :] = dot_nn(aw_s[ds, :], wd).astype(jnp.bfloat16)
            back = dot_nt(gg_s[ds, :], wg) + dot_nt(gu_s[ds, :], wu)
            rows_s[e, ds, :] = back.astype(jnp.bfloat16)

    @pl.when(step >= blocks + experts)
    def _():
        order = step - blocks - experts
        b = table_ref[2 + blocks + jnp.where(order < half, order + half, order - half)]
        at = pl.multiple_of(b * slots, slots)
        picks = (dot_nt(meta_s[b], pick_ref[...]) == 0.0).astype(jnp.bfloat16)
        flat = (experts * slots, width)
        y = dot_nn(picks, crow_s[:, pl.ds(at, slots), :].reshape(flat)).astype(jnp.bfloat16)
        g = dot_nn(picks, rows_s[:, pl.ds(at, slots), :].reshape(flat)).astype(jnp.bfloat16)
        flat = (experts * slots, extra)
        p = dot_nn(picks, mrow_s[:, pl.ds(at, slots), :].reshape(flat)).astype(jnp.bfloat16)

        @pl.when(order < half)
        def _():
            y1_ref[0] = y
            g1_ref[0, :, :width] = g
            g1_ref[0, :, width:] = p

        @pl.when(order >= half)
        def _():
            y0_ref[0] = y
            g0_ref[0, :, :width] = g
            g0_ref[0, :, width:] = p

    @pl.when(step == 2 * blocks + experts - 1)
    def _():
        if first:
            store(experts - 2, (experts - 2) % 2).wait()
        store(experts - 1, (experts - 1) % 2).wait()


def expert_chunk(table, x, c, picks, wg, wu, wd, acc, slots, all_experts):
    blocks, rows, full = x.shape
    width = c.shape[2]
    extra = full - width
    experts, _, hidden = wg.shape
    total = blocks * slots
    half = blocks // 2
    first = acc is None
    sizes = (blocks, experts, slots, rows, width, extra, hidden, all_experts)

    def clip(v, top):
        return jnp.clip(v, 0, top)

    def block_at(i, table):
        return (jnp.minimum(i, blocks - 1), 0, 0)

    def cot_at(i, table):
        return (table[2 + jnp.minimum(i, blocks - 1)], table[1], 0)

    def expert_at(i, table):
        return (clip(i - blocks, experts - 1), 0, 0)

    def late(i, table):
        return (clip(i - blocks - experts, half - 1), 0, 0)

    def early(i, table):
        return (clip(i - blocks - experts - half, half - 1), 0, 0)

    in_specs = [
        pl.BlockSpec((1, rows, full), block_at),
        pl.BlockSpec((1, rows, width), cot_at),
        pl.BlockSpec(picks.shape, lambda i, table: (0, 0)),
        pl.BlockSpec((1, width, hidden), expert_at),
        pl.BlockSpec((1, width, hidden), expert_at),
        pl.BlockSpec((1, hidden, width), expert_at),
    ]
    args = [table, x, c, picks, wg, wu, wd]
    if not first:
        in_specs.append(pl.BlockSpec(memory_space=pl.ANY))
        args.append(acc)
    out_specs = [
        pl.BlockSpec((1, rows, width), early),
        pl.BlockSpec((1, rows, width), late),
        pl.BlockSpec((1, rows, full), early),
        pl.BlockSpec((1, rows, full), late),
        pl.BlockSpec(memory_space=pl.ANY),
    ]
    out_shape = [
        jax.ShapeDtypeStruct((half, rows, width), jnp.bfloat16),
        jax.ShapeDtypeStruct((half, rows, width), jnp.bfloat16),
        jax.ShapeDtypeStruct((half, rows, full), jnp.bfloat16),
        jax.ShapeDtypeStruct((half, rows, full), jnp.bfloat16),
        jax.ShapeDtypeStruct((experts, 3, hidden, width), jnp.float32),
    ]
    scratch = [
        pltpu.VMEM((experts, total, width), jnp.bfloat16),
        pltpu.VMEM((experts, total, width), jnp.bfloat16),
        pltpu.VMEM((experts, total, extra), jnp.bfloat16),
        pltpu.VMEM((blocks, rows, extra), jnp.bfloat16),
        pltpu.VMEM((total, hidden), jnp.bfloat16),
        pltpu.VMEM((total, hidden), jnp.bfloat16),
        pltpu.VMEM((total, hidden), jnp.bfloat16),
        pltpu.VMEM((hidden, total), jnp.bfloat16),
        pltpu.VMEM((2, 3, hidden, width), jnp.float32),
        pltpu.SemaphoreType.DMA((2,)),
        pltpu.SemaphoreType.DMA((2,)),
    ]
    flops = 2 * experts * total * width * (hidden * 9 + 4 * rows)
    return pl.pallas_call(
        functools.partial(expert_kernel, sizes, first),
        grid_spec=pltpu.PrefetchScalarGridSpec(
            num_scalar_prefetch=1,
            grid=(2 * blocks + experts,),
            in_specs=in_specs,
            out_specs=out_specs,
            scratch_shapes=scratch,
        ),
        out_shape=out_shape,
        input_output_aliases={} if first else {7: 4},
        compiler_params=pltpu.CompilerParams(
            dimension_semantics=("arbitrary",), vmem_limit_bytes=66_000_000
        ),
        cost_estimate=pl.CostEstimate(
            flops=flops, bytes_accessed=4 * blocks * rows * full * 2 + 40_000_000, transcendentals=0
        ),
        name="experts",
    )(*args)


def wide(values):
    return values.astype(jnp.float32)


def low(values):
    return values.astype(jnp.bfloat16)


def tie(*values):
    return lax.optimization_barrier(values)


def ring_sum(values, count):
    total = wide(values)
    for step in range(1, count):
        pairs = [(i, (i + step) % count) for i in range(count)]
        total = total + wide(lax.ppermute(low(values), "tensor", pairs))
    return total


class Plane:
    def __init__(self, count):
        self.outer = count // 4
        everyone = range(count)
        self.core = [(i, i ^ 1) for i in everyone]
        self.inner = [(i, i ^ 2) for i in everyone]
        self.count = count

    def pull(self, values, k):
        pairs = [((i + 4 * k) % self.count, i) for i in range(self.count)]
        return lax.ppermute(values, "dp", pairs)

    def push(self, values, k):
        pairs = [(i, (i + 4 * k) % self.count) for i in range(self.count)]
        return lax.ppermute(values, "dp", pairs)

    def swap_inner(self, values):
        return lax.ppermute(values, "dp", self.inner)

    def swap_core(self, values):
        return lax.ppermute(values, "dp", self.core)

    def gather(self, own):
        half = own.shape[0] // 2
        near = self.swap_inner(own)
        far = [self.pull(own, k) for k in range(1, self.outer)]
        mine = [own, near]
        for k in range(1, self.outer):
            top = self.pull(near[:half], k)
            bottom = self.swap_inner(far[k - 1][half:])
            mine += [far[k - 1], jnp.concatenate([top, bottom], axis=0)]
        other = [self.swap_core(part) for part in mine]
        return mine + other

    def fold_core(self, same, other):
        return low(wide(same) + wide(self.swap_core(other)))

    def fold_diagonal(self, both):
        half = both.shape[1] // 2
        near = wide(both[1])
        fars = []
        for k in range(1, self.outer):
            diagonal = both[2 * k + 1]
            top = self.push(diagonal[:half], k)
            bottom = self.swap_inner(diagonal[half:])
            near = near + wide(jnp.concatenate([top, jnp.zeros_like(top)], axis=0))
            fars.append(
                low(wide(both[2 * k]) + wide(jnp.concatenate([jnp.zeros_like(bottom), bottom], axis=0)))
            )
        return both[0], low(near), fars

    def fold_rest(self, own, near, fars):
        total = wide(own) + wide(self.swap_inner(near))
        for k, far in enumerate(fars):
            total = total + wide(self.push(far, k + 1))
        return total

    def tables(self):
        here = lax.axis_index("dp")
        outer, rest = here // 4, lax.rem(here, 4)
        core, inner = lax.rem(rest, 2), rest // 2
        half = self.count // 2
        place = jnp.arange(self.count)
        k, b, c = place // 4, place // 2 % 2, place % 2
        to_relative = (c ^ core) * half + lax.rem(k - outer + self.outer, self.outer) * 2 + (b ^ inner)
        c, k, b = place // half, place % half // 2, place % 2
        to_absolute = lax.rem(k + outer, self.outer) * 4 + (b ^ inner) * 2 + (c ^ core)
        return to_relative.astype(jnp.int32), to_absolute.astype(jnp.int32)


def per_device(
    tokens,
    lengths,
    routes,
    attn_gain,
    w_query,
    w_key,
    w_value,
    w_out,
    q_gain,
    k_gain,
    ffn_gain,
    router_weight,
    w_gate,
    w_up,
    w_down,
    cotangent,
):
    tensor_count = lax.axis_size("tensor")
    data_count = lax.axis_size("dp")
    tensor_rank = lax.axis_index("tensor")
    block_rows = tokens.shape[1]
    width = tokens.shape[2]
    full_length = block_rows * tensor_count
    route_count = routes.shape[2]
    local_experts = w_gate.shape[0]
    all_experts = local_experts * data_count
    head_dim = q_gain.shape[0]
    local_width = w_query.shape[1]
    capacity = max(2, (block_rows * route_count * 5 + 4 * all_experts - 1) // (4 * all_experts))
    query_rows = min(512, full_length)
    scale = head_dim ** (-0.5)
    own_start = tensor_rank * block_rows
    token_values = tokens[0].astype(jnp.float32)
    seq_length = lengths[0]
    own_valid = (own_start + jnp.arange(block_rows) < seq_length).astype(jnp.float32)
    key_valid = jnp.arange(full_length) < seq_length
    normed = rms_scale(token_values, attn_gain).astype(jnp.bfloat16)
    gathered = lax.all_gather(normed, "tensor", axis=0, tiled=True)
    plane = Plane(data_count)
    cot_all = jnp.stack(plane.gather(cotangent[0]))
    query_unrotated = jnp.dot(gathered, w_query, preferred_element_type=jnp.float32)
    key_raw = jnp.dot(gathered, w_key, preferred_element_type=jnp.float32)
    value_raw = jnp.dot(gathered, w_value, preferred_element_type=jnp.float32)
    query_low = prepare(query_unrotated, q_gain).astype(jnp.bfloat16)
    key_low = prepare(key_raw, k_gain).astype(jnp.bfloat16)
    value_low = value_raw.astype(jnp.bfloat16).reshape(full_length, -1, head_dim)

    def block_scores(query_block):
        scores = (
            jnp.einsum("qhd,khd->hqk", query_block, key_low, preferred_element_type=jnp.float32)
            * scale
        )
        return jnp.where(key_valid[None, None, :], scores, NEG)

    mixed_parts = []
    log_totals = []
    for start in range(0, full_length, query_rows):
        scores = block_scores(query_low[start : start + query_rows])
        row_peak = jnp.max(scores, axis=-1, keepdims=True)
        powers = jnp.exp(scores - row_peak)
        total = jnp.sum(powers, axis=-1, keepdims=True)
        weights = (powers / total).astype(jnp.bfloat16)
        mixed_parts.append(
            jnp.einsum("hqk,khd->qhd", weights, value_low, preferred_element_type=jnp.float32)
        )
        log_totals.append(row_peak + jnp.log(total))
    attended = (
        jnp.concatenate(mixed_parts, axis=0).reshape(full_length, local_width).astype(jnp.bfloat16)
    )
    attn_own = lax.psum_scatter(
        jnp.einsum("lh,dh->ld", attended, w_out, preferred_element_type=jnp.float32).astype(
            jnp.bfloat16
        ),
        "tensor",
        scatter_dimension=0,
        tiled=True,
    ).astype(jnp.float32)
    residual = token_values + own_valid[:, None] * attn_own
    moe_own = rms_scale(residual, ffn_gain).astype(jnp.bfloat16)
    router_logits = jnp.dot(moe_own, router_weight, preferred_element_type=jnp.float32)
    own_probs = jax.nn.softmax(router_logits, axis=-1)
    own_routes = lax.dynamic_slice_in_dim(routes[0], own_start, block_rows, 0)
    onehot = own_routes[:, :, None] == jnp.arange(all_experts)[None, None, :]
    named = jnp.any(onehot, axis=1) & (own_valid[:, None] > 0.0)
    named_low = named.astype(jnp.bfloat16)
    before = jnp.arange(block_rows)[:, None] > jnp.arange(block_rows)[None, :]
    order = jnp.dot(before.astype(jnp.bfloat16), named_low, preferred_element_type=jnp.float32)
    place = jnp.where(named, order, -1.0).astype(jnp.bfloat16)
    weight = jnp.where(named, own_probs, 0.0)
    weight_high = weight.astype(jnp.bfloat16)
    weight_low = (weight - weight_high.astype(jnp.float32)).astype(jnp.bfloat16)
    used = 3 * all_experts + 1
    extra = (used + 127) // 128 * 128
    meta = jnp.concatenate(
        [
            weight_high,
            weight_low,
            place,
            jnp.ones((block_rows, 1), jnp.bfloat16),
            jnp.zeros((block_rows, extra - used), jnp.bfloat16),
        ],
        axis=1,
    )
    slots = (capacity + 15) // 16 * 16
    first_expert = lax.axis_index("dp") * local_experts
    slot_row = jnp.arange(local_experts * slots)[:, None]
    slot_column = jnp.arange(extra)[None, :]
    picks = jnp.where(
        slot_column == 2 * all_experts + first_expert + slot_row // slots,
        1.0,
        jnp.where(slot_column == 3 * all_experts, -(slot_row % slots).astype(jnp.float32), 0.0),
    ).astype(jnp.bfloat16)
    packed = jnp.concatenate([moe_own, meta], axis=1)
    to_relative, to_absolute = plane.tables()
    sums = None
    shift_in = [
        [((i + step) % tensor_count, i) for i in range(tensor_count)] for step in range(tensor_count)
    ]
    shift_out = [
        [(i, (i + step) % tensor_count) for i in range(tensor_count)] for step in range(tensor_count)
    ]
    gathered_rows = [
        lax.all_gather(
            packed if step == 0 else lax.ppermute(packed, "tensor", shift_in[step]), "dp", axis=0
        )
        for step in range(tensor_count)
    ]
    out_parts = []
    cores = {}
    ends = {}
    grad_parts = []
    for step in range(tensor_count):
        x_all = gathered_rows[step]
        if step >= 2:
            x_all, cores[step - 2] = tie(x_all, cores[step - 2])
        if step >= 3:
            x_all, ends[step - 3] = tie(x_all, ends[step - 3])
        here = lax.rem(tensor_rank + step, tensor_count)
        head = jnp.stack([first_expert, here]).astype(jnp.int32)
        table = jnp.concatenate([head, to_relative, to_absolute])
        y0, y1, g0, g1, sums = expert_chunk(
            table, x_all, cot_all, picks, w_gate, w_up, w_down, sums, slots, all_experts
        )
        out_parts.append((y0, y1))
        cores[step] = plane.fold_core(g0, g1)
        if step >= 1:
            ends[step - 1] = plane.fold_diagonal(cores[step - 1])
    ends[tensor_count - 1] = plane.fold_diagonal(cores[tensor_count - 1])
    for step in range(tensor_count):
        part = plane.fold_rest(*ends[step])
        if step > 0:
            part = wide(lax.ppermute(low(part), "tensor", shift_out[step]))
        grad_parts.append(part)
    grad_gate = jnp.swapaxes(sums[:, 0], 1, 2)
    grad_up = jnp.swapaxes(sums[:, 1], 1, 2)
    grad_down = sums[:, 2]
    grad_sum = sum(grad_parts[1:], grad_parts[0])
    grad_moe = grad_sum[:, :width]
    grad_probs = grad_sum[:, width : width + all_experts]
    grad_own = lax.dynamic_slice_in_dim(cotangent[0], own_start, block_rows, 0).astype(jnp.float32)
    grad_logits = (
        own_probs * (grad_probs - jnp.sum(own_probs * grad_probs, axis=-1, keepdims=True))
    ).astype(jnp.bfloat16)
    grad_moe = grad_moe + jnp.einsum(
        "re,de->rd", grad_logits, router_weight, preferred_element_type=jnp.float32
    )
    router_part = jnp.einsum("rd,re->de", moe_own, grad_logits, preferred_element_type=jnp.float32)
    ffn_pull = jax.vjp(rms_scale, residual, ffn_gain)[1]
    grad_res_norm, ffn_part = ffn_pull(grad_moe)
    grad_residual = grad_own + grad_res_norm
    grad_attn = (grad_residual * own_valid[:, None]).astype(jnp.bfloat16)
    out_cores = [plane.fold_core(y0, y1) for y0, y1 in out_parts]
    grad_attn, out_cores = tie(grad_attn, out_cores)
    grad_attn_all = lax.all_gather(grad_attn, "tensor", axis=0, tiled=True)
    out_ends = [plane.fold_diagonal(both) for both in out_cores]
    grad_attn_all, out_ends = tie(grad_attn_all, out_ends)
    grad_mixed = jnp.dot(grad_attn_all, w_out, preferred_element_type=jnp.float32).astype(
        jnp.bfloat16
    )
    grad_mixed = grad_mixed.reshape(full_length, -1, head_dim)
    out_part = jnp.einsum("ld,lh->dh", grad_attn_all, attended, preferred_element_type=jnp.float32)
    grad_query_parts = []
    grad_keys = jnp.zeros(key_low.shape, jnp.float32)
    grad_values = jnp.zeros(value_low.shape, jnp.float32)
    for order, start in enumerate(range(0, full_length, query_rows)):
        query_block = query_low[start : start + query_rows]
        grad_block = grad_mixed[start : start + query_rows]
        probs_block = jnp.exp(block_scores(query_block) - log_totals[order])
        probs_low = probs_block.astype(jnp.bfloat16)
        grad_values = grad_values + jnp.einsum(
            "hqk,qhd->khd", probs_low, grad_block, preferred_element_type=jnp.float32
        )
        grad_probs_block = jnp.einsum(
            "qhd,khd->hqk", grad_block, value_low, preferred_element_type=jnp.float32
        )
        delta = jnp.sum(probs_block * grad_probs_block, axis=-1, keepdims=True)
        grad_scores = (probs_block * (grad_probs_block - delta)).astype(jnp.bfloat16)
        grad_query_parts.append(
            jnp.einsum("hqk,khd->qhd", grad_scores, key_low, preferred_element_type=jnp.float32)
            * scale
        )
        grad_keys = (
            grad_keys
            + jnp.einsum(
                "hqk,qhd->khd", grad_scores, query_block, preferred_element_type=jnp.float32
            )
            * scale
        )
    grad_queries = jnp.concatenate(grad_query_parts, axis=0)
    query_pull = jax.vjp(prepare, query_unrotated, q_gain)[1]
    grad_query_raw, q_part = query_pull(grad_queries)
    key_pull = jax.vjp(prepare, key_raw, k_gain)[1]
    grad_key_raw, k_part = key_pull(grad_keys)
    grad_q_low = grad_query_raw.astype(jnp.bfloat16)
    grad_k_low = grad_key_raw.astype(jnp.bfloat16)
    grad_v_low = grad_values.reshape(full_length, local_width).astype(jnp.bfloat16)
    query_part = jnp.einsum("ld,lh->dh", gathered, grad_q_low, preferred_element_type=jnp.float32)
    key_part = jnp.einsum("ld,lh->dh", gathered, grad_k_low, preferred_element_type=jnp.float32)
    value_part = jnp.einsum("ld,lh->dh", gathered, grad_v_low, preferred_element_type=jnp.float32)
    from_query = jnp.einsum("lh,dh->ld", grad_q_low, w_query, preferred_element_type=jnp.float32)
    from_key = jnp.einsum("lh,dh->ld", grad_k_low, w_key, preferred_element_type=jnp.float32)
    from_value = jnp.einsum("lh,dh->ld", grad_v_low, w_value, preferred_element_type=jnp.float32)
    output = residual
    for step in range(tensor_count):
        part = plane.fold_rest(*out_ends[step])
        if step > 0:
            part = wide(lax.ppermute(low(part), "tensor", shift_out[step]))
        output = output + part
    output = low(output)
    early = jnp.concatenate(
        [
            low(out_part),
            low(value_part),
            low(ring_sum(jnp.concatenate([router_part, ffn_part[:, None]], axis=1), tensor_count)),
        ],
        axis=1,
    )
    early = wide(lax.psum_scatter(early, "dp", scatter_dimension=0, tiled=True))
    grad_normed = wide(
        lax.psum_scatter(
            low(from_query + from_key + from_value), "tensor", scatter_dimension=0, tiled=True
        )
    )
    attn_pull = jax.vjp(rms_scale, token_values, attn_gain)[1]
    grad_tok_norm, attn_part = attn_pull(grad_normed)
    grad_tokens = (grad_residual + grad_tok_norm).astype(jnp.bfloat16)
    piece = head_dim // data_count
    gains = jnp.stack([q_part, k_part]).reshape(2, data_count, piece)
    gains = jnp.pad(gains, ((0, 0), (0, 0), (0, width // data_count - piece)))
    small = jnp.concatenate([attn_part[:, None], gains.reshape(2, width).T], axis=1)
    late = jnp.concatenate(
        [low(query_part), low(key_part), low(ring_sum(small, tensor_count))], axis=1
    )
    late = wide(lax.psum_scatter(late, "dp", scatter_dimension=0, tiled=True))
    end = 2 * local_width
    return (
        output[None],
        grad_tokens[None],
        late[:, end],
        late[:, :local_width],
        late[:, local_width:end],
        early[:, local_width:end],
        early[:, :local_width],
        late[:piece, end + 1],
        late[:piece, end + 2],
        early[:, end + all_experts],
        early[:, end : end + all_experts],
        grad_gate,
        grad_up,
        grad_down,
    )


def solution(mesh):
    return jax.shard_map(
        per_device,
        mesh=mesh,
        in_specs=(
            P("dp", "tensor", None),
            P("dp"),
            P("dp", None, None),
            P(),
            P(None, "tensor"),
            P(None, "tensor"),
            P(None, "tensor"),
            P(None, "tensor"),
            P(),
            P(),
            P(),
            P(),
            P("dp", None, "tensor"),
            P("dp", None, "tensor"),
            P("dp", "tensor", None),
            P("dp", None, None),
        ),
        out_specs=(
            P("dp", "tensor", None),
            P("dp", "tensor", None),
            P("dp"),
            P("dp", "tensor"),
            P("dp", "tensor"),
            P("dp", "tensor"),
            P("dp", "tensor"),
            P("dp"),
            P("dp"),
            P("dp"),
            P("dp", None),
            P("dp", None, "tensor"),
            P("dp", None, "tensor"),
            P("dp", "tensor", None),
        ),
        check_vma=False,
    )
```

```python
import functools

import jax
import jax.numpy as jnp
from jax import lax
from jax.experimental import pallas as pl
from jax.experimental.pallas import tpu as pltpu
from jax.sharding import PartitionSpec as P

EPS = 1e-06
THETA = 50000.0
NEG = -1e30


def rms_scale(values, gain):
    return values * lax.rsqrt(jnp.mean(values * values, axis=-1, keepdims=True) + EPS) * gain


def rotate(values):
    length = values.shape[-3]
    half_dim = values.shape[-1] // 2
    positions = jnp.arange(length).astype(jnp.float32)
    rates = THETA ** (-jnp.arange(half_dim).astype(jnp.float32) / half_dim)
    angles = positions[:, None] * rates[None, :]
    cosine = jnp.cos(angles)[:, None, :]
    sine = jnp.sin(angles)[:, None, :]
    first = values[..., :half_dim]
    second = values[..., half_dim:]
    return jnp.concatenate(
        [first * cosine - second * sine, second * cosine + first * sine], axis=-1
    )


def prepare(raw, gain):
    shaped = raw.reshape(raw.shape[0], -1, gain.shape[0])
    return rotate(rms_scale(shaped, gain))


def dot_nt(a, b):
    return lax.dot_general(a, b, (((1,), (1,)), ((), ())), preferred_element_type=jnp.float32)


def dot_nn(a, b):
    return jnp.dot(a, b, preferred_element_type=jnp.float32)


def largest_tile(total, limit, unit):
    best = unit
    for tile in range(unit, limit + 1, unit):
        if total % tile == 0:
            best = tile
    return best


def moe_kernel(
    sizes,
    own_ref,
    cot_ref,
    pick_ref,
    wg_ref,
    wu_ref,
    wd_ref,
    final_ref,
    acc_ref,
    mine_ref,
    gather_ref,
    other_ref,
    both_ref,
    core_in,
    top_in,
    bottom_in,
    near_in,
    far_in,
    ring_out,
    ring_in,
    in_s,
    out_s,
    rows_s,
    crow_s,
    mrow_s,
    meta_s,
    aw_s,
    gg_s,
    gu_s,
    turn_s,
    acc_s,
    load_sem,
    store_sem,
    x_sem,
    c_sem,
    out_sem,
    fold_sem,
    plane_send,
    plane_recv,
    sum_send,
    sum_recv,
    ring_send,
    ring_recv,
    last_send,
    last_recv,
):
    outer, chunks, experts, slots, rows, width, extra, all_experts = sizes
    blocks, half, cut = 4 * outer, 2 * outer, rows // 2
    full = width + extra
    span = full + width
    total = blocks * slots
    ring = gather_ref.shape[0]
    j = pl.program_id(0)
    s = pl.program_id(1)
    steps = 2 * blocks + experts
    me = lax.axis_index("dp")
    z = lax.axis_index("tensor")
    a, rest = me // 4, me % 4
    inner_id = me + 2 - 4 * ((me // 2) % 2)
    core_id = me + 1 - 2 * (me % 2)
    upper, lower = pl.ds(0, cut), pl.ds(cut, cut)
    x_part, y_part = pl.ds(0, full), pl.ds(full, width)

    def outer_id(k):
        return ((a + k + outer) % outer) * 4 + rest

    def remote(src, dst, send, recv, where, axis="dp"):
        return pltpu.make_async_remote_copy(
            src_ref=src,
            dst_ref=dst,
            send_sem=send,
            recv_sem=recv,
            device_id={axis: where},
            device_id_type=pl.DeviceIdType.MESH,
        )

    def plane_copy(c, src, dst, rows_at, ident, where):
        first = isinstance(src, int) and src == 0
        near = src if isinstance(src, int) else dst
        source = mine_ref.at[c] if first else gather_ref.at[c % ring, near - 1]
        target = gather_ref.at[c % ring, dst - 1]
        if rows_at is not None:
            source, target = source.at[rows_at], target.at[rows_at]
        return remote(source, target, plane_send.at[c, ident], plane_recv.at[c, ident], where)

    def near_copy(c):
        return plane_copy(c, 0, 1, None, 0, inner_id)

    def far_copy(c, k):
        return plane_copy(c, 0, 2 * k, None, k, outer_id(-k))

    def top_copy(c, k):
        return plane_copy(c, 1, 2 * k + 1, upper, outer - 1 + k, outer_id(-k))

    def bottom_copy(c, k):
        return plane_copy(c, 2 * k, 2 * k + 1, lower, 2 * outer - 2 + k, inner_id)

    def core_copy(c, q):
        return plane_copy(c, q, half + q, None, 3 * outer - 2 + q, core_id)

    def ring_copy(k):
        where = (z - k + chunks) % chunks
        return remote(own_ref, mine_ref.at[k], ring_send.at[k], ring_recv.at[k], where, "tensor")

    others = range(1, outer)

    def first_hop(c):
        near_copy(c).start()
        for k in others:
            far_copy(c, k).start()
        core_copy(c, 0).start()

    def second_hop(c):
        near_copy(c).wait_recv()
        for k in others:
            top_copy(c, k).start()
        for k in others:
            far_copy(c, k).wait_recv()
            bottom_copy(c, k).start()
        for q in [1] + [2 * k for k in others]:
            core_copy(c, q).start()

    def third_hop(c):
        for k in others:
            top_copy(c, k).wait_recv()
            bottom_copy(c, k).wait_recv()
            core_copy(c, 2 * k + 1).start()

    def drain_gather(c):
        near_copy(c).wait_send()
        for k in others:
            far_copy(c, k).wait_send()
            top_copy(c, k).wait_send()
            bottom_copy(c, k).wait_send()
        for q in range(half):
            core_copy(c, q).wait_send()

    def sum_copy(c, src, dst, ident, where):
        return remote(src, dst, sum_send.at[c, ident], sum_recv.at[c, ident], where)

    def swap_copy(c, q):
        return sum_copy(c, other_ref.at[c % 2, q], core_in.at[c % 2, q], q, core_id)

    def both_at(c, q, rows_at):
        return both_ref.at[c % 2, q, rows_at]

    def up_copy(c, k):
        ident = half + k - 1
        return sum_copy(c, both_at(c, 2 * k + 1, upper), top_in.at[c % 2, k - 1], ident, outer_id(k))

    def down_copy(c, k):
        ident = half + outer - 1 + k - 1
        source = both_at(c, 2 * k + 1, lower)
        return sum_copy(c, source, bottom_in.at[c % 2, k - 1], ident, inner_id)

    def home_near(c, part):
        rows_at = (upper, lower)[part]
        ident = half + 2 * outer - 2 + part
        return sum_copy(c, both_at(c, 1, rows_at), near_in.at[c % 2, rows_at], ident, inner_id)

    def home_far(c, k, part):
        rows_at = (upper, lower)[part]
        ident = half + 2 * outer + 2 * (k - 1) + part
        target = far_in.at[c % 2, k - 1, rows_at]
        return sum_copy(c, both_at(c, 2 * k, rows_at), target, ident, outer_id(k))

    def last_copy(c):
        where = (z + c) % chunks
        return remote(ring_out.at[c], ring_in.at[c], last_send.at[c], last_recv.at[c], where, "tensor")

    def local(src, dst, sem):
        return pltpu.make_async_copy(src, dst, sem)

    def together(*copies):
        for copy in copies:
            copy.start()
        for copy in copies:
            copy.wait()

    def fold_halves(c):
        for k in others:
            up_copy(c, k).wait_recv()
            down_copy(c, k).wait_recv()
            copies = [
                local(both_at(c, 2 * k, lower), in_s.at[0, lower], fold_sem.at[0]),
                local(top_in.at[c % 2, k - 1], in_s.at[1, upper], fold_sem.at[1]),
                local(bottom_in.at[c % 2, k - 1], in_s.at[1, lower], fold_sem.at[2]),
            ]
            if k == 1:
                copies.append(local(both_at(c, 1, upper), in_s.at[0, upper], fold_sem.at[3]))
            together(*copies)

            @pl.loop(0, rows // 16)
            def _(i):
                at = pl.ds(pl.multiple_of(i * 16, 16), 16)
                in_s[0, at, :] = low(wide(in_s[0, at, :]) + wide(in_s[1, at, :]))

            together(local(in_s.at[0, lower], both_at(c, 2 * k, lower), fold_sem.at[0]))
        together(local(in_s.at[0, upper], both_at(c, 1, upper), fold_sem.at[0]))
        for k in others:
            home_far(c, k, 1).start()
        home_near(c, 0).start()

    def fold_home(c):
        for part in (0, 1):
            home_near(c, part).wait_recv()
        together(
            local(both_ref.at[c % 2, 0], in_s.at[0], fold_sem.at[0]),
            local(near_in.at[c % 2], in_s.at[1], fold_sem.at[1]),
        )

        @pl.loop(0, rows // 16)
        def _(i):
            at = pl.ds(pl.multiple_of(i * 16, 16), 16)
            in_s[0, at, :] = low(wide(in_s[0, at, :]) + wide(in_s[1, at, :]))

        for k in others:
            for part in (0, 1):
                home_far(c, k, part).wait_recv()
            together(local(far_in.at[c % 2, k - 1], in_s.at[1], fold_sem.at[1]))

            @pl.loop(0, rows // 16)
            def _(i):
                at = pl.ds(pl.multiple_of(i * 16, 16), 16)
                in_s[0, at, :] = low(wide(in_s[0, at, :]) + wide(in_s[1, at, :]))

        together(local(in_s.at[0], ring_out.at[c], fold_sem.at[0]))

    def drain_sum(c):
        for q in range(half):
            swap_copy(c, q).wait_send()
        for k in others:
            up_copy(c, k).wait_send()
            down_copy(c, k).wait_send()
            for part in (0, 1):
                home_far(c, k, part).wait_send()
        for part in (0, 1):
            home_near(c, part).wait_send()

    def fetch(c, at):
        q, side, slot = at // 2, at % 2, at % 2
        r = side * half + q

        @pl.when(side == 1)
        def _():
            core_copy(c, q).wait_recv()

        rows_at = pl.ds(pl.multiple_of(((z + c) % chunks) * rows, rows), rows)
        @pl.when(r == 0)
        def _():
            local(mine_ref.at[c], in_s.at[slot, :, x_part], x_sem.at[slot]).start()

        @pl.when(r > 0)
        def _():
            source = gather_ref.at[c % ring, jnp.maximum(r - 1, 0)]
            local(source, in_s.at[slot, :, x_part], x_sem.at[slot]).start()

        local(cot_ref.at[r, rows_at], in_s.at[slot, :, y_part], c_sem.at[slot]).start()

    def fetched(slot):
        local(mine_ref.at[0], in_s.at[slot, :, x_part], x_sem.at[slot]).wait()
        local(cot_ref.at[0, pl.ds(0, rows)], in_s.at[slot, :, y_part], c_sem.at[slot]).wait()

    def load(e, slot):
        return local(acc_ref.at[e], acc_s.at[slot], load_sem.at[slot])

    def store(e, slot):
        return local(acc_s.at[slot], acc_ref.at[e], store_sem.at[slot])

    @pl.when((j == 0) & (s == 0))
    def _():
        barrier = pltpu.get_barrier_semaphore()
        peers = [("dp", core_id), ("dp", inner_id)] + [("dp", outer_id(k)) for k in others]
        peers += [("tensor", (z + k) % chunks) for k in range(1, chunks)]
        for axis, where in peers:
            pl.semaphore_signal(
                barrier, inc=1, device_id={axis: where}, device_id_type=pl.DeviceIdType.MESH
            )
        pl.semaphore_wait(barrier, len(peers))
        for k in range(1, chunks):
            ring_copy(k).start()
        together(local(own_ref, in_s.at[0, :, x_part], fold_sem.at[0]))
        together(local(in_s.at[0, :, x_part], mine_ref.at[0], fold_sem.at[0]))
        first_hop(0)
        fetch(0, 0)
        second_hop(0)
        ring_copy(1).wait_recv()
        first_hop(1)

    @pl.when((s == 0) & (j > 0))
    def _():
        load(0, 0).start()

    @pl.when((j == 0) & (s == 4))
    def _():
        third_hop(0)

    @pl.when((s == blocks + 1) & (j + 1 < chunks))
    def _():
        second_hop(j + 1)

    @pl.when((s == blocks + experts) & (j + 1 < chunks))
    def _():
        third_hop(j + 1)

    @pl.when((s == blocks + 2) & (j >= 1))
    def _():
        fold_halves(j - 1)

    @pl.when((s == blocks + 2) & (j + 2 < chunks))
    def _():
        ring_copy(j + 2).wait_recv()
        first_hop(j + 2)

    @pl.when(s == blocks + 3)
    def _():
        drain_gather(j)

    @pl.when((s == blocks + experts + half - 1) & (j >= 1))
    def _():
        fold_home(j - 1)

        @pl.when(j >= 2)
        def _():
            last_copy(j - 1).start()

        drain_sum(j - 1)

    @pl.when(s < blocks)
    def _():
        slot = s % 2

        @pl.when(s + 1 < blocks)
        def _():
            fetch(j, s + 1)

        fetched(slot)
        meta = in_s[slot, :, width:full]
        picks = (dot_nt(pick_ref[...], meta) == 0.0).astype(jnp.bfloat16)
        at = pl.multiple_of(s * slots, slots)
        got = low(dot_nn(picks, in_s[slot, :, :full]))
        cot = low(dot_nn(picks, in_s[slot, :, full:]))
        for e in range(experts):
            part = slice(e * slots, (e + 1) * slots)
            rows_s[e, pl.ds(at, slots), :] = got[part, :width]
            mrow_s[e, pl.ds(at, slots), :] = got[part, width:]
            crow_s[e, pl.ds(at, slots), :] = cot[part]
        meta_s[s] = meta

    @pl.when((s >= blocks) & (s < blocks + experts))
    def _():
        e = s - blocks
        slot = e % 2
        tile = largest_tile(total, 320, 16)
        expert = me * experts + e
        wg = wg_ref[0]
        wu = wu_ref[0]
        wd = wd_ref[0]

        @pl.loop(0, total // tile)
        def _(m):
            ds = pl.ds(pl.multiple_of(m * tile, tile), tile)
            picked_rows = rows_s[e, ds, :]
            gate = dot_nn(picked_rows, wg)
            up = dot_nn(picked_rows, wu)
            grad_act = dot_nt(crow_s[e, ds, :], wd)
            meta = wide(mrow_s[e, ds, :])
            column = lax.broadcasted_iota(jnp.int32, meta.shape, 1)
            wanted = (column == expert) | (column == expert + all_experts)
            weight = jnp.sum(jnp.where(wanted, meta, 0.0), axis=1, keepdims=True)
            sig = jax.nn.sigmoid(gate)
            silu = gate * sig
            act = silu * up
            g_pick = jnp.sum(act * grad_act, axis=1, keepdims=True)
            scaled = weight * grad_act
            aw_s[ds, :] = low(weight * act)
            gg_s[ds, :] = low(scaled * up * sig * (1.0 + gate * (1.0 - sig)))
            gu_s[ds, :] = low(scaled * silu)
            mrow_s[e, ds, :] = low(jnp.where(column == expert, g_pick, 0.0))

        @pl.when(e >= 1)
        def _():
            store(e - 1, 1 - slot).wait()

        @pl.when(j == 0)
        def _():
            acc_s[slot] = jnp.zeros(acc_s.shape[1:], jnp.float32)

        @pl.when(j > 0)
        def _():
            load(e, slot).wait()

            @pl.when(e + 1 < experts)
            def _():
                load(e + 1, 1 - slot).start()

        cols = largest_tile(width, 512, 128)
        for which, (left, right) in enumerate(((gg_s, rows_s), (gu_s, rows_s), (aw_s, crow_s))):
            turn_s[...] = left[...].T

            @pl.loop(0, width // cols)
            def _(n):
                ds = pl.ds(pl.multiple_of(n * cols, cols), cols)
                add = dot_nn(turn_s[...], right[e, :, ds])
                acc_s[slot, which, :, ds] = acc_s[slot, which, :, ds] + add

        store(e, slot).start()

        @pl.loop(0, total // tile)
        def _(m):
            ds = pl.ds(pl.multiple_of(m * tile, tile), tile)
            crow_s[e, ds, :] = low(dot_nn(aw_s[ds, :], wd))
            rows_s[e, ds, :] = low(dot_nt(gg_s[ds, :], wg) + dot_nt(gu_s[ds, :], wu))

    first = blocks + experts

    def written(c, o):
        q, slot = half - 1 - o % half, o % 2

        @pl.when(o < half)
        def _():
            local(out_s.at[slot], other_ref.at[c % 2, q], out_sem.at[slot]).wait()
            swap_copy(c, q).start()

        @pl.when(o >= half)
        def _():
            local(out_s.at[slot], both_ref.at[c % 2, q], out_sem.at[slot]).wait()

        for k in others:

            @pl.when((o >= half) & (q == 2 * k + 1))
            def _():
                up_copy(c, k).start()
                down_copy(c, k).start()

            @pl.when((o >= half) & (q == 2 * k))
            def _():
                home_far(c, k, 0).start()

        @pl.when((o >= half) & (q == 1))
        def _():
            home_near(c, 1).start()

    @pl.when(s >= first)
    def _():
        o = s - first
        slot = o % 2
        q = half - 1 - o % half
        side = 1 - o // half
        place = 2 * q + side
        at = pl.multiple_of(place * slots, slots)

        @pl.when(o >= 1)
        def _():
            written(j, o - 1)

        @pl.when((o >= half - 1) & (o < 2 * half - 1))
        def _():
            coming = half - 1 - (o + 1) % half
            swap_copy(j, coming).wait_recv()
            local(core_in.at[j % 2, coming], in_s.at[1 - slot], x_sem.at[1 - slot]).start()

        @pl.when(o >= half)
        def _():
            local(core_in.at[j % 2, q], in_s.at[slot], x_sem.at[slot]).wait()

        @pl.when(o < half)
        def _():
            in_s[slot] = jnp.zeros((rows, span), jnp.bfloat16)

        picks = (dot_nt(meta_s[place], pick_ref[...]) == 0.0).astype(jnp.bfloat16)
        flat = (experts * slots, width)
        g = dot_nn(picks, rows_s[:, pl.ds(at, slots), :].reshape(flat))
        out_s[slot, :, :width] = low(g + wide(in_s[slot, :, :width]))
        flat = (experts * slots, extra)
        p = dot_nn(picks, mrow_s[:, pl.ds(at, slots), :].reshape(flat))
        out_s[slot, :, width:full] = low(p + wide(in_s[slot, :, width:full]))
        flat = (experts * slots, width)
        y = dot_nn(picks, crow_s[:, pl.ds(at, slots), :].reshape(flat))
        out_s[slot, :, full:] = low(y + wide(in_s[slot, :, full:]))

        @pl.when(o < half)
        def _():
            local(out_s.at[slot], other_ref.at[j % 2, q], out_sem.at[slot]).start()

        @pl.when(o >= half)
        def _():
            local(out_s.at[slot], both_ref.at[j % 2, q], out_sem.at[slot]).start()

        @pl.when(s == steps - 1)
        def _():
            written(j, o)
            store(experts - 1, (experts - 1) % 2).wait()

        @pl.when((s == steps - 1) & (j + 1 < chunks))
        def _():
            fetch(j + 1, 0)

    @pl.when((s == steps - 1) & (j == chunks - 1))
    def _():
        fold_halves(chunks - 1)
        fold_home(chunks - 1)
        last_copy(chunks - 1).start()
        drain_sum(chunks - 1)
        together(local(ring_out.at[0], in_s.at[0], fold_sem.at[0]))
        for k in range(1, chunks):
            last_copy(k).wait_recv()
            together(local(ring_in.at[k], in_s.at[1], fold_sem.at[1]))

            @pl.loop(0, rows // 16)
            def _(i):
                at = pl.ds(pl.multiple_of(i * 16, 16), 16)
                in_s[0, at, :] = low(wide(in_s[0, at, :]) + wide(in_s[1, at, :]))

        together(local(in_s.at[0], final_ref, fold_sem.at[0]))
        for k in range(1, chunks):
            last_copy(k).wait_send()
            ring_copy(k).wait_send()


def moe(own, cot, picks, wg, wu, wd, outer, chunks, slots, all_experts):
    rows, full = own.shape
    width = cot.shape[2]
    extra = full - width
    span = full + width
    experts, _, hidden = wg.shape
    blocks, half, cut = 4 * outer, 2 * outer, rows // 2
    total = blocks * slots
    sizes = (outer, chunks, experts, slots, rows, width, extra, all_experts)

    def expert_at(j, s):
        return (jnp.clip(s - blocks, 0, experts - 1), 0, 0)

    anywhere = pl.BlockSpec(memory_space=pl.ANY)
    in_specs = [
        anywhere,
        anywhere,
        pl.BlockSpec(picks.shape, lambda j, s: (0, 0)),
        pl.BlockSpec((1, width, hidden), expert_at),
        pl.BlockSpec((1, width, hidden), expert_at),
        pl.BlockSpec((1, hidden, width), expert_at),
    ]
    bf16 = jnp.bfloat16
    shapes = [
        ((rows, span), bf16),
        ((experts, 3, hidden, width), jnp.float32),
        ((chunks, rows, full), bf16),
        ((chunks if chunks <= 4 else 3, blocks - 1, rows, full), bf16),
        ((2, half, rows, span), bf16),
        ((2, half, rows, span), bf16),
        ((2, half, rows, span), bf16),
        ((2, outer - 1, cut, span), bf16),
        ((2, outer - 1, cut, span), bf16),
        ((2, rows, span), bf16),
        ((2, outer - 1, rows, span), bf16),
        ((chunks, rows, span), bf16),
        ((chunks, rows, span), bf16),
    ]
    dma = pltpu.SemaphoreType.DMA
    gathers, sums = 5 * outer - 2, 6 * outer - 2
    scratch = [
        pltpu.VMEM((2, rows, span), bf16),
        pltpu.VMEM((2, rows, span), bf16),
        pltpu.VMEM((experts, total, width), bf16),
        pltpu.VMEM((experts, total, width), bf16),
        pltpu.VMEM((experts, total, extra), bf16),
        pltpu.VMEM((blocks, rows, extra), bf16),
        pltpu.VMEM((total, hidden), bf16),
        pltpu.VMEM((total, hidden), bf16),
        pltpu.VMEM((total, hidden), bf16),
        pltpu.VMEM((hidden, total), bf16),
        pltpu.VMEM((2, 3, hidden, width), jnp.float32),
        dma((2,)),
        dma((2,)),
        dma((2,)),
        dma((2,)),
        dma((2,)),
        dma((4,)),
        dma((chunks, gathers)),
        dma((chunks, gathers)),
        dma((chunks, sums)),
        dma((chunks, sums)),
        dma((chunks,)),
        dma((chunks,)),
        dma((chunks,)),
        dma((chunks,)),
    ]
    flops = 2 * chunks * experts * total * width * (hidden * 9 + 4 * rows)
    results = pl.pallas_call(
        functools.partial(moe_kernel, sizes),
        grid=(chunks, 2 * blocks + experts),
        in_specs=in_specs,
        out_specs=[anywhere] * len(shapes),
        out_shape=[jax.ShapeDtypeStruct(*shape) for shape in shapes],
        scratch_shapes=scratch,
        compiler_params=pltpu.CompilerParams(
            dimension_semantics=("arbitrary", "arbitrary"),
            vmem_limit_bytes=66_500_000,
            collective_id=0,
            has_side_effects=True,
        ),
        cost_estimate=pl.CostEstimate(
            flops=flops, bytes_accessed=blocks * chunks * rows * full * 8, transcendentals=0
        ),
        name="moe",
    )(own, cot, picks, wg, wu, wd)
    return results[:2]


def wide(values):
    return values.astype(jnp.float32)


def low(values):
    return values.astype(jnp.bfloat16)


def tie(*values):
    return lax.optimization_barrier(values)


def ring_sum(values, count):
    total = wide(values)
    for step in range(1, count):
        pairs = [(i, (i + step) % count) for i in range(count)]
        total = total + wide(lax.ppermute(low(values), "tensor", pairs))
    return total


class Plane:
    def __init__(self, count):
        self.outer = count // 4
        everyone = range(count)
        self.core = [(i, i ^ 1) for i in everyone]
        self.inner = [(i, i ^ 2) for i in everyone]
        self.count = count

    def pull(self, values, k):
        pairs = [((i + 4 * k) % self.count, i) for i in range(self.count)]
        return lax.ppermute(values, "dp", pairs)

    def swap_inner(self, values):
        return lax.ppermute(values, "dp", self.inner)

    def swap_core(self, values):
        return lax.ppermute(values, "dp", self.core)

    def first(self, own):
        return self.swap_inner(own), [self.pull(own, k) for k in range(1, self.outer)]

    def second(self, near, fars):
        half = near.shape[0] // 2
        return [
            jnp.concatenate([self.pull(near[:half], k + 1), self.swap_inner(far[half:])], axis=0)
            for k, far in enumerate(fars)
        ]

    def third(self, own, near, fars, diagonals):
        mine = [own, near]
        for far, diagonal in zip(fars, diagonals):
            mine += [far, diagonal]
        return mine + [self.swap_core(part) for part in mine]


def per_device(
    tokens,
    lengths,
    routes,
    attn_gain,
    w_query,
    w_key,
    w_value,
    w_out,
    q_gain,
    k_gain,
    ffn_gain,
    router_weight,
    w_gate,
    w_up,
    w_down,
    cotangent,
):
    tensor_count = lax.axis_size("tensor")
    data_count = lax.axis_size("dp")
    tensor_rank = lax.axis_index("tensor")
    block_rows = tokens.shape[1]
    width = tokens.shape[2]
    full_length = block_rows * tensor_count
    route_count = routes.shape[2]
    local_experts = w_gate.shape[0]
    all_experts = local_experts * data_count
    head_dim = q_gain.shape[0]
    local_width = w_query.shape[1]
    capacity = max(2, (block_rows * route_count * 5 + 4 * all_experts - 1) // (4 * all_experts))
    query_rows = min(512, full_length)
    scale = head_dim ** (-0.5)
    own_start = tensor_rank * block_rows
    token_values = tokens[0].astype(jnp.float32)
    seq_length = lengths[0]
    own_valid = (own_start + jnp.arange(block_rows) < seq_length).astype(jnp.float32)
    key_valid = jnp.arange(full_length) < seq_length
    normed = rms_scale(token_values, attn_gain).astype(jnp.bfloat16)
    gathered = lax.all_gather(normed, "tensor", axis=0, tiled=True)
    plane = Plane(data_count)
    near, fars = plane.first(cotangent[0])
    gathered, near, fars = tie(gathered, near, fars)
    query_unrotated = jnp.dot(gathered, w_query, preferred_element_type=jnp.float32)
    key_raw = jnp.dot(gathered, w_key, preferred_element_type=jnp.float32)
    value_raw = jnp.dot(gathered, w_value, preferred_element_type=jnp.float32)
    query_low = prepare(query_unrotated, q_gain).astype(jnp.bfloat16)
    key_low = prepare(key_raw, k_gain).astype(jnp.bfloat16)
    value_low = value_raw.astype(jnp.bfloat16).reshape(full_length, -1, head_dim)

    def block_scores(query_block):
        scores = (
            jnp.einsum("qhd,khd->hqk", query_block, key_low, preferred_element_type=jnp.float32)
            * scale
        )
        return jnp.where(key_valid[None, None, :], scores, NEG)

    mixed_parts = []
    log_totals = []
    for start in range(0, full_length, query_rows):
        scores = block_scores(query_low[start : start + query_rows])
        row_peak = jnp.max(scores, axis=-1, keepdims=True)
        powers = jnp.exp(scores - row_peak)
        total = jnp.sum(powers, axis=-1, keepdims=True)
        weights = (powers / total).astype(jnp.bfloat16)
        mixed_parts.append(
            jnp.einsum("hqk,khd->qhd", weights, value_low, preferred_element_type=jnp.float32)
        )
        log_totals.append(row_peak + jnp.log(total))
    attended = (
        jnp.concatenate(mixed_parts, axis=0).reshape(full_length, local_width).astype(jnp.bfloat16)
    )
    diagonals = plane.second(near, fars)
    attended, diagonals = tie(attended, diagonals)
    cot_all = plane.third(cotangent[0], near, fars, diagonals)
    attn_own = lax.psum_scatter(
        jnp.einsum("lh,dh->ld", attended, w_out, preferred_element_type=jnp.float32).astype(
            jnp.bfloat16
        ),
        "tensor",
        scatter_dimension=0,
        tiled=True,
    ).astype(jnp.float32)
    cot_all = jnp.stack(cot_all)
    residual = token_values + own_valid[:, None] * attn_own
    moe_own = rms_scale(residual, ffn_gain).astype(jnp.bfloat16)
    router_logits = jnp.dot(moe_own, router_weight, preferred_element_type=jnp.float32)
    own_probs = jax.nn.softmax(router_logits, axis=-1)
    own_routes = lax.dynamic_slice_in_dim(routes[0], own_start, block_rows, 0)
    onehot = own_routes[:, :, None] == jnp.arange(all_experts)[None, None, :]
    named = jnp.any(onehot, axis=1) & (own_valid[:, None] > 0.0)
    named_low = named.astype(jnp.bfloat16)
    before = jnp.arange(block_rows)[:, None] > jnp.arange(block_rows)[None, :]
    order = jnp.dot(before.astype(jnp.bfloat16), named_low, preferred_element_type=jnp.float32)
    place = jnp.where(named, order, -1.0).astype(jnp.bfloat16)
    weight = jnp.where(named, own_probs, 0.0)
    weight_high = weight.astype(jnp.bfloat16)
    weight_low = (weight - weight_high.astype(jnp.float32)).astype(jnp.bfloat16)
    used = 3 * all_experts + 1
    extra = (used + 127) // 128 * 128
    meta = jnp.concatenate(
        [
            weight_high,
            weight_low,
            place,
            jnp.ones((block_rows, 1), jnp.bfloat16),
            jnp.zeros((block_rows, extra - used), jnp.bfloat16),
        ],
        axis=1,
    )
    slots = (capacity + 15) // 16 * 16
    first_expert = lax.axis_index("dp") * local_experts
    slot_row = jnp.arange(local_experts * slots)[:, None]
    slot_column = jnp.arange(extra)[None, :]
    picks = jnp.where(
        slot_column == 2 * all_experts + first_expert + slot_row // slots,
        1.0,
        jnp.where(slot_column == 3 * all_experts, -(slot_row % slots).astype(jnp.float32), 0.0),
    ).astype(jnp.bfloat16)
    packed = jnp.concatenate([moe_own, meta], axis=1)
    combined, sums = moe(
        packed,
        cot_all,
        picks,
        w_gate,
        w_up,
        w_down,
        data_count // 4,
        tensor_count,
        slots,
        all_experts,
    )
    combined = wide(combined)
    grad_gate = jnp.swapaxes(sums[:, 0], 1, 2)
    grad_up = jnp.swapaxes(sums[:, 1], 1, 2)
    grad_down = sums[:, 2]
    grad_moe = combined[:, :width]
    grad_probs = combined[:, width : width + all_experts]
    output = low(residual + combined[:, width + extra :])
    grad_own = lax.dynamic_slice_in_dim(cotangent[0], own_start, block_rows, 0).astype(jnp.float32)
    grad_logits = (
        own_probs * (grad_probs - jnp.sum(own_probs * grad_probs, axis=-1, keepdims=True))
    ).astype(jnp.bfloat16)
    grad_moe = grad_moe + jnp.einsum(
        "re,de->rd", grad_logits, router_weight, preferred_element_type=jnp.float32
    )
    router_part = jnp.einsum("rd,re->de", moe_own, grad_logits, preferred_element_type=jnp.float32)
    ffn_pull = jax.vjp(rms_scale, residual, ffn_gain)[1]
    grad_res_norm, ffn_part = ffn_pull(grad_moe)
    grad_residual = grad_own + grad_res_norm
    grad_attn = (grad_residual * own_valid[:, None]).astype(jnp.bfloat16)
    grad_attn_all = lax.all_gather(grad_attn, "tensor", axis=0, tiled=True)
    grad_mixed = jnp.dot(grad_attn_all, w_out, preferred_element_type=jnp.float32).astype(
        jnp.bfloat16
    )
    grad_mixed = grad_mixed.reshape(full_length, -1, head_dim)
    out_part = jnp.einsum("ld,lh->dh", grad_attn_all, attended, preferred_element_type=jnp.float32)
    grad_query_parts = []
    grad_keys = jnp.zeros(key_low.shape, jnp.float32)
    grad_values = jnp.zeros(value_low.shape, jnp.float32)
    for order, start in enumerate(range(0, full_length, query_rows)):
        query_block = query_low[start : start + query_rows]
        grad_block = grad_mixed[start : start + query_rows]
        probs_block = jnp.exp(block_scores(query_block) - log_totals[order])
        probs_low = probs_block.astype(jnp.bfloat16)
        grad_values = grad_values + jnp.einsum(
            "hqk,qhd->khd", probs_low, grad_block, preferred_element_type=jnp.float32
        )
        grad_probs_block = jnp.einsum(
            "qhd,khd->hqk", grad_block, value_low, preferred_element_type=jnp.float32
        )
        delta = jnp.sum(probs_block * grad_probs_block, axis=-1, keepdims=True)
        grad_scores = (probs_block * (grad_probs_block - delta)).astype(jnp.bfloat16)
        grad_query_parts.append(
            jnp.einsum("hqk,khd->qhd", grad_scores, key_low, preferred_element_type=jnp.float32)
            * scale
        )
        grad_keys = (
            grad_keys
            + jnp.einsum(
                "hqk,qhd->khd", grad_scores, query_block, preferred_element_type=jnp.float32
            )
            * scale
        )
    grad_queries = jnp.concatenate(grad_query_parts, axis=0)
    query_pull = jax.vjp(prepare, query_unrotated, q_gain)[1]
    grad_query_raw, q_part = query_pull(grad_queries)
    key_pull = jax.vjp(prepare, key_raw, k_gain)[1]
    grad_key_raw, k_part = key_pull(grad_keys)
    grad_q_low = grad_query_raw.astype(jnp.bfloat16)
    grad_k_low = grad_key_raw.astype(jnp.bfloat16)
    grad_v_low = grad_values.reshape(full_length, local_width).astype(jnp.bfloat16)
    query_part = jnp.einsum("ld,lh->dh", gathered, grad_q_low, preferred_element_type=jnp.float32)
    key_part = jnp.einsum("ld,lh->dh", gathered, grad_k_low, preferred_element_type=jnp.float32)
    value_part = jnp.einsum("ld,lh->dh", gathered, grad_v_low, preferred_element_type=jnp.float32)
    from_query = jnp.einsum("lh,dh->ld", grad_q_low, w_query, preferred_element_type=jnp.float32)
    from_key = jnp.einsum("lh,dh->ld", grad_k_low, w_key, preferred_element_type=jnp.float32)
    from_value = jnp.einsum("lh,dh->ld", grad_v_low, w_value, preferred_element_type=jnp.float32)
    early = jnp.concatenate(
        [
            low(out_part),
            low(value_part),
            low(ring_sum(jnp.concatenate([router_part, ffn_part[:, None]], axis=1), tensor_count)),
        ],
        axis=1,
    )
    early = wide(lax.psum_scatter(early, "dp", scatter_dimension=0, tiled=True))
    grad_normed = wide(
        lax.psum_scatter(
            low(from_query + from_key + from_value), "tensor", scatter_dimension=0, tiled=True
        )
    )
    attn_pull = jax.vjp(rms_scale, token_values, attn_gain)[1]
    grad_tok_norm, attn_part = attn_pull(grad_normed)
    grad_tokens = (grad_residual + grad_tok_norm).astype(jnp.bfloat16)
    piece = head_dim // data_count
    gains = jnp.stack([q_part, k_part]).reshape(2, data_count, piece)
    gains = jnp.pad(gains, ((0, 0), (0, 0), (0, width // data_count - piece)))
    small = jnp.concatenate([attn_part[:, None], gains.reshape(2, width).T], axis=1)
    late = jnp.concatenate(
        [low(query_part), low(key_part), low(ring_sum(small, tensor_count))], axis=1
    )
    late = wide(lax.psum_scatter(late, "dp", scatter_dimension=0, tiled=True))
    end = 2 * local_width
    return (
        output[None],
        grad_tokens[None],
        late[:, end],
        late[:, :local_width],
        late[:, local_width:end],
        early[:, local_width:end],
        early[:, :local_width],
        late[:piece, end + 1],
        late[:piece, end + 2],
        early[:, end + all_experts],
        early[:, end : end + all_experts],
        grad_gate,
        grad_up,
        grad_down,
    )


def solution(mesh):
    return jax.shard_map(
        per_device,
        mesh=mesh,
        in_specs=(
            P("dp", "tensor", None),
            P("dp"),
            P("dp", None, None),
            P(),
            P(None, "tensor"),
            P(None, "tensor"),
            P(None, "tensor"),
            P(None, "tensor"),
            P(),
            P(),
            P(),
            P(),
            P("dp", None, "tensor"),
            P("dp", None, "tensor"),
            P("dp", "tensor", None),
            P("dp", None, None),
        ),
        out_specs=(
            P("dp", "tensor", None),
            P("dp", "tensor", None),
            P("dp"),
            P("dp", "tensor"),
            P("dp", "tensor"),
            P("dp", "tensor"),
            P("dp", "tensor"),
            P("dp"),
            P("dp"),
            P("dp"),
            P("dp", None),
            P("dp", None, "tensor"),
            P("dp", None, "tensor"),
            P("dp", "tensor", None),
        ),
        check_vma=False,
    )
```

```python
import functools

import jax
import jax.numpy as jnp
from jax import lax
from jax.experimental import pallas as pl
from jax.experimental.pallas import tpu as pltpu
from jax.sharding import PartitionSpec as P

EPS = 1e-06
THETA = 50000.0
NEG = -1e30


def rms_scale(values, gain):
    return values * lax.rsqrt(jnp.mean(values * values, axis=-1, keepdims=True) + EPS) * gain


def rotate(values):
    length = values.shape[-3]
    half_dim = values.shape[-1] // 2
    positions = jnp.arange(length).astype(jnp.float32)
    rates = THETA ** (-jnp.arange(half_dim).astype(jnp.float32) / half_dim)
    angles = positions[:, None] * rates[None, :]
    cosine = jnp.cos(angles)[:, None, :]
    sine = jnp.sin(angles)[:, None, :]
    first = values[..., :half_dim]
    second = values[..., half_dim:]
    return jnp.concatenate(
        [first * cosine - second * sine, second * cosine + first * sine], axis=-1
    )


def prepare(raw, gain):
    shaped = raw.reshape(raw.shape[0], -1, gain.shape[0])
    return rotate(rms_scale(shaped, gain))


def dot_nt(a, b):
    return lax.dot_general(a, b, (((1,), (1,)), ((), ())), preferred_element_type=jnp.float32)


def dot_nn(a, b):
    return jnp.dot(a, b, preferred_element_type=jnp.float32)


def largest_tile(total, limit, unit):
    best = unit
    for tile in range(unit, limit + 1, unit):
        if total % tile == 0:
            best = tile
    return best


def moe_kernel(
    sizes,
    own_ref,
    *others_refs,
):
    blocks = 4 * sizes[0]
    moe_body(sizes, own_ref, others_refs[:blocks], *others_refs[blocks:])


def moe_body(
    sizes,
    own_ref,
    cot_refs,
    pick_ref,
    wg_ref,
    wu_ref,
    wd_ref,
    final_ref,
    acc_ref,
    mine_ref,
    gather_ref,
    other_ref,
    both_ref,
    core_in,
    top_in,
    bottom_in,
    near_in,
    far_in,
    ring_out,
    ring_in,
    in_s,
    out_s,
    rows_s,
    crow_s,
    mrow_s,
    meta_s,
    aw_s,
    gg_s,
    gu_s,
    turn_s,
    acc_s,
    load_sem,
    store_sem,
    x_sem,
    c_sem,
    out_sem,
    fold_sem,
    plane_send,
    plane_recv,
    sum_send,
    sum_recv,
    ring_send,
    ring_recv,
    last_send,
    last_recv,
):
    outer, chunks, experts, slots, rows, width, extra, all_experts = sizes
    blocks, half, cut = 4 * outer, 2 * outer, rows // 2
    full = width + extra
    span = full + width
    total = blocks * slots
    ring = gather_ref.shape[0]
    j = pl.program_id(0)
    s = pl.program_id(1)
    steps = 2 * blocks + experts
    me = lax.axis_index("dp")
    z = lax.axis_index("tensor")
    a, rest = me // 4, me % 4
    inner_id = me + 2 - 4 * ((me // 2) % 2)
    core_id = me + 1 - 2 * (me % 2)
    upper, lower = pl.ds(0, cut), pl.ds(cut, cut)
    x_part, y_part = pl.ds(0, full), pl.ds(full, width)

    def outer_id(k):
        return ((a + k + outer) % outer) * 4 + rest

    def remote(src, dst, send, recv, where, axis="dp"):
        return pltpu.make_async_remote_copy(
            src_ref=src,
            dst_ref=dst,
            send_sem=send,
            recv_sem=recv,
            device_id={axis: where},
            device_id_type=pl.DeviceIdType.MESH,
        )

    def plane_copy(c, src, dst, rows_at, ident, where):
        first = isinstance(src, int) and src == 0
        near = src if isinstance(src, int) else dst
        source = mine_ref.at[c] if first else gather_ref.at[c % ring, near - 1]
        target = gather_ref.at[c % ring, dst - 1]
        if rows_at is not None:
            source, target = source.at[rows_at], target.at[rows_at]
        return remote(source, target, plane_send.at[c, ident], plane_recv.at[c, ident], where)

    def near_copy(c):
        return plane_copy(c, 0, 1, None, 0, inner_id)

    def far_copy(c, k):
        return plane_copy(c, 0, 2 * k, None, k, outer_id(-k))

    def top_copy(c, k):
        return plane_copy(c, 1, 2 * k + 1, upper, outer - 1 + k, outer_id(-k))

    def bottom_copy(c, k):
        return plane_copy(c, 2 * k, 2 * k + 1, lower, 2 * outer - 2 + k, inner_id)

    def core_copy(c, q):
        return plane_copy(c, q, half + q, None, 3 * outer - 2 + q, core_id)

    def ring_copy(k):
        where = (z - k + chunks) % chunks
        return remote(own_ref, mine_ref.at[k], ring_send.at[k], ring_recv.at[k], where, "tensor")

    others = range(1, outer)

    def first_hop(c):
        near_copy(c).start()
        for k in others:
            far_copy(c, k).start()
        core_copy(c, 0).start()

    def second_hop(c):
        near_copy(c).wait_recv()
        for k in others:
            top_copy(c, k).start()
        for k in others:
            far_copy(c, k).wait_recv()
            bottom_copy(c, k).start()
        for q in [1] + [2 * k for k in others]:
            core_copy(c, q).start()

    def third_hop(c):
        for k in others:
            top_copy(c, k).wait_recv()
            bottom_copy(c, k).wait_recv()
            core_copy(c, 2 * k + 1).start()

    def drain_gather(c):
        near_copy(c).wait_send()
        for k in others:
            far_copy(c, k).wait_send()
            top_copy(c, k).wait_send()
            bottom_copy(c, k).wait_send()
        for q in range(half):
            core_copy(c, q).wait_send()

    def sum_copy(c, src, dst, ident, where):
        return remote(src, dst, sum_send.at[c, ident], sum_recv.at[c, ident], where)

    def swap_copy(c, q):
        return sum_copy(c, other_ref.at[c % 2, q], core_in.at[c % 2, q], q, core_id)

    def both_at(c, q, rows_at):
        return both_ref.at[c % 2, q, rows_at]

    def up_copy(c, k):
        ident = half + k - 1
        return sum_copy(c, both_at(c, 2 * k + 1, upper), top_in.at[c % 2, k - 1], ident, outer_id(k))

    def down_copy(c, k):
        ident = half + outer - 1 + k - 1
        source = both_at(c, 2 * k + 1, lower)
        return sum_copy(c, source, bottom_in.at[c % 2, k - 1], ident, inner_id)

    def home_near(c, part):
        rows_at = (upper, lower)[part]
        ident = half + 2 * outer - 2 + part
        return sum_copy(c, both_at(c, 1, rows_at), near_in.at[c % 2, rows_at], ident, inner_id)

    def home_far(c, k, part):
        rows_at = (upper, lower)[part]
        ident = half + 2 * outer + 2 * (k - 1) + part
        target = far_in.at[c % 2, k - 1, rows_at]
        return sum_copy(c, both_at(c, 2 * k, rows_at), target, ident, outer_id(k))

    def last_copy(c):
        where = (z + c) % chunks
        return remote(ring_out.at[c], ring_in.at[c], last_send.at[c], last_recv.at[c], where, "tensor")

    def local(src, dst, sem):
        return pltpu.make_async_copy(src, dst, sem)

    def together(*copies):
        for copy in copies:
            copy.start()
        for copy in copies:
            copy.wait()

    def fold_halves(c):
        for k in others:
            up_copy(c, k).wait_recv()
            down_copy(c, k).wait_recv()
            copies = [
                local(both_at(c, 2 * k, lower), in_s.at[0, lower], fold_sem.at[0]),
                local(top_in.at[c % 2, k - 1], in_s.at[1, upper], fold_sem.at[1]),
                local(bottom_in.at[c % 2, k - 1], in_s.at[1, lower], fold_sem.at[2]),
            ]
            if k == 1:
                copies.append(local(both_at(c, 1, upper), in_s.at[0, upper], fold_sem.at[3]))
            together(*copies)

            @pl.loop(0, rows // 16)
            def _(i):
                at = pl.ds(pl.multiple_of(i * 16, 16), 16)
                in_s[0, at, :] = low(wide(in_s[0, at, :]) + wide(in_s[1, at, :]))

            together(local(in_s.at[0, lower], both_at(c, 2 * k, lower), fold_sem.at[0]))
        together(local(in_s.at[0, upper], both_at(c, 1, upper), fold_sem.at[0]))
        for k in others:
            home_far(c, k, 1).start()
        home_near(c, 0).start()

    def fold_home(c):
        for part in (0, 1):
            home_near(c, part).wait_recv()
        together(
            local(both_ref.at[c % 2, 0], in_s.at[0], fold_sem.at[0]),
            local(near_in.at[c % 2], in_s.at[1], fold_sem.at[1]),
        )

        @pl.loop(0, rows // 16)
        def _(i):
            at = pl.ds(pl.multiple_of(i * 16, 16), 16)
            in_s[0, at, :] = low(wide(in_s[0, at, :]) + wide(in_s[1, at, :]))

        for k in others:
            for part in (0, 1):
                home_far(c, k, part).wait_recv()
            together(local(far_in.at[c % 2, k - 1], in_s.at[1], fold_sem.at[1]))

            @pl.loop(0, rows // 16)
            def _(i):
                at = pl.ds(pl.multiple_of(i * 16, 16), 16)
                in_s[0, at, :] = low(wide(in_s[0, at, :]) + wide(in_s[1, at, :]))

        together(local(in_s.at[0], ring_out.at[c], fold_sem.at[0]))

    def drain_sum(c):
        for q in range(half):
            swap_copy(c, q).wait_send()
        for k in others:
            up_copy(c, k).wait_send()
            down_copy(c, k).wait_send()
            for part in (0, 1):
                home_far(c, k, part).wait_send()
        for part in (0, 1):
            home_near(c, part).wait_send()

    def fetch(c, at):
        q, side, slot = at // 2, at % 2, at % 2
        r = side * half + q

        @pl.when(side == 1)
        def _():
            core_copy(c, q).wait_recv()

        rows_at = pl.ds(pl.multiple_of(((z + c) % chunks) * rows, rows), rows)
        @pl.when(r == 0)
        def _():
            local(mine_ref.at[c], in_s.at[slot, :, x_part], x_sem.at[slot]).start()

        @pl.when(r > 0)
        def _():
            source = gather_ref.at[c % ring, jnp.maximum(r - 1, 0)]
            local(source, in_s.at[slot, :, x_part], x_sem.at[slot]).start()

        for place, cot_ref in enumerate(cot_refs):

            @pl.when(r == place)
            def _():
                local(cot_ref.at[rows_at], in_s.at[slot, :, y_part], c_sem.at[slot]).start()


    def fetched(slot):
        local(mine_ref.at[0], in_s.at[slot, :, x_part], x_sem.at[slot]).wait()
        local(cot_refs[0].at[pl.ds(0, rows)], in_s.at[slot, :, y_part], c_sem.at[slot]).wait()

    def load(e, slot):
        return local(acc_ref.at[e], acc_s.at[slot], load_sem.at[slot])

    def store(e, slot):
        return local(acc_s.at[slot], acc_ref.at[e], store_sem.at[slot])

    @pl.when((j == 0) & (s == 0))
    def _():
        barrier = pltpu.get_barrier_semaphore()
        peers = [("dp", core_id), ("dp", inner_id)] + [("dp", outer_id(k)) for k in others]
        peers += [("tensor", (z + k) % chunks) for k in range(1, chunks)]
        for axis, where in peers:
            pl.semaphore_signal(
                barrier, inc=1, device_id={axis: where}, device_id_type=pl.DeviceIdType.MESH
            )
        pl.semaphore_wait(barrier, len(peers))
        for k in range(1, chunks):
            ring_copy(k).start()
        together(local(own_ref, in_s.at[0, :, x_part], fold_sem.at[0]))
        together(local(in_s.at[0, :, x_part], mine_ref.at[0], fold_sem.at[0]))
        first_hop(0)
        fetch(0, 0)
        second_hop(0)
        ring_copy(1).wait_recv()
        first_hop(1)

    @pl.when((s == 0) & (j > 0))
    def _():
        load(0, 0).start()

    @pl.when((j == 0) & (s == 4))
    def _():
        third_hop(0)

    @pl.when((s == blocks + 1) & (j + 1 < chunks))
    def _():
        second_hop(j + 1)

    @pl.when((s == blocks + experts) & (j + 1 < chunks))
    def _():
        third_hop(j + 1)

    @pl.when((s == blocks + 2) & (j >= 1))
    def _():
        fold_halves(j - 1)

    @pl.when((s == blocks + 2) & (j + 2 < chunks))
    def _():
        ring_copy(j + 2).wait_recv()
        first_hop(j + 2)

    @pl.when(s == blocks + 3)
    def _():
        drain_gather(j)

    @pl.when((s == blocks + experts + half - 1) & (j >= 1))
    def _():
        fold_home(j - 1)

        @pl.when(j >= 2)
        def _():
            last_copy(j - 1).start()

        drain_sum(j - 1)

    @pl.when(s < blocks)
    def _():
        slot = s % 2

        @pl.when(s + 1 < blocks)
        def _():
            fetch(j, s + 1)

        fetched(slot)
        meta = in_s[slot, :, width:full]
        picks = (dot_nt(pick_ref[...], meta) == 0.0).astype(jnp.bfloat16)
        at = pl.multiple_of(s * slots, slots)
        got = low(dot_nn(picks, in_s[slot, :, :full]))
        cot = low(dot_nn(picks, in_s[slot, :, full:]))
        for e in range(experts):
            part = slice(e * slots, (e + 1) * slots)
            rows_s[e, pl.ds(at, slots), :] = got[part, :width]
            mrow_s[e, pl.ds(at, slots), :] = got[part, width:]
            crow_s[e, pl.ds(at, slots), :] = cot[part]
        meta_s[s] = meta

    @pl.when((s >= blocks) & (s < blocks + experts))
    def _():
        e = s - blocks
        slot = e % 2
        tile = largest_tile(total, 320, 16)
        expert = me * experts + e
        wg = wg_ref[0]
        wu = wu_ref[0]
        wd = wd_ref[0]

        @pl.loop(0, total // tile)
        def _(m):
            ds = pl.ds(pl.multiple_of(m * tile, tile), tile)
            picked_rows = rows_s[e, ds, :]
            gate = dot_nn(picked_rows, wg)
            up = dot_nn(picked_rows, wu)
            grad_act = dot_nt(crow_s[e, ds, :], wd)
            meta = wide(mrow_s[e, ds, :])
            column = lax.broadcasted_iota(jnp.int32, meta.shape, 1)
            wanted = (column == expert) | (column == expert + all_experts)
            weight = jnp.sum(jnp.where(wanted, meta, 0.0), axis=1, keepdims=True)
            sig = jax.nn.sigmoid(gate)
            silu = gate * sig
            act = silu * up
            g_pick = jnp.sum(act * grad_act, axis=1, keepdims=True)
            scaled = weight * grad_act
            aw_s[ds, :] = low(weight * act)
            gg_s[ds, :] = low(scaled * up * sig * (1.0 + gate * (1.0 - sig)))
            gu_s[ds, :] = low(scaled * silu)
            mrow_s[e, ds, :] = low(jnp.where(column == expert, g_pick, 0.0))

        @pl.when(e >= 1)
        def _():
            store(e - 1, 1 - slot).wait()

        @pl.when(j == 0)
        def _():
            acc_s[slot] = jnp.zeros(acc_s.shape[1:], jnp.float32)

        @pl.when(j > 0)
        def _():
            load(e, slot).wait()

            @pl.when(e + 1 < experts)
            def _():
                load(e + 1, 1 - slot).start()

        cols = largest_tile(width, 512, 128)
        for which, (left, right) in enumerate(((gg_s, rows_s), (gu_s, rows_s), (aw_s, crow_s))):
            turn_s[...] = left[...].T

            @pl.loop(0, width // cols)
            def _(n):
                ds = pl.ds(pl.multiple_of(n * cols, cols), cols)
                add = dot_nn(turn_s[...], right[e, :, ds])
                acc_s[slot, which, :, ds] = acc_s[slot, which, :, ds] + add

        store(e, slot).start()

        @pl.loop(0, total // tile)
        def _(m):
            ds = pl.ds(pl.multiple_of(m * tile, tile), tile)
            crow_s[e, ds, :] = low(dot_nn(aw_s[ds, :], wd))
            rows_s[e, ds, :] = low(dot_nt(gg_s[ds, :], wg) + dot_nt(gu_s[ds, :], wu))

    first = blocks + experts

    def written(c, o):
        q, slot = half - 1 - o % half, o % 2

        @pl.when(o < half)
        def _():
            local(out_s.at[slot], other_ref.at[c % 2, q], out_sem.at[slot]).wait()
            swap_copy(c, q).start()

        @pl.when(o >= half)
        def _():
            local(out_s.at[slot], both_ref.at[c % 2, q], out_sem.at[slot]).wait()

        for k in others:

            @pl.when((o >= half) & (q == 2 * k + 1))
            def _():
                up_copy(c, k).start()
                down_copy(c, k).start()

            @pl.when((o >= half) & (q == 2 * k))
            def _():
                home_far(c, k, 0).start()

        @pl.when((o >= half) & (q == 1))
        def _():
            home_near(c, 1).start()

    @pl.when(s >= first)
    def _():
        o = s - first
        slot = o % 2
        q = half - 1 - o % half
        side = 1 - o // half
        place = 2 * q + side
        at = pl.multiple_of(place * slots, slots)

        @pl.when(o >= 1)
        def _():
            written(j, o - 1)

        @pl.when((o >= half - 1) & (o < 2 * half - 1))
        def _():
            coming = half - 1 - (o + 1) % half
            swap_copy(j, coming).wait_recv()
            local(core_in.at[j % 2, coming], in_s.at[1 - slot], x_sem.at[1 - slot]).start()

        @pl.when(o >= half)
        def _():
            local(core_in.at[j % 2, q], in_s.at[slot], x_sem.at[slot]).wait()

        @pl.when(o < half)
        def _():
            in_s[slot] = jnp.zeros((rows, span), jnp.bfloat16)

        picks = (dot_nt(meta_s[place], pick_ref[...]) == 0.0).astype(jnp.bfloat16)
        flat = (experts * slots, width)
        g = dot_nn(picks, rows_s[:, pl.ds(at, slots), :].reshape(flat))
        out_s[slot, :, :width] = low(g + wide(in_s[slot, :, :width]))
        flat = (experts * slots, extra)
        p = dot_nn(picks, mrow_s[:, pl.ds(at, slots), :].reshape(flat))
        out_s[slot, :, width:full] = low(p + wide(in_s[slot, :, width:full]))
        flat = (experts * slots, width)
        y = dot_nn(picks, crow_s[:, pl.ds(at, slots), :].reshape(flat))
        out_s[slot, :, full:] = low(y + wide(in_s[slot, :, full:]))

        @pl.when(o < half)
        def _():
            local(out_s.at[slot], other_ref.at[j % 2, q], out_sem.at[slot]).start()

        @pl.when(o >= half)
        def _():
            local(out_s.at[slot], both_ref.at[j % 2, q], out_sem.at[slot]).start()

        @pl.when(s == steps - 1)
        def _():
            written(j, o)
            store(experts - 1, (experts - 1) % 2).wait()

        @pl.when((s == steps - 1) & (j + 1 < chunks))
        def _():
            fetch(j + 1, 0)

    @pl.when((s == steps - 1) & (j == chunks - 1))
    def _():
        fold_halves(chunks - 1)
        fold_home(chunks - 1)
        last_copy(chunks - 1).start()
        drain_sum(chunks - 1)
        together(local(ring_out.at[0], in_s.at[0], fold_sem.at[0]))
        for k in range(1, chunks):
            last_copy(k).wait_recv()
            together(local(ring_in.at[k], in_s.at[1], fold_sem.at[1]))

            @pl.loop(0, rows // 16)
            def _(i):
                at = pl.ds(pl.multiple_of(i * 16, 16), 16)
                in_s[0, at, :] = low(wide(in_s[0, at, :]) + wide(in_s[1, at, :]))

        together(local(in_s.at[0], final_ref, fold_sem.at[0]))
        for k in range(1, chunks):
            last_copy(k).wait_send()
            ring_copy(k).wait_send()


def moe(own, cot, picks, wg, wu, wd, outer, chunks, slots, all_experts):
    rows, full = own.shape
    width = cot[0].shape[1]
    extra = full - width
    span = full + width
    experts, _, hidden = wg.shape
    blocks, half, cut = 4 * outer, 2 * outer, rows // 2
    total = blocks * slots
    sizes = (outer, chunks, experts, slots, rows, width, extra, all_experts)

    def expert_at(j, s):
        return (jnp.clip(s - blocks, 0, experts - 1), 0, 0)

    anywhere = pl.BlockSpec(memory_space=pl.ANY)
    in_specs = [
        *[anywhere] * (1 + len(cot)),
        pl.BlockSpec(picks.shape, lambda j, s: (0, 0)),
        pl.BlockSpec((1, width, hidden), expert_at),
        pl.BlockSpec((1, width, hidden), expert_at),
        pl.BlockSpec((1, hidden, width), expert_at),
    ]
    bf16 = jnp.bfloat16
    shapes = [
        ((rows, span), bf16),
        ((experts, 3, hidden, width), jnp.float32),
        ((chunks, rows, full), bf16),
        ((chunks if chunks <= 4 else 3, blocks - 1, rows, full), bf16),
        ((2, half, rows, span), bf16),
        ((2, half, rows, span), bf16),
        ((2, half, rows, span), bf16),
        ((2, outer - 1, cut, span), bf16),
        ((2, outer - 1, cut, span), bf16),
        ((2, rows, span), bf16),
        ((2, outer - 1, rows, span), bf16),
        ((chunks, rows, span), bf16),
        ((chunks, rows, span), bf16),
    ]
    dma = pltpu.SemaphoreType.DMA
    gathers, sums = 5 * outer - 2, 6 * outer - 2
    scratch = [
        pltpu.VMEM((2, rows, span), bf16),
        pltpu.VMEM((2, rows, span), bf16),
        pltpu.VMEM((experts, total, width), bf16),
        pltpu.VMEM((experts, total, width), bf16),
        pltpu.VMEM((experts, total, extra), bf16),
        pltpu.VMEM((blocks, rows, extra), bf16),
        pltpu.VMEM((total, hidden), bf16),
        pltpu.VMEM((total, hidden), bf16),
        pltpu.VMEM((total, hidden), bf16),
        pltpu.VMEM((hidden, total), bf16),
        pltpu.VMEM((2, 3, hidden, width), jnp.float32),
        dma((2,)),
        dma((2,)),
        dma((2,)),
        dma((2,)),
        dma((2,)),
        dma((4,)),
        dma((chunks, gathers)),
        dma((chunks, gathers)),
        dma((chunks, sums)),
        dma((chunks, sums)),
        dma((chunks,)),
        dma((chunks,)),
        dma((chunks,)),
        dma((chunks,)),
    ]
    flops = 2 * chunks * experts * total * width * (hidden * 9 + 4 * rows)
    results = pl.pallas_call(
        functools.partial(moe_kernel, sizes),
        grid=(chunks, 2 * blocks + experts),
        in_specs=in_specs,
        out_specs=[anywhere] * len(shapes),
        out_shape=[jax.ShapeDtypeStruct(*shape) for shape in shapes],
        scratch_shapes=scratch,
        compiler_params=pltpu.CompilerParams(
            dimension_semantics=("arbitrary", "arbitrary"),
            vmem_limit_bytes=66_500_000,
            collective_id=0,
            has_side_effects=True,
        ),
        cost_estimate=pl.CostEstimate(
            flops=flops, bytes_accessed=blocks * chunks * rows * full * 8, transcendentals=0
        ),
        name="moe",
    )(own, *cot, picks, wg, wu, wd)
    return results[:2]


def wide(values):
    return values.astype(jnp.float32)


def low(values):
    return values.astype(jnp.bfloat16)


def tie(*values):
    return lax.optimization_barrier(values)


def ring_sum(values, count):
    total = values
    for step in range(1, count):
        pairs = [(i, (i + step) % count) for i in range(count)]
        total = total + lax.ppermute(values, "tensor", pairs)
    return total


def pick(values, at, axis):
    return lax.dynamic_index_in_dim(values, at, axis, keepdims=False)


class Plane:
    def __init__(self, count):
        self.outer = count // 4
        everyone = range(count)
        self.core = [(i, i ^ 1) for i in everyone]
        self.inner = [(i, i ^ 2) for i in everyone]
        self.count = count

    def pull(self, values, k):
        pairs = [((i + 4 * k) % self.count, i) for i in range(self.count)]
        return lax.ppermute(values, "dp", pairs)

    def swap_inner(self, values):
        return lax.ppermute(values, "dp", self.inner)

    def swap_core(self, values):
        return lax.ppermute(values, "dp", self.core)

    def push(self, values, k):
        pairs = [(i, (i + 4 * k) % self.count) for i in range(self.count)]
        return lax.ppermute(values, "dp", pairs)

    def fold_inner(self, parts, b, axis, kind):
        given = self.swap_inner(pick(parts, 1 - b, axis).astype(kind))
        return wide(pick(parts, b, axis)) + wide(given)

    def fold_outer(self, parts, a, kind):
        total = wide(pick(parts, a, 0))
        for k in range(1, self.outer):
            given = pick(parts, (a + k) % self.outer, 0).astype(kind)
            total = total + wide(self.push(given, k))
        return total

    def scatter(self, values, inner_first):
        kind = values.dtype
        index = lax.axis_index("dp")
        core, b, a = index % 2, index // 2 % 2, index // 4
        parts = values.reshape(self.outer, 2, 2, values.shape[0] // self.count, values.shape[1])
        given = self.swap_core(pick(parts, 1 - core, 2))
        parts = (wide(pick(parts, core, 2)) + wide(given)).astype(kind)
        if inner_first:
            return self.fold_outer(self.fold_inner(parts, b, 1, kind).astype(kind), a, kind)
        return self.fold_inner(self.fold_outer(parts, a, kind).astype(kind), b, 0, kind)

    def first(self, own):
        return self.swap_inner(own), [self.pull(own, k) for k in range(1, self.outer)]

    def second(self, near, fars):
        half = near.shape[0] // 2
        return [
            jnp.concatenate([self.pull(near[:half], k + 1), self.swap_inner(far[half:])], axis=0)
            for k, far in enumerate(fars)
        ]

    def third(self, own, near, fars, diagonals):
        mine = [own, near]
        for far, diagonal in zip(fars, diagonals):
            mine += [far, diagonal]
        return mine + [self.swap_core(part) for part in mine]


def per_device(
    tokens,
    lengths,
    routes,
    attn_gain,
    w_query,
    w_key,
    w_value,
    w_out,
    q_gain,
    k_gain,
    ffn_gain,
    router_weight,
    w_gate,
    w_up,
    w_down,
    cotangent,
):
    tensor_count = lax.axis_size("tensor")
    data_count = lax.axis_size("dp")
    tensor_rank = lax.axis_index("tensor")
    block_rows = tokens.shape[1]
    width = tokens.shape[2]
    full_length = block_rows * tensor_count
    route_count = routes.shape[2]
    local_experts = w_gate.shape[0]
    all_experts = local_experts * data_count
    head_dim = q_gain.shape[0]
    local_width = w_query.shape[1]
    capacity = max(2, (block_rows * route_count * 5 + 4 * all_experts - 1) // (4 * all_experts))
    query_rows = min(512, full_length)
    scale = head_dim ** (-0.5)
    own_start = tensor_rank * block_rows
    token_values = tokens[0].astype(jnp.float32)
    seq_length = lengths[0]
    own_valid = (own_start + jnp.arange(block_rows) < seq_length).astype(jnp.float32)
    key_valid = jnp.arange(full_length) < seq_length
    normed = rms_scale(token_values, attn_gain).astype(jnp.bfloat16)
    gathered = lax.all_gather(normed, "tensor", axis=0, tiled=True)
    plane = Plane(data_count)
    near, fars = plane.first(cotangent[0])
    core = lax.axis_index("dp") % 2
    depth = width // 2
    out_half = lax.dynamic_slice_in_dim(w_out, core * depth, depth, 0)
    gathered, near, fars, out_half = tie(gathered, near, fars, out_half)
    out_mine = lax.all_gather(out_half, "tensor", axis=0)
    query_unrotated = jnp.dot(gathered, w_query, preferred_element_type=jnp.float32)
    key_raw = jnp.dot(gathered, w_key, preferred_element_type=jnp.float32)
    value_raw = jnp.dot(gathered, w_value, preferred_element_type=jnp.float32)
    query_low = prepare(query_unrotated, q_gain).astype(jnp.bfloat16)
    key_low = prepare(key_raw, k_gain).astype(jnp.bfloat16)
    value_low = value_raw.astype(jnp.bfloat16).reshape(full_length, -1, head_dim)

    def block_scores(query_block):
        scores = (
            jnp.einsum("qhd,khd->hqk", query_block, key_low, preferred_element_type=jnp.float32)
            * scale
        )
        return jnp.where(key_valid[None, None, :], scores, NEG)

    mixed_parts = []
    log_totals = []
    for start in range(0, full_length, query_rows):
        scores = block_scores(query_low[start : start + query_rows])
        row_peak = jnp.max(scores, axis=-1, keepdims=True)
        powers = jnp.exp(scores - row_peak)
        total = jnp.sum(powers, axis=-1, keepdims=True)
        weights = (powers / total).astype(jnp.bfloat16)
        mixed_parts.append(
            jnp.einsum("hqk,khd->qhd", weights, value_low, preferred_element_type=jnp.float32)
        )
        log_totals.append(row_peak + jnp.log(total))
    attended = (
        jnp.concatenate(mixed_parts, axis=0).reshape(full_length, local_width).astype(jnp.bfloat16)
    )
    diagonals = plane.second(near, fars)
    attended, diagonals = tie(attended, diagonals)
    cot_all = plane.third(cotangent[0], near, fars, diagonals)
    out_other = plane.swap_core(out_mine)
    heads_own = lax.all_to_all(
        attended.reshape(tensor_count, block_rows, local_width), "tensor", 0, 0
    )
    heads_own = heads_own.reshape(tensor_count, block_rows, local_width)

    def from_heads(out_weight):
        return sum(dot_nt(heads_own[t], out_weight[t]) for t in range(tensor_count))

    attn_mine, attn_other = from_heads(out_mine), from_heads(out_other)
    attn_own = jnp.where(
        core == 0,
        jnp.concatenate([attn_mine, attn_other], axis=1),
        jnp.concatenate([attn_other, attn_mine], axis=1),
    )
    residual = token_values + own_valid[:, None] * attn_own
    moe_own = rms_scale(residual, ffn_gain).astype(jnp.bfloat16)
    router_logits = jnp.dot(moe_own, router_weight, preferred_element_type=jnp.float32)
    own_probs = jax.nn.softmax(router_logits, axis=-1)
    own_routes = lax.dynamic_slice_in_dim(routes[0], own_start, block_rows, 0)
    onehot = own_routes[:, :, None] == jnp.arange(all_experts)[None, None, :]
    named = jnp.any(onehot, axis=1) & (own_valid[:, None] > 0.0)
    named_low = named.astype(jnp.bfloat16)
    before = jnp.arange(block_rows)[:, None] > jnp.arange(block_rows)[None, :]
    order = jnp.dot(before.astype(jnp.bfloat16), named_low, preferred_element_type=jnp.float32)
    place = jnp.where(named, order, -1.0).astype(jnp.bfloat16)
    weight = jnp.where(named, own_probs, 0.0)
    weight_high = weight.astype(jnp.bfloat16)
    weight_low = (weight - weight_high.astype(jnp.float32)).astype(jnp.bfloat16)
    used = 3 * all_experts + 1
    extra = (used + 127) // 128 * 128
    meta = jnp.concatenate(
        [
            weight_high,
            weight_low,
            place,
            jnp.ones((block_rows, 1), jnp.bfloat16),
            jnp.zeros((block_rows, extra - used), jnp.bfloat16),
        ],
        axis=1,
    )
    slots = (capacity + 15) // 16 * 16
    first_expert = lax.axis_index("dp") * local_experts
    slot_row = jnp.arange(local_experts * slots)[:, None]
    slot_column = jnp.arange(extra)[None, :]
    picks = jnp.where(
        slot_column == 2 * all_experts + first_expert + slot_row // slots,
        1.0,
        jnp.where(slot_column == 3 * all_experts, -(slot_row % slots).astype(jnp.float32), 0.0),
    ).astype(jnp.bfloat16)
    packed = jnp.concatenate([moe_own, meta], axis=1)
    combined, sums = moe(
        packed,
        cot_all,
        picks,
        w_gate,
        w_up,
        w_down,
        data_count // 4,
        tensor_count,
        slots,
        all_experts,
    )
    combined = wide(combined)
    grad_gate = jnp.swapaxes(sums[:, 0], 1, 2)
    grad_up = jnp.swapaxes(sums[:, 1], 1, 2)
    grad_down = sums[:, 2]
    grad_moe = combined[:, :width]
    grad_probs = combined[:, width : width + all_experts]
    output = low(residual + combined[:, width + extra :])
    grad_own = lax.dynamic_slice_in_dim(cotangent[0], own_start, block_rows, 0).astype(jnp.float32)
    grad_logits = (
        own_probs * (grad_probs - jnp.sum(own_probs * grad_probs, axis=-1, keepdims=True))
    ).astype(jnp.bfloat16)
    grad_moe = grad_moe + jnp.einsum(
        "re,de->rd", grad_logits, router_weight, preferred_element_type=jnp.float32
    )
    router_part = jnp.einsum("rd,re->de", moe_own, grad_logits, preferred_element_type=jnp.float32)
    ffn_pull = jax.vjp(rms_scale, residual, ffn_gain)[1]
    grad_res_norm, ffn_part = ffn_pull(grad_moe)
    grad_residual = grad_own + grad_res_norm
    grad_attn = (grad_residual * own_valid[:, None]).astype(jnp.bfloat16)
    attn_lower = lax.dynamic_slice_in_dim(grad_attn, core * depth, depth, 1)
    attn_upper = lax.dynamic_slice_in_dim(grad_attn, depth - core * depth, depth, 1)
    grad_heads = jnp.stack(
        [
            low(dot_nn(attn_lower, out_mine[t]) + dot_nn(attn_upper, out_other[t]))
            for t in range(tensor_count)
        ]
    )
    grad_mixed = lax.all_to_all(grad_heads, "tensor", 0, 0)
    grad_mixed, grad_attn = tie(grad_mixed, grad_attn)
    grad_attn_all = lax.all_gather(grad_attn, "tensor", axis=0, tiled=True)
    grad_mixed = grad_mixed.reshape(full_length, -1, head_dim)
    out_part = jnp.einsum("ld,lh->dh", grad_attn_all, attended, preferred_element_type=jnp.float32)
    grad_query_parts = []
    grad_keys = jnp.zeros(key_low.shape, jnp.float32)
    grad_values = jnp.zeros(value_low.shape, jnp.float32)
    for order, start in enumerate(range(0, full_length, query_rows)):
        query_block = query_low[start : start + query_rows]
        grad_block = grad_mixed[start : start + query_rows]
        probs_block = jnp.exp(block_scores(query_block) - log_totals[order])
        probs_low = probs_block.astype(jnp.bfloat16)
        grad_values = grad_values + jnp.einsum(
            "hqk,qhd->khd", probs_low, grad_block, preferred_element_type=jnp.float32
        )
        grad_probs_block = jnp.einsum(
            "qhd,khd->hqk", grad_block, value_low, preferred_element_type=jnp.float32
        )
        delta = jnp.sum(probs_block * grad_probs_block, axis=-1, keepdims=True)
        grad_scores = (probs_block * (grad_probs_block - delta)).astype(jnp.bfloat16)
        grad_query_parts.append(
            jnp.einsum("hqk,khd->qhd", grad_scores, key_low, preferred_element_type=jnp.float32)
            * scale
        )
        grad_keys = (
            grad_keys
            + jnp.einsum(
                "hqk,qhd->khd", grad_scores, query_block, preferred_element_type=jnp.float32
            )
            * scale
        )
    grad_queries = jnp.concatenate(grad_query_parts, axis=0)
    query_pull = jax.vjp(prepare, query_unrotated, q_gain)[1]
    grad_query_raw, q_part = query_pull(grad_queries)
    key_pull = jax.vjp(prepare, key_raw, k_gain)[1]
    grad_key_raw, k_part = key_pull(grad_keys)
    grad_q_low = grad_query_raw.astype(jnp.bfloat16)
    grad_k_low = grad_key_raw.astype(jnp.bfloat16)
    grad_v_low = grad_values.reshape(full_length, local_width).astype(jnp.bfloat16)
    query_part = jnp.einsum("ld,lh->dh", gathered, grad_q_low, preferred_element_type=jnp.float32)
    key_part = jnp.einsum("ld,lh->dh", gathered, grad_k_low, preferred_element_type=jnp.float32)
    value_part = jnp.einsum("ld,lh->dh", gathered, grad_v_low, preferred_element_type=jnp.float32)
    from_query = jnp.einsum("lh,dh->ld", grad_q_low, w_query, preferred_element_type=jnp.float32)
    from_key = jnp.einsum("lh,dh->ld", grad_k_low, w_key, preferred_element_type=jnp.float32)
    from_value = jnp.einsum("lh,dh->ld", grad_v_low, w_value, preferred_element_type=jnp.float32)
    grad_normed = wide(
        lax.psum_scatter(
            low(from_query + from_key + from_value), "tensor", scatter_dimension=0, tiled=True
        )
    )
    attn_pull = jax.vjp(rms_scale, token_values, attn_gain)[1]
    grad_tok_norm, attn_part = attn_pull(grad_normed)
    grad_tokens = (grad_residual + grad_tok_norm).astype(jnp.bfloat16)
    grad_out = plane.scatter(low(out_part), True)
    grad_value = plane.scatter(low(value_part), False)
    grad_query = plane.scatter(low(query_part), True)
    grad_key = plane.scatter(low(key_part), False)
    routing = plane.scatter(jnp.concatenate([router_part, ffn_part[:, None]], axis=1), False)
    routing = ring_sum(routing, tensor_count)
    parts = [v.reshape(data_count, -1) for v in (attn_part, q_part, k_part)]
    gains = ring_sum(plane.scatter(jnp.concatenate(parts, axis=1), True), tensor_count)[0]
    piece = width // data_count
    last = piece + head_dim // data_count
    return (
        output[None],
        grad_tokens[None],
        gains[:piece],
        grad_query,
        grad_key,
        grad_value,
        grad_out,
        gains[piece:last],
        gains[last:],
        routing[:, all_experts],
        routing[:, :all_experts],
        grad_gate,
        grad_up,
        grad_down,
    )


def solution(mesh):
    return jax.shard_map(
        per_device,
        mesh=mesh,
        in_specs=(
            P("dp", "tensor", None),
            P("dp"),
            P("dp", None, None),
            P(),
            P(None, "tensor"),
            P(None, "tensor"),
            P(None, "tensor"),
            P(None, "tensor"),
            P(),
            P(),
            P(),
            P(),
            P("dp", None, "tensor"),
            P("dp", None, "tensor"),
            P("dp", "tensor", None),
            P("dp", None, None),
        ),
        out_specs=(
            P("dp", "tensor", None),
            P("dp", "tensor", None),
            P("dp"),
            P("dp", "tensor"),
            P("dp", "tensor"),
            P("dp", "tensor"),
            P("dp", "tensor"),
            P("dp"),
            P("dp"),
            P("dp"),
            P("dp", None),
            P("dp", None, "tensor"),
            P("dp", None, "tensor"),
            P("dp", "tensor", None),
        ),
        check_vma=False,
    )
```

```python
import functools

import jax
import jax.numpy as jnp
from jax import lax
from jax.experimental import pallas as pl
from jax.experimental.pallas import tpu as pltpu
from jax.sharding import PartitionSpec as P

EPS = 1e-06
THETA = 50000.0
NEG = -1e30


def rms_scale(values, gain):
    return values * lax.rsqrt(jnp.mean(values * values, axis=-1, keepdims=True) + EPS) * gain


def rotate(values):
    length = values.shape[-3]
    half_dim = values.shape[-1] // 2
    positions = jnp.arange(length).astype(jnp.float32)
    rates = THETA ** (-jnp.arange(half_dim).astype(jnp.float32) / half_dim)
    angles = positions[:, None] * rates[None, :]
    cosine = jnp.cos(angles)[:, None, :]
    sine = jnp.sin(angles)[:, None, :]
    first = values[..., :half_dim]
    second = values[..., half_dim:]
    return jnp.concatenate(
        [first * cosine - second * sine, second * cosine + first * sine], axis=-1
    )


def prepare(raw, gain):
    shaped = raw.reshape(raw.shape[0], -1, gain.shape[0])
    return rotate(rms_scale(shaped, gain))


def dot_nt(a, b):
    return lax.dot_general(a, b, (((1,), (1,)), ((), ())), preferred_element_type=jnp.float32)


def dot_nn(a, b):
    return jnp.dot(a, b, preferred_element_type=jnp.float32)


def largest_tile(total, limit, unit):
    best = unit
    for tile in range(unit, limit + 1, unit):
        if total % tile == 0:
            best = tile
    return best


def moe_kernel(
    sizes,
    own_ref,
    *others_refs,
):
    blocks = 4 * sizes[0]
    moe_body(sizes, own_ref, others_refs[:blocks], *others_refs[blocks:])


def moe_body(
    sizes,
    own_ref,
    cot_refs,
    pick_ref,
    wg_ref,
    wu_ref,
    wd_ref,
    final_ref,
    acc_ref,
    mine_ref,
    gather_ref,
    other_ref,
    both_ref,
    core_in,
    top_in,
    bottom_in,
    near_in,
    far_in,
    ring_out,
    ring_in,
    in_s,
    out_s,
    rows_s,
    crow_s,
    mrow_s,
    meta_s,
    aw_s,
    gg_s,
    gu_s,
    turn_s,
    acc_s,
    load_sem,
    store_sem,
    x_sem,
    c_sem,
    out_sem,
    fold_sem,
    plane_send,
    plane_recv,
    sum_send,
    sum_recv,
    ring_send,
    ring_recv,
    last_send,
    last_recv,
):
    outer, chunks, experts, slots, rows, width, extra, all_experts = sizes
    blocks, half, cut = 4 * outer, 2 * outer, rows // 2
    full = width + extra
    span = full + width
    total = blocks * slots
    ring = gather_ref.shape[0]
    j = pl.program_id(0)
    s = pl.program_id(1)
    steps = 2 * blocks + experts
    me = lax.axis_index("dp")
    z = lax.axis_index("tensor")
    a, rest = me // 4, me % 4
    inner_id = me + 2 - 4 * ((me // 2) % 2)
    core_id = me + 1 - 2 * (me % 2)
    upper, lower = pl.ds(0, cut), pl.ds(cut, cut)
    x_part, y_part = pl.ds(0, full), pl.ds(full, width)

    def outer_id(k):
        return ((a + k + outer) % outer) * 4 + rest

    def remote(src, dst, send, recv, where, axis="dp"):
        return pltpu.make_async_remote_copy(
            src_ref=src,
            dst_ref=dst,
            send_sem=send,
            recv_sem=recv,
            device_id={axis: where},
            device_id_type=pl.DeviceIdType.MESH,
        )

    def plane_copy(c, src, dst, rows_at, ident, where):
        first = isinstance(src, int) and src == 0
        near = src if isinstance(src, int) else dst
        source = mine_ref.at[c] if first else gather_ref.at[c % ring, near - 1]
        target = gather_ref.at[c % ring, dst - 1]
        if rows_at is not None:
            source, target = source.at[rows_at], target.at[rows_at]
        return remote(source, target, plane_send.at[c, ident], plane_recv.at[c, ident], where)

    def near_copy(c):
        return plane_copy(c, 0, 1, None, 0, inner_id)

    def far_copy(c, k):
        return plane_copy(c, 0, 2 * k, None, k, outer_id(-k))

    def top_copy(c, k):
        return plane_copy(c, 1, 2 * k + 1, upper, outer - 1 + k, outer_id(-k))

    def bottom_copy(c, k):
        return plane_copy(c, 2 * k, 2 * k + 1, lower, 2 * outer - 2 + k, inner_id)

    def core_copy(c, q):
        return plane_copy(c, q, half + q, None, 3 * outer - 2 + q, core_id)

    def ring_copy(k):
        where = (z - k + chunks) % chunks
        return remote(own_ref, mine_ref.at[k], ring_send.at[k], ring_recv.at[k], where, "tensor")

    others = range(1, outer)

    def first_hop(c):
        near_copy(c).start()
        for k in others:
            far_copy(c, k).start()
        core_copy(c, 0).start()

    def second_hop(c):
        near_copy(c).wait_recv()
        for k in others:
            top_copy(c, k).start()
        for k in others:
            far_copy(c, k).wait_recv()
            bottom_copy(c, k).start()
        for q in [1] + [2 * k for k in others]:
            core_copy(c, q).start()

    def third_hop(c):
        for k in others:
            top_copy(c, k).wait_recv()
            bottom_copy(c, k).wait_recv()
            core_copy(c, 2 * k + 1).start()

    def drain_gather(c):
        near_copy(c).wait_send()
        for k in others:
            far_copy(c, k).wait_send()
            top_copy(c, k).wait_send()
            bottom_copy(c, k).wait_send()
        for q in range(half):
            core_copy(c, q).wait_send()

    def sum_copy(c, src, dst, ident, where):
        return remote(src, dst, sum_send.at[c, ident], sum_recv.at[c, ident], where)

    def swap_copy(c, q):
        return sum_copy(c, other_ref.at[c % 2, q], core_in.at[c % 2, q], q, core_id)

    def both_at(c, q, rows_at):
        return both_ref.at[c % 2, q, rows_at]

    def up_copy(c, k):
        ident = half + k - 1
        return sum_copy(c, both_at(c, 2 * k + 1, upper), top_in.at[c % 2, k - 1], ident, outer_id(k))

    def down_copy(c, k):
        ident = half + outer - 1 + k - 1
        source = both_at(c, 2 * k + 1, lower)
        return sum_copy(c, source, bottom_in.at[c % 2, k - 1], ident, inner_id)

    def home_near(c, part):
        rows_at = (upper, lower)[part]
        ident = half + 2 * outer - 2 + part
        return sum_copy(c, both_at(c, 1, rows_at), near_in.at[c % 2, rows_at], ident, inner_id)

    def home_far(c, k, part):
        rows_at = (upper, lower)[part]
        ident = half + 2 * outer + 2 * (k - 1) + part
        target = far_in.at[c % 2, k - 1, rows_at]
        return sum_copy(c, both_at(c, 2 * k, rows_at), target, ident, outer_id(k))

    def last_copy(c):
        where = (z + c) % chunks
        return remote(ring_out.at[c], ring_in.at[c], last_send.at[c], last_recv.at[c], where, "tensor")

    def local(src, dst, sem):
        return pltpu.make_async_copy(src, dst, sem)

    def together(*copies):
        for copy in copies:
            copy.start()
        for copy in copies:
            copy.wait()

    def fold_halves(c):
        for k in others:
            up_copy(c, k).wait_recv()
            down_copy(c, k).wait_recv()
            copies = [
                local(both_at(c, 2 * k, lower), in_s.at[0, lower], fold_sem.at[0]),
                local(top_in.at[c % 2, k - 1], in_s.at[1, upper], fold_sem.at[1]),
                local(bottom_in.at[c % 2, k - 1], in_s.at[1, lower], fold_sem.at[2]),
            ]
            if k == 1:
                copies.append(local(both_at(c, 1, upper), in_s.at[0, upper], fold_sem.at[3]))
            together(*copies)

            @pl.loop(0, rows // 16)
            def _(i):
                at = pl.ds(pl.multiple_of(i * 16, 16), 16)
                in_s[0, at, :] = low(wide(in_s[0, at, :]) + wide(in_s[1, at, :]))

            together(local(in_s.at[0, lower], both_at(c, 2 * k, lower), fold_sem.at[0]))
        together(local(in_s.at[0, upper], both_at(c, 1, upper), fold_sem.at[0]))
        for k in others:
            home_far(c, k, 1).start()
        home_near(c, 0).start()

    def fold_home(c):
        for part in (0, 1):
            home_near(c, part).wait_recv()
        together(
            local(both_ref.at[c % 2, 0], in_s.at[0], fold_sem.at[0]),
            local(near_in.at[c % 2], in_s.at[1], fold_sem.at[1]),
        )

        @pl.loop(0, rows // 16)
        def _(i):
            at = pl.ds(pl.multiple_of(i * 16, 16), 16)
            in_s[0, at, :] = low(wide(in_s[0, at, :]) + wide(in_s[1, at, :]))

        for k in others:
            for part in (0, 1):
                home_far(c, k, part).wait_recv()
            together(local(far_in.at[c % 2, k - 1], in_s.at[1], fold_sem.at[1]))

            @pl.loop(0, rows // 16)
            def _(i):
                at = pl.ds(pl.multiple_of(i * 16, 16), 16)
                in_s[0, at, :] = low(wide(in_s[0, at, :]) + wide(in_s[1, at, :]))

        together(local(in_s.at[0], ring_out.at[c], fold_sem.at[0]))

    def drain_sum(c):
        for q in range(half):
            swap_copy(c, q).wait_send()
        for k in others:
            up_copy(c, k).wait_send()
            down_copy(c, k).wait_send()
            for part in (0, 1):
                home_far(c, k, part).wait_send()
        for part in (0, 1):
            home_near(c, part).wait_send()

    def fetch(c, at):
        q, side, slot = at // 2, at % 2, at % 2
        r = side * half + q

        @pl.when(side == 1)
        def _():
            core_copy(c, q).wait_recv()

        rows_at = pl.ds(pl.multiple_of(((z + c) % chunks) * rows, rows), rows)
        @pl.when(r == 0)
        def _():
            local(mine_ref.at[c], in_s.at[slot, :, x_part], x_sem.at[slot]).start()

        @pl.when(r > 0)
        def _():
            source = gather_ref.at[c % ring, jnp.maximum(r - 1, 0)]
            local(source, in_s.at[slot, :, x_part], x_sem.at[slot]).start()

        for place, cot_ref in enumerate(cot_refs):

            @pl.when(r == place)
            def _():
                local(cot_ref.at[rows_at], in_s.at[slot, :, y_part], c_sem.at[slot]).start()


    def fetched(slot):
        local(mine_ref.at[0], in_s.at[slot, :, x_part], x_sem.at[slot]).wait()
        local(cot_refs[0].at[pl.ds(0, rows)], in_s.at[slot, :, y_part], c_sem.at[slot]).wait()

    def load(e, slot):
        return local(acc_ref.at[e], acc_s.at[slot], load_sem.at[slot])

    def store(e, slot):
        return local(acc_s.at[slot], acc_ref.at[e], store_sem.at[slot])

    @pl.when((j == 0) & (s == 0))
    def _():
        barrier = pltpu.get_barrier_semaphore()
        peers = [("dp", core_id), ("dp", inner_id)] + [("dp", outer_id(k)) for k in others]
        peers += [("tensor", (z + k) % chunks) for k in range(1, chunks)]
        for axis, where in peers:
            pl.semaphore_signal(
                barrier, inc=1, device_id={axis: where}, device_id_type=pl.DeviceIdType.MESH
            )
        pl.semaphore_wait(barrier, len(peers))
        for k in range(1, chunks):
            ring_copy(k).start()
        together(local(own_ref, in_s.at[0, :, x_part], fold_sem.at[0]))
        together(local(in_s.at[0, :, x_part], mine_ref.at[0], fold_sem.at[0]))
        first_hop(0)
        fetch(0, 0)
        second_hop(0)
        ring_copy(1).wait_recv()
        first_hop(1)

    @pl.when((s == 0) & (j > 0))
    def _():
        load(0, 0).start()

    @pl.when((j == 0) & (s == 4))
    def _():
        third_hop(0)

    @pl.when((s == blocks + 1) & (j + 1 < chunks))
    def _():
        second_hop(j + 1)

    @pl.when((s == blocks + experts) & (j + 1 < chunks))
    def _():
        third_hop(j + 1)

    @pl.when((s == blocks + 2) & (j >= 1))
    def _():
        fold_halves(j - 1)

    @pl.when((s == blocks + 2) & (j + 2 < chunks))
    def _():
        ring_copy(j + 2).wait_recv()
        first_hop(j + 2)

    @pl.when(s == blocks + 3)
    def _():
        drain_gather(j)

    @pl.when((s == blocks + experts + half - 1) & (j >= 1))
    def _():
        fold_home(j - 1)

        @pl.when(j >= 2)
        def _():
            last_copy(j - 1).start()

        drain_sum(j - 1)

    @pl.when(s < blocks)
    def _():
        slot = s % 2

        @pl.when(s + 1 < blocks)
        def _():
            fetch(j, s + 1)

        fetched(slot)
        meta = in_s[slot, :, width:full]
        picks = (dot_nt(pick_ref[...], meta) == 0.0).astype(jnp.bfloat16)
        at = pl.multiple_of(s * slots, slots)
        got = low(dot_nn(picks, in_s[slot, :, :full]))
        cot = low(dot_nn(picks, in_s[slot, :, full:]))
        for e in range(experts):
            part = slice(e * slots, (e + 1) * slots)
            rows_s[e, pl.ds(at, slots), :] = got[part, :width]
            mrow_s[e, pl.ds(at, slots), :] = got[part, width:]
            crow_s[e, pl.ds(at, slots), :] = cot[part]
        meta_s[s] = meta

    @pl.when((s >= blocks) & (s < blocks + experts))
    def _():
        e = s - blocks
        slot = e % 2
        tile = largest_tile(total, 320, 16)
        expert = me * experts + e
        wg = wg_ref[0]
        wu = wu_ref[0]
        wd = wd_ref[0]

        @pl.loop(0, total // tile)
        def _(m):
            ds = pl.ds(pl.multiple_of(m * tile, tile), tile)
            picked_rows = rows_s[e, ds, :]
            gate = dot_nn(picked_rows, wg)
            up = dot_nn(picked_rows, wu)
            grad_act = dot_nt(crow_s[e, ds, :], wd)
            meta = wide(mrow_s[e, ds, :])
            column = lax.broadcasted_iota(jnp.int32, meta.shape, 1)
            wanted = (column == expert) | (column == expert + all_experts)
            weight = jnp.sum(jnp.where(wanted, meta, 0.0), axis=1, keepdims=True)
            sig = jax.nn.sigmoid(gate)
            silu = gate * sig
            act = silu * up
            g_pick = jnp.sum(act * grad_act, axis=1, keepdims=True)
            scaled = weight * grad_act
            aw_s[ds, :] = low(weight * act)
            gg_s[ds, :] = low(scaled * up * sig * (1.0 + gate * (1.0 - sig)))
            gu_s[ds, :] = low(scaled * silu)
            mrow_s[e, ds, :] = low(jnp.where(column == expert, g_pick, 0.0))

        @pl.when(e >= 1)
        def _():
            store(e - 1, 1 - slot).wait()

        @pl.when(j == 0)
        def _():
            acc_s[slot] = jnp.zeros(acc_s.shape[1:], jnp.float32)

        @pl.when(j > 0)
        def _():
            load(e, slot).wait()

            @pl.when(e + 1 < experts)
            def _():
                load(e + 1, 1 - slot).start()

        cols = largest_tile(width, 512, 128)
        for which, (left, right) in enumerate(((gg_s, rows_s), (gu_s, rows_s), (aw_s, crow_s))):
            turn_s[...] = left[...].T

            @pl.loop(0, width // cols)
            def _(n):
                ds = pl.ds(pl.multiple_of(n * cols, cols), cols)
                add = dot_nn(turn_s[...], right[e, :, ds])
                acc_s[slot, which, :, ds] = acc_s[slot, which, :, ds] + add

        store(e, slot).start()

        @pl.loop(0, total // tile)
        def _(m):
            ds = pl.ds(pl.multiple_of(m * tile, tile), tile)
            crow_s[e, ds, :] = low(dot_nn(aw_s[ds, :], wd))
            rows_s[e, ds, :] = low(dot_nt(gg_s[ds, :], wg) + dot_nt(gu_s[ds, :], wu))

    first = blocks + experts

    def written(c, o):
        q, slot = half - 1 - o % half, o % 2

        @pl.when(o < half)
        def _():
            local(out_s.at[slot], other_ref.at[c % 2, q], out_sem.at[slot]).wait()
            swap_copy(c, q).start()

        @pl.when(o >= half)
        def _():
            local(out_s.at[slot], both_ref.at[c % 2, q], out_sem.at[slot]).wait()

        for k in others:

            @pl.when((o >= half) & (q == 2 * k + 1))
            def _():
                up_copy(c, k).start()
                down_copy(c, k).start()

            @pl.when((o >= half) & (q == 2 * k))
            def _():
                home_far(c, k, 0).start()

        @pl.when((o >= half) & (q == 1))
        def _():
            home_near(c, 1).start()

    @pl.when(s >= first)
    def _():
        o = s - first
        slot = o % 2
        q = half - 1 - o % half
        side = 1 - o // half
        place = 2 * q + side
        at = pl.multiple_of(place * slots, slots)

        @pl.when(o >= 1)
        def _():
            written(j, o - 1)

        @pl.when((o >= half - 1) & (o < 2 * half - 1))
        def _():
            coming = half - 1 - (o + 1) % half
            swap_copy(j, coming).wait_recv()
            local(core_in.at[j % 2, coming], in_s.at[1 - slot], x_sem.at[1 - slot]).start()

        @pl.when(o >= half)
        def _():
            local(core_in.at[j % 2, q], in_s.at[slot], x_sem.at[slot]).wait()

        @pl.when(o < half)
        def _():
            in_s[slot] = jnp.zeros((rows, span), jnp.bfloat16)

        picks = (dot_nt(meta_s[place], pick_ref[...]) == 0.0).astype(jnp.bfloat16)
        flat = (experts * slots, width)
        g = dot_nn(picks, rows_s[:, pl.ds(at, slots), :].reshape(flat))
        out_s[slot, :, :width] = low(g + wide(in_s[slot, :, :width]))
        flat = (experts * slots, extra)
        p = dot_nn(picks, mrow_s[:, pl.ds(at, slots), :].reshape(flat))
        out_s[slot, :, width:full] = low(p + wide(in_s[slot, :, width:full]))
        flat = (experts * slots, width)
        y = dot_nn(picks, crow_s[:, pl.ds(at, slots), :].reshape(flat))
        out_s[slot, :, full:] = low(y + wide(in_s[slot, :, full:]))

        @pl.when(o < half)
        def _():
            local(out_s.at[slot], other_ref.at[j % 2, q], out_sem.at[slot]).start()

        @pl.when(o >= half)
        def _():
            local(out_s.at[slot], both_ref.at[j % 2, q], out_sem.at[slot]).start()

        @pl.when(s == steps - 1)
        def _():
            written(j, o)
            store(experts - 1, (experts - 1) % 2).wait()

        @pl.when((s == steps - 1) & (j + 1 < chunks))
        def _():
            fetch(j + 1, 0)

    @pl.when((s == steps - 1) & (j == chunks - 1))
    def _():
        fold_halves(chunks - 1)
        fold_home(chunks - 1)
        last_copy(chunks - 1).start()
        drain_sum(chunks - 1)
        together(local(ring_out.at[0], in_s.at[0], fold_sem.at[0]))
        for k in range(1, chunks):
            last_copy(k).wait_recv()
            together(local(ring_in.at[k], in_s.at[1], fold_sem.at[1]))

            @pl.loop(0, rows // 16)
            def _(i):
                at = pl.ds(pl.multiple_of(i * 16, 16), 16)
                in_s[0, at, :] = low(wide(in_s[0, at, :]) + wide(in_s[1, at, :]))

        together(local(in_s.at[0], final_ref, fold_sem.at[0]))
        for k in range(1, chunks):
            last_copy(k).wait_send()
            ring_copy(k).wait_send()


def moe(own, cot, picks, wg, wu, wd, outer, chunks, slots, all_experts):
    rows, full = own.shape
    width = cot[0].shape[1]
    extra = full - width
    span = full + width
    experts, _, hidden = wg.shape
    blocks, half, cut = 4 * outer, 2 * outer, rows // 2
    total = blocks * slots
    sizes = (outer, chunks, experts, slots, rows, width, extra, all_experts)

    def expert_at(j, s):
        return (jnp.clip(s - blocks, 0, experts - 1), 0, 0)

    anywhere = pl.BlockSpec(memory_space=pl.ANY)
    in_specs = [
        *[anywhere] * (1 + len(cot)),
        pl.BlockSpec(picks.shape, lambda j, s: (0, 0)),
        pl.BlockSpec((1, width, hidden), expert_at),
        pl.BlockSpec((1, width, hidden), expert_at),
        pl.BlockSpec((1, hidden, width), expert_at),
    ]
    bf16 = jnp.bfloat16
    shapes = [
        ((rows, span), bf16),
        ((experts, 3, hidden, width), jnp.float32),
        ((chunks, rows, full), bf16),
        ((chunks if chunks <= 4 else 3, blocks - 1, rows, full), bf16),
        ((2, half, rows, span), bf16),
        ((2, half, rows, span), bf16),
        ((2, half, rows, span), bf16),
        ((2, outer - 1, cut, span), bf16),
        ((2, outer - 1, cut, span), bf16),
        ((2, rows, span), bf16),
        ((2, outer - 1, rows, span), bf16),
        ((chunks, rows, span), bf16),
        ((chunks, rows, span), bf16),
    ]
    dma = pltpu.SemaphoreType.DMA
    gathers, sums = 5 * outer - 2, 6 * outer - 2
    scratch = [
        pltpu.VMEM((2, rows, span), bf16),
        pltpu.VMEM((2, rows, span), bf16),
        pltpu.VMEM((experts, total, width), bf16),
        pltpu.VMEM((experts, total, width), bf16),
        pltpu.VMEM((experts, total, extra), bf16),
        pltpu.VMEM((blocks, rows, extra), bf16),
        pltpu.VMEM((total, hidden), bf16),
        pltpu.VMEM((total, hidden), bf16),
        pltpu.VMEM((total, hidden), bf16),
        pltpu.VMEM((hidden, total), bf16),
        pltpu.VMEM((2, 3, hidden, width), jnp.float32),
        dma((2,)),
        dma((2,)),
        dma((2,)),
        dma((2,)),
        dma((2,)),
        dma((4,)),
        dma((chunks, gathers)),
        dma((chunks, gathers)),
        dma((chunks, sums)),
        dma((chunks, sums)),
        dma((chunks,)),
        dma((chunks,)),
        dma((chunks,)),
        dma((chunks,)),
    ]
    flops = 2 * chunks * experts * total * width * (hidden * 9 + 4 * rows)
    results = pl.pallas_call(
        functools.partial(moe_kernel, sizes),
        grid=(chunks, 2 * blocks + experts),
        in_specs=in_specs,
        out_specs=[anywhere] * len(shapes),
        out_shape=[jax.ShapeDtypeStruct(*shape) for shape in shapes],
        scratch_shapes=scratch,
        compiler_params=pltpu.CompilerParams(
            dimension_semantics=("arbitrary", "arbitrary"),
            vmem_limit_bytes=66_500_000,
            collective_id=0,
            has_side_effects=True,
        ),
        cost_estimate=pl.CostEstimate(
            flops=flops, bytes_accessed=blocks * chunks * rows * full * 8, transcendentals=0
        ),
        name="moe",
    )(own, *cot, picks, wg, wu, wd)
    return results[:2]


def wide(values):
    return values.astype(jnp.float32)


def low(values):
    return values.astype(jnp.bfloat16)


def tie(*values):
    return lax.optimization_barrier(values)


def ring_sum(values, count):
    total = values
    for step in range(1, count):
        pairs = [(i, (i + step) % count) for i in range(count)]
        total = total + lax.ppermute(values, "tensor", pairs)
    return total


def pick(values, at, axis):
    return lax.dynamic_index_in_dim(values, at, axis, keepdims=False)


class Plane:
    def __init__(self, count):
        self.outer = count // 4
        everyone = range(count)
        self.core = [(i, i ^ 1) for i in everyone]
        self.inner = [(i, i ^ 2) for i in everyone]
        self.count = count

    def pull(self, values, k):
        pairs = [((i + 4 * k) % self.count, i) for i in range(self.count)]
        return lax.ppermute(values, "dp", pairs)

    def swap_inner(self, values):
        return lax.ppermute(values, "dp", self.inner)

    def swap_core(self, values):
        return lax.ppermute(values, "dp", self.core)

    def push(self, values, k):
        pairs = [(i, (i + 4 * k) % self.count) for i in range(self.count)]
        return lax.ppermute(values, "dp", pairs)

    def fold_inner(self, parts, b, axis, kind):
        given = self.swap_inner(pick(parts, 1 - b, axis).astype(kind))
        return wide(pick(parts, b, axis)) + wide(given)

    def fold_outer(self, parts, a, kind):
        total = wide(pick(parts, a, 0))
        for k in range(1, self.outer):
            given = pick(parts, (a + k) % self.outer, 0).astype(kind)
            total = total + wide(self.push(given, k))
        return total

    def scatter(self, values, inner_first):
        kind = values.dtype
        index = lax.axis_index("dp")
        core, b, a = index % 2, index // 2 % 2, index // 4
        parts = values.reshape(self.outer, 2, 2, values.shape[0] // self.count, values.shape[1])
        given = self.swap_core(pick(parts, 1 - core, 2))
        parts = (wide(pick(parts, core, 2)) + wide(given)).astype(kind)
        if inner_first:
            return self.fold_outer(self.fold_inner(parts, b, 1, kind).astype(kind), a, kind)
        return self.fold_inner(self.fold_outer(parts, a, kind).astype(kind), b, 0, kind)

    def first(self, own):
        return self.swap_inner(own), [self.pull(own, k) for k in range(1, self.outer)]

    def second(self, near, fars):
        half = near.shape[0] // 2
        return [
            jnp.concatenate([self.pull(near[:half], k + 1), self.swap_inner(far[half:])], axis=0)
            for k, far in enumerate(fars)
        ]

    def third(self, own, near, fars, diagonals):
        mine = [own, near]
        for far, diagonal in zip(fars, diagonals):
            mine += [far, diagonal]
        return mine + [self.swap_core(part) for part in mine]


def per_device(
    tokens,
    lengths,
    routes,
    attn_gain,
    w_query,
    w_key,
    w_value,
    w_out,
    q_gain,
    k_gain,
    ffn_gain,
    router_weight,
    w_gate,
    w_up,
    w_down,
    cotangent,
):
    tensor_count = lax.axis_size("tensor")
    data_count = lax.axis_size("dp")
    tensor_rank = lax.axis_index("tensor")
    block_rows = tokens.shape[1]
    width = tokens.shape[2]
    full_length = block_rows * tensor_count
    route_count = routes.shape[2]
    local_experts = w_gate.shape[0]
    all_experts = local_experts * data_count
    head_dim = q_gain.shape[0]
    local_width = w_query.shape[1]
    capacity = max(2, (block_rows * route_count * 5 + 4 * all_experts - 1) // (4 * all_experts))
    query_rows = min(512, full_length)
    scale = head_dim ** (-0.5)
    own_start = tensor_rank * block_rows
    token_values = tokens[0].astype(jnp.float32)
    seq_length = lengths[0]
    own_valid = (own_start + jnp.arange(block_rows) < seq_length).astype(jnp.float32)
    key_valid = jnp.arange(full_length) < seq_length
    normed = rms_scale(token_values, attn_gain).astype(jnp.bfloat16)
    gathered = lax.all_gather(normed, "tensor", axis=0, tiled=True)
    plane = Plane(data_count)
    near, fars = plane.first(cotangent[0])
    core = lax.axis_index("dp") % 2
    depth = width // 2
    out_half = lax.dynamic_slice_in_dim(w_out, core * depth, depth, 0)
    gathered, near, fars, out_half = tie(gathered, near, fars, out_half)
    out_mine = lax.all_gather(out_half, "tensor", axis=0)
    query_unrotated = jnp.dot(gathered, w_query, preferred_element_type=jnp.float32)
    key_raw = jnp.dot(gathered, w_key, preferred_element_type=jnp.float32)
    value_raw = jnp.dot(gathered, w_value, preferred_element_type=jnp.float32)
    query_low = prepare(query_unrotated, q_gain).astype(jnp.bfloat16)
    key_low = prepare(key_raw, k_gain).astype(jnp.bfloat16)
    value_low = value_raw.astype(jnp.bfloat16).reshape(full_length, -1, head_dim)

    def block_scores(query_block):
        scores = (
            jnp.einsum("qhd,khd->hqk", query_block, key_low, preferred_element_type=jnp.float32)
            * scale
        )
        return jnp.where(key_valid[None, None, :], scores, NEG)

    mixed_parts = []
    log_totals = []
    for start in range(0, full_length, query_rows):
        scores = block_scores(query_low[start : start + query_rows])
        row_peak = jnp.max(scores, axis=-1, keepdims=True)
        powers = jnp.exp(scores - row_peak)
        total = jnp.sum(powers, axis=-1, keepdims=True)
        weights = (powers / total).astype(jnp.bfloat16)
        mixed_parts.append(
            jnp.einsum("hqk,khd->qhd", weights, value_low, preferred_element_type=jnp.float32)
        )
        log_totals.append(row_peak + jnp.log(total))
    attended = (
        jnp.concatenate(mixed_parts, axis=0).reshape(full_length, local_width).astype(jnp.bfloat16)
    )
    diagonals = plane.second(near, fars)
    attended, diagonals = tie(attended, diagonals)
    cot_all = plane.third(cotangent[0], near, fars, diagonals)
    heads_own = lax.all_to_all(
        attended.reshape(tensor_count, block_rows, local_width), "tensor", 0, 0
    )
    heads_own, out_mine = tie(heads_own, out_mine)
    out_other = plane.swap_core(out_mine)
    heads_own = heads_own.reshape(tensor_count, block_rows, local_width)

    def from_heads(out_weight):
        return sum(dot_nt(heads_own[t], out_weight[t]) for t in range(tensor_count))

    attn_mine, attn_other = from_heads(out_mine), from_heads(out_other)
    attn_own = jnp.where(
        core == 0,
        jnp.concatenate([attn_mine, attn_other], axis=1),
        jnp.concatenate([attn_other, attn_mine], axis=1),
    )
    residual = token_values + own_valid[:, None] * attn_own
    moe_own = rms_scale(residual, ffn_gain).astype(jnp.bfloat16)
    router_logits = jnp.dot(moe_own, router_weight, preferred_element_type=jnp.float32)
    own_probs = jax.nn.softmax(router_logits, axis=-1)
    own_routes = lax.dynamic_slice_in_dim(routes[0], own_start, block_rows, 0)
    onehot = own_routes[:, :, None] == jnp.arange(all_experts)[None, None, :]
    named = jnp.any(onehot, axis=1) & (own_valid[:, None] > 0.0)
    named_low = named.astype(jnp.bfloat16)
    before = jnp.arange(block_rows)[:, None] > jnp.arange(block_rows)[None, :]
    order = jnp.dot(before.astype(jnp.bfloat16), named_low, preferred_element_type=jnp.float32)
    place = jnp.where(named, order, -1.0).astype(jnp.bfloat16)
    weight = jnp.where(named, own_probs, 0.0)
    weight_high = weight.astype(jnp.bfloat16)
    weight_low = (weight - weight_high.astype(jnp.float32)).astype(jnp.bfloat16)
    used = 3 * all_experts + 1
    extra = (used + 127) // 128 * 128
    meta = jnp.concatenate(
        [
            weight_high,
            weight_low,
            place,
            jnp.ones((block_rows, 1), jnp.bfloat16),
            jnp.zeros((block_rows, extra - used), jnp.bfloat16),
        ],
        axis=1,
    )
    slots = (capacity + 15) // 16 * 16
    first_expert = lax.axis_index("dp") * local_experts
    slot_row = jnp.arange(local_experts * slots)[:, None]
    slot_column = jnp.arange(extra)[None, :]
    picks = jnp.where(
        slot_column == 2 * all_experts + first_expert + slot_row // slots,
        1.0,
        jnp.where(slot_column == 3 * all_experts, -(slot_row % slots).astype(jnp.float32), 0.0),
    ).astype(jnp.bfloat16)
    packed = jnp.concatenate([moe_own, meta], axis=1)
    combined, sums = moe(
        packed,
        cot_all,
        picks,
        w_gate,
        w_up,
        w_down,
        data_count // 4,
        tensor_count,
        slots,
        all_experts,
    )
    combined = wide(combined)
    grad_moe = combined[:, :width]
    grad_probs = combined[:, width : width + all_experts]
    output = low(residual + combined[:, width + extra :])
    grad_own = lax.dynamic_slice_in_dim(cotangent[0], own_start, block_rows, 0).astype(jnp.float32)
    grad_logits = (
        own_probs * (grad_probs - jnp.sum(own_probs * grad_probs, axis=-1, keepdims=True))
    ).astype(jnp.bfloat16)
    grad_moe = grad_moe + jnp.einsum(
        "re,de->rd", grad_logits, router_weight, preferred_element_type=jnp.float32
    )
    router_part = jnp.einsum("rd,re->de", moe_own, grad_logits, preferred_element_type=jnp.float32)
    ffn_pull = jax.vjp(rms_scale, residual, ffn_gain)[1]
    grad_res_norm, ffn_part = ffn_pull(grad_moe)
    grad_residual = grad_own + grad_res_norm
    grad_attn = (grad_residual * own_valid[:, None]).astype(jnp.bfloat16)
    attn_lower = lax.dynamic_slice_in_dim(grad_attn, core * depth, depth, 1)
    attn_upper = lax.dynamic_slice_in_dim(grad_attn, depth - core * depth, depth, 1)
    grad_heads = jnp.stack(
        [
            low(dot_nn(attn_lower, out_mine[t]) + dot_nn(attn_upper, out_other[t]))
            for t in range(tensor_count)
        ]
    )
    grad_mixed = lax.all_to_all(grad_heads, "tensor", 0, 0)
    grad_mixed, grad_attn = tie(grad_mixed, grad_attn)
    grad_attn_all = lax.all_gather(grad_attn, "tensor", axis=0, tiled=True)
    grad_mixed = grad_mixed.reshape(full_length, -1, head_dim)
    grad_query_parts = []
    grad_keys = jnp.zeros(key_low.shape, jnp.float32)
    grad_values = jnp.zeros(value_low.shape, jnp.float32)
    for order, start in enumerate(range(0, full_length, query_rows)):
        query_block = query_low[start : start + query_rows]
        grad_block = grad_mixed[start : start + query_rows]
        probs_block = jnp.exp(block_scores(query_block) - log_totals[order])
        probs_low = probs_block.astype(jnp.bfloat16)
        grad_values = grad_values + jnp.einsum(
            "hqk,qhd->khd", probs_low, grad_block, preferred_element_type=jnp.float32
        )
        grad_probs_block = jnp.einsum(
            "qhd,khd->hqk", grad_block, value_low, preferred_element_type=jnp.float32
        )
        delta = jnp.sum(probs_block * grad_probs_block, axis=-1, keepdims=True)
        grad_scores = (probs_block * (grad_probs_block - delta)).astype(jnp.bfloat16)
        grad_query_parts.append(
            jnp.einsum("hqk,khd->qhd", grad_scores, key_low, preferred_element_type=jnp.float32)
            * scale
        )
        grad_keys = (
            grad_keys
            + jnp.einsum(
                "hqk,qhd->khd", grad_scores, query_block, preferred_element_type=jnp.float32
            )
            * scale
        )
    grad_queries = jnp.concatenate(grad_query_parts, axis=0)
    query_pull = jax.vjp(prepare, query_unrotated, q_gain)[1]
    grad_query_raw, q_part = query_pull(grad_queries)
    key_pull = jax.vjp(prepare, key_raw, k_gain)[1]
    grad_key_raw, k_part = key_pull(grad_keys)
    grad_q_low = grad_query_raw.astype(jnp.bfloat16)
    grad_k_low = grad_key_raw.astype(jnp.bfloat16)
    grad_v_low = grad_values.reshape(full_length, local_width).astype(jnp.bfloat16)
    query_part = jnp.einsum("ld,lh->dh", gathered, grad_q_low, preferred_element_type=jnp.float32)
    key_part = jnp.einsum("ld,lh->dh", gathered, grad_k_low, preferred_element_type=jnp.float32)
    value_part = jnp.einsum("ld,lh->dh", gathered, grad_v_low, preferred_element_type=jnp.float32)
    from_query = jnp.einsum("lh,dh->ld", grad_q_low, w_query, preferred_element_type=jnp.float32)
    from_key = jnp.einsum("lh,dh->ld", grad_k_low, w_key, preferred_element_type=jnp.float32)
    from_value = jnp.einsum("lh,dh->ld", grad_v_low, w_value, preferred_element_type=jnp.float32)
    grad_gathered, grad_attn_all, sums, router_part = tie(
        low(from_query + from_key + from_value), grad_attn_all, sums, router_part
    )
    grad_normed = wide(
        lax.psum_scatter(grad_gathered, "tensor", scatter_dimension=0, tiled=True)
    )
    grad_gate = jnp.swapaxes(sums[:, 0], 1, 2)
    grad_up = jnp.swapaxes(sums[:, 1], 1, 2)
    grad_down = sums[:, 2]
    out_part = jnp.einsum("ld,lh->dh", grad_attn_all, attended, preferred_element_type=jnp.float32)
    attn_pull = jax.vjp(rms_scale, token_values, attn_gain)[1]
    grad_tok_norm, attn_part = attn_pull(grad_normed)
    grad_tokens = (grad_residual + grad_tok_norm).astype(jnp.bfloat16)
    grad_out = plane.scatter(low(out_part), True)
    grad_value = plane.scatter(low(value_part), False)
    grad_query = plane.scatter(low(query_part), True)
    grad_key = plane.scatter(low(key_part), False)
    routing = plane.scatter(jnp.concatenate([router_part, ffn_part[:, None]], axis=1), False)
    routing = ring_sum(routing, tensor_count)
    parts = [v.reshape(data_count, -1) for v in (attn_part, q_part, k_part)]
    gains = jnp.repeat(jnp.concatenate(parts, axis=1), tensor_count, axis=0)
    gains = jnp.sum(lax.all_to_all(gains, ("dp", "tensor"), 0, 0, tiled=True), axis=0)
    piece = width // data_count
    last = piece + head_dim // data_count
    return (
        output[None],
        grad_tokens[None],
        gains[:piece],
        grad_query,
        grad_key,
        grad_value,
        grad_out,
        gains[piece:last],
        gains[last:],
        routing[:, all_experts],
        routing[:, :all_experts],
        grad_gate,
        grad_up,
        grad_down,
    )


def solution(mesh):
    return jax.shard_map(
        per_device,
        mesh=mesh,
        in_specs=(
            P("dp", "tensor", None),
            P("dp"),
            P("dp", None, None),
            P(),
            P(None, "tensor"),
            P(None, "tensor"),
            P(None, "tensor"),
            P(None, "tensor"),
            P(),
            P(),
            P(),
            P(),
            P("dp", None, "tensor"),
            P("dp", None, "tensor"),
            P("dp", "tensor", None),
            P("dp", None, None),
        ),
        out_specs=(
            P("dp", "tensor", None),
            P("dp", "tensor", None),
            P("dp"),
            P("dp", "tensor"),
            P("dp", "tensor"),
            P("dp", "tensor"),
            P("dp", "tensor"),
            P("dp"),
            P("dp"),
            P("dp"),
            P("dp", None),
            P("dp", None, "tensor"),
            P("dp", None, "tensor"),
            P("dp", "tensor", None),
        ),
        check_vma=False,
    )
```

```python
import functools

import jax
import jax.numpy as jnp
from jax import lax
from jax.experimental import pallas as pl
from jax.experimental.pallas import tpu as pltpu
from jax.sharding import PartitionSpec as P

EPS = 1e-06
THETA = 50000.0
NEG = -1e30


def rms_scale(values, gain):
    return values * lax.rsqrt(jnp.mean(values * values, axis=-1, keepdims=True) + EPS) * gain


def rotate(values):
    length = values.shape[-3]
    half_dim = values.shape[-1] // 2
    positions = jnp.arange(length).astype(jnp.float32)
    rates = THETA ** (-jnp.arange(half_dim).astype(jnp.float32) / half_dim)
    angles = positions[:, None] * rates[None, :]
    cosine = jnp.cos(angles)[:, None, :]
    sine = jnp.sin(angles)[:, None, :]
    first = values[..., :half_dim]
    second = values[..., half_dim:]
    return jnp.concatenate(
        [first * cosine - second * sine, second * cosine + first * sine], axis=-1
    )


def prepare(raw, gain):
    shaped = raw.reshape(raw.shape[0], -1, gain.shape[0])
    return rotate(rms_scale(shaped, gain))


def dot_nt(a, b):
    return lax.dot_general(a, b, (((1,), (1,)), ((), ())), preferred_element_type=jnp.float32)


def dot_nn(a, b):
    return jnp.dot(a, b, preferred_element_type=jnp.float32)


def largest_tile(total, limit, unit):
    best = unit
    for tile in range(unit, limit + 1, unit):
        if total % tile == 0:
            best = tile
    return best


def moe_kernel(
    sizes,
    own_ref,
    *others_refs,
):
    blocks = 4 * sizes[0]
    moe_body(sizes, own_ref, others_refs[:blocks], *others_refs[blocks:])


def moe_body(
    sizes,
    own_ref,
    cot_refs,
    pick_ref,
    wg_ref,
    wu_ref,
    wd_ref,
    final_ref,
    acc_ref,
    mine_ref,
    gather_ref,
    other_ref,
    both_ref,
    core_in,
    top_in,
    bottom_in,
    near_in,
    far_in,
    ring_out,
    ring_in,
    in_s,
    out_s,
    rows_s,
    crow_s,
    mrow_s,
    meta_s,
    aw_s,
    gg_s,
    gu_s,
    turn_s,
    acc_s,
    load_sem,
    store_sem,
    x_sem,
    c_sem,
    out_sem,
    fold_sem,
    plane_send,
    plane_recv,
    sum_send,
    sum_recv,
    ring_send,
    ring_recv,
    last_send,
    last_recv,
):
    outer, chunks, experts, slots, rows, width, extra, all_experts = sizes
    blocks, half, cut = 4 * outer, 2 * outer, rows // 2
    full = width + extra
    span = full + width
    total = blocks * slots
    ring = gather_ref.shape[0]
    j = pl.program_id(0)
    s = pl.program_id(1)
    steps = 2 * blocks + experts
    me = lax.axis_index("dp")
    z = lax.axis_index("tensor")
    a, rest = me // 4, me % 4
    inner_id = me + 2 - 4 * ((me // 2) % 2)
    core_id = me + 1 - 2 * (me % 2)
    upper, lower = pl.ds(0, cut), pl.ds(cut, cut)
    x_part, y_part = pl.ds(0, full), pl.ds(full, width)

    def outer_id(k):
        return ((a + k + outer) % outer) * 4 + rest

    def remote(src, dst, send, recv, where, axis="dp"):
        return pltpu.make_async_remote_copy(
            src_ref=src,
            dst_ref=dst,
            send_sem=send,
            recv_sem=recv,
            device_id={axis: where},
            device_id_type=pl.DeviceIdType.MESH,
        )

    def plane_copy(c, src, dst, rows_at, ident, where):
        first = isinstance(src, int) and src == 0
        near = src if isinstance(src, int) else dst
        source = mine_ref.at[c] if first else gather_ref.at[c % ring, near - 1]
        target = gather_ref.at[c % ring, dst - 1]
        if rows_at is not None:
            source, target = source.at[rows_at], target.at[rows_at]
        return remote(source, target, plane_send.at[c, ident], plane_recv.at[c, ident], where)

    def near_copy(c):
        return plane_copy(c, 0, 1, None, 0, inner_id)

    def far_copy(c, k):
        return plane_copy(c, 0, 2 * k, None, k, outer_id(-k))

    def top_copy(c, k):
        return plane_copy(c, 1, 2 * k + 1, upper, outer - 1 + k, outer_id(-k))

    def bottom_copy(c, k):
        return plane_copy(c, 2 * k, 2 * k + 1, lower, 2 * outer - 2 + k, inner_id)

    def core_copy(c, q):
        return plane_copy(c, q, half + q, None, 3 * outer - 2 + q, core_id)

    def column(c):
        return (z + c + 1) % chunks

    def ring_copy(k):
        where = (z - k - 1 + chunks) % chunks
        return remote(own_ref, mine_ref.at[k], ring_send.at[k], ring_recv.at[k], where, "tensor")

    others = range(1, outer)

    def first_hop(c):
        near_copy(c).start()
        for k in others:
            far_copy(c, k).start()
        core_copy(c, 0).start()

    def second_hop(c):
        near_copy(c).wait_recv()
        for k in others:
            top_copy(c, k).start()
        for k in others:
            far_copy(c, k).wait_recv()
            bottom_copy(c, k).start()
        for q in [1] + [2 * k for k in others]:
            core_copy(c, q).start()

    def third_hop(c):
        for k in others:
            top_copy(c, k).wait_recv()
            bottom_copy(c, k).wait_recv()
            core_copy(c, 2 * k + 1).start()

    def drain_gather(c):
        near_copy(c).wait_send()
        for k in others:
            far_copy(c, k).wait_send()
            top_copy(c, k).wait_send()
            bottom_copy(c, k).wait_send()
        for q in range(half):
            core_copy(c, q).wait_send()

    def sum_copy(c, src, dst, ident, where):
        return remote(src, dst, sum_send.at[c, ident], sum_recv.at[c, ident], where)

    def swap_copy(c, q):
        return sum_copy(c, other_ref.at[c % 2, q], core_in.at[c % 2, q], q, core_id)

    def both_at(c, q, rows_at):
        return both_ref.at[c % 2, q, rows_at]

    def up_copy(c, k):
        ident = half + k - 1
        return sum_copy(c, both_at(c, 2 * k + 1, upper), top_in.at[c % 2, k - 1], ident, outer_id(k))

    def down_copy(c, k):
        ident = half + outer - 1 + k - 1
        source = both_at(c, 2 * k + 1, lower)
        return sum_copy(c, source, bottom_in.at[c % 2, k - 1], ident, inner_id)

    def home_near(c, part):
        rows_at = (upper, lower)[part]
        ident = half + 2 * outer - 2 + part
        return sum_copy(c, both_at(c, 1, rows_at), near_in.at[c % 2, rows_at], ident, inner_id)

    def home_far(c, k, part):
        rows_at = (upper, lower)[part]
        ident = half + 2 * outer + 2 * (k - 1) + part
        target = far_in.at[c % 2, k - 1, rows_at]
        return sum_copy(c, both_at(c, 2 * k, rows_at), target, ident, outer_id(k))

    def last_copy(c):
        source, target = ring_out.at[c], ring_in.at[c]
        return remote(source, target, last_send.at[c], last_recv.at[c], column(c), "tensor")

    def local(src, dst, sem):
        return pltpu.make_async_copy(src, dst, sem)

    def together(*copies):
        for copy in copies:
            copy.start()
        for copy in copies:
            copy.wait()

    def fold_halves(c):
        for k in others:
            up_copy(c, k).wait_recv()
            down_copy(c, k).wait_recv()
            copies = [
                local(both_at(c, 2 * k, lower), in_s.at[0, lower], fold_sem.at[0]),
                local(top_in.at[c % 2, k - 1], in_s.at[1, upper], fold_sem.at[1]),
                local(bottom_in.at[c % 2, k - 1], in_s.at[1, lower], fold_sem.at[2]),
            ]
            if k == 1:
                copies.append(local(both_at(c, 1, upper), in_s.at[0, upper], fold_sem.at[3]))
            together(*copies)

            @pl.loop(0, rows // 16)
            def _(i):
                at = pl.ds(pl.multiple_of(i * 16, 16), 16)
                in_s[0, at, :] = low(wide(in_s[0, at, :]) + wide(in_s[1, at, :]))

            together(local(in_s.at[0, lower], both_at(c, 2 * k, lower), fold_sem.at[0]))
        together(local(in_s.at[0, upper], both_at(c, 1, upper), fold_sem.at[0]))
        for k in others:
            home_far(c, k, 1).start()
        home_near(c, 0).start()

    def fold_home(c):
        for part in (0, 1):
            home_near(c, part).wait_recv()
        together(
            local(both_ref.at[c % 2, 0], in_s.at[0], fold_sem.at[0]),
            local(near_in.at[c % 2], in_s.at[1], fold_sem.at[1]),
        )

        @pl.loop(0, rows // 16)
        def _(i):
            at = pl.ds(pl.multiple_of(i * 16, 16), 16)
            in_s[0, at, :] = low(wide(in_s[0, at, :]) + wide(in_s[1, at, :]))

        for k in others:
            for part in (0, 1):
                home_far(c, k, part).wait_recv()
            together(local(far_in.at[c % 2, k - 1], in_s.at[1], fold_sem.at[1]))

            @pl.loop(0, rows // 16)
            def _(i):
                at = pl.ds(pl.multiple_of(i * 16, 16), 16)
                in_s[0, at, :] = low(wide(in_s[0, at, :]) + wide(in_s[1, at, :]))


    def drain_sum(c):
        for q in range(half):
            swap_copy(c, q).wait_send()
        for k in others:
            up_copy(c, k).wait_send()
            down_copy(c, k).wait_send()
            for part in (0, 1):
                home_far(c, k, part).wait_send()
        for part in (0, 1):
            home_near(c, part).wait_send()

    def fetch(c, at):
        q, side, slot = at // 2, at % 2, at % 2
        r = side * half + q

        @pl.when(side == 1)
        def _():
            core_copy(c, q).wait_recv()

        rows_at = pl.ds(pl.multiple_of(column(c) * rows, rows), rows)
        @pl.when(r == 0)
        def _():
            local(mine_ref.at[c], in_s.at[slot, :, x_part], x_sem.at[slot]).start()

        @pl.when(r > 0)
        def _():
            source = gather_ref.at[c % ring, jnp.maximum(r - 1, 0)]
            local(source, in_s.at[slot, :, x_part], x_sem.at[slot]).start()

        for place, cot_ref in enumerate(cot_refs):

            @pl.when(r == place)
            def _():
                local(cot_ref.at[rows_at], in_s.at[slot, :, y_part], c_sem.at[slot]).start()


    def fetched(slot):
        local(mine_ref.at[0], in_s.at[slot, :, x_part], x_sem.at[slot]).wait()
        local(cot_refs[0].at[pl.ds(0, rows)], in_s.at[slot, :, y_part], c_sem.at[slot]).wait()

    def load(e, slot):
        return local(acc_ref.at[e], acc_s.at[slot], load_sem.at[slot])

    def store(e, slot):
        return local(acc_s.at[slot], acc_ref.at[e], store_sem.at[slot])

    @pl.when((j == 0) & (s == 0))
    def _():
        barrier = pltpu.get_barrier_semaphore()
        peers = [("dp", core_id), ("dp", inner_id)] + [("dp", outer_id(k)) for k in others]
        peers += [("tensor", (z + k) % chunks) for k in range(1, chunks)]
        for axis, where in peers:
            pl.semaphore_signal(
                barrier, inc=1, device_id={axis: where}, device_id_type=pl.DeviceIdType.MESH
            )
        pl.semaphore_wait(barrier, len(peers))
        ring_copy(0).start()
        together(local(own_ref, in_s.at[0, :, x_part], fold_sem.at[0]))
        together(local(in_s.at[0, :, x_part], mine_ref.at[chunks - 1], fold_sem.at[0]))
        ring_copy(0).wait_recv()
        for k in range(1, chunks - 1):
            ring_copy(k).start()
        first_hop(0)
        fetch(0, 0)
        second_hop(0)

    @pl.when((s == 0) & (j > 0))
    def _():
        load(0, 0).start()

    @pl.when((j == 0) & (s == 4))
    def _():
        third_hop(0)
        if chunks > 2:
            ring_copy(1).wait_recv()
        first_hop(1)

    @pl.when((s == blocks + experts) & (j + 1 < chunks))
    def _():
        third_hop(j + 1)

    @pl.when((s == blocks + 2) & (j >= 1))
    def _():
        fold_halves(j - 1)

    @pl.when((s == blocks + 2) & (j + 1 < chunks))
    def _():
        second_hop(j + 1)

    @pl.when((s == blocks + 2) & (j + 3 < chunks))
    def _():
        ring_copy(j + 2).wait_recv()

    @pl.when((s == blocks + 2) & (j + 2 < chunks))
    def _():
        first_hop(j + 2)

    @pl.when(s == blocks + 3)
    def _():
        drain_gather(j)

    @pl.when((s == blocks + experts + half - 1) & (j >= 1))
    def _():
        fold_home(j - 1)
        together(local(in_s.at[0], ring_out.at[j - 1], fold_sem.at[0]))
        last_copy(j - 1).start()
        drain_sum(j - 1)

    @pl.when(s < blocks)
    def _():
        slot = s % 2

        @pl.when(s + 1 < blocks)
        def _():
            fetch(j, s + 1)

        fetched(slot)
        meta = in_s[slot, :, width:full]
        picks = (dot_nt(pick_ref[...], meta) == 0.0).astype(jnp.bfloat16)
        at = pl.multiple_of(s * slots, slots)
        got = low(dot_nn(picks, in_s[slot, :, :full]))
        cot = low(dot_nn(picks, in_s[slot, :, full:]))
        for e in range(experts):
            part = slice(e * slots, (e + 1) * slots)
            rows_s[e, pl.ds(at, slots), :] = got[part, :width]
            mrow_s[e, pl.ds(at, slots), :] = got[part, width:]
            crow_s[e, pl.ds(at, slots), :] = cot[part]
        meta_s[s] = meta

    @pl.when((s >= blocks) & (s < blocks + experts))
    def _():
        e = s - blocks
        slot = e % 2
        tile = largest_tile(total, 320, 16)
        expert = me * experts + e
        wg = wg_ref[0]
        wu = wu_ref[0]
        wd = wd_ref[0]

        @pl.loop(0, total // tile)
        def _(m):
            ds = pl.ds(pl.multiple_of(m * tile, tile), tile)
            picked_rows = rows_s[e, ds, :]
            gate = dot_nn(picked_rows, wg)
            up = dot_nn(picked_rows, wu)
            grad_act = dot_nt(crow_s[e, ds, :], wd)
            meta = wide(mrow_s[e, ds, :])
            column = lax.broadcasted_iota(jnp.int32, meta.shape, 1)
            wanted = (column == expert) | (column == expert + all_experts)
            weight = jnp.sum(jnp.where(wanted, meta, 0.0), axis=1, keepdims=True)
            sig = jax.nn.sigmoid(gate)
            silu = gate * sig
            act = silu * up
            g_pick = jnp.sum(act * grad_act, axis=1, keepdims=True)
            scaled = weight * grad_act
            aw_s[ds, :] = low(weight * act)
            gg_s[ds, :] = low(scaled * up * sig * (1.0 + gate * (1.0 - sig)))
            gu_s[ds, :] = low(scaled * silu)
            mrow_s[e, ds, :] = low(jnp.where(column == expert, g_pick, 0.0))

        @pl.when(e >= 1)
        def _():
            store(e - 1, 1 - slot).wait()

        @pl.when(j == 0)
        def _():
            acc_s[slot] = jnp.zeros(acc_s.shape[1:], jnp.float32)

        @pl.when(j > 0)
        def _():
            load(e, slot).wait()

            @pl.when(e + 1 < experts)
            def _():
                load(e + 1, 1 - slot).start()

        cols = largest_tile(width, 512, 128)
        for which, (left, right) in enumerate(((gg_s, rows_s), (gu_s, rows_s), (aw_s, crow_s))):
            turn_s[...] = left[...].T

            @pl.loop(0, width // cols)
            def _(n):
                ds = pl.ds(pl.multiple_of(n * cols, cols), cols)
                add = dot_nn(turn_s[...], right[e, :, ds])
                acc_s[slot, which, :, ds] = acc_s[slot, which, :, ds] + add

        store(e, slot).start()

        @pl.loop(0, total // tile)
        def _(m):
            ds = pl.ds(pl.multiple_of(m * tile, tile), tile)
            crow_s[e, ds, :] = low(dot_nn(aw_s[ds, :], wd))
            rows_s[e, ds, :] = low(dot_nt(gg_s[ds, :], wg) + dot_nt(gu_s[ds, :], wu))

    first = blocks + experts

    def written(c, o):
        q, slot = half - 1 - o % half, o % 2

        @pl.when(o < half)
        def _():
            local(out_s.at[slot], other_ref.at[c % 2, q], out_sem.at[slot]).wait()
            swap_copy(c, q).start()

        @pl.when(o >= half)
        def _():
            local(out_s.at[slot], both_ref.at[c % 2, q], out_sem.at[slot]).wait()

        for k in others:

            @pl.when((o >= half) & (q == 2 * k + 1))
            def _():
                up_copy(c, k).start()
                down_copy(c, k).start()

            @pl.when((o >= half) & (q == 2 * k))
            def _():
                home_far(c, k, 0).start()

        @pl.when((o >= half) & (q == 1))
        def _():
            home_near(c, 1).start()

    @pl.when(s >= first)
    def _():
        o = s - first
        slot = o % 2
        q = half - 1 - o % half
        side = 1 - o // half
        place = 2 * q + side
        at = pl.multiple_of(place * slots, slots)

        @pl.when(o >= 1)
        def _():
            written(j, o - 1)

        @pl.when((o >= half - 1) & (o < 2 * half - 1))
        def _():
            coming = half - 1 - (o + 1) % half
            swap_copy(j, coming).wait_recv()
            local(core_in.at[j % 2, coming], in_s.at[1 - slot], x_sem.at[1 - slot]).start()

        @pl.when(o >= half)
        def _():
            local(core_in.at[j % 2, q], in_s.at[slot], x_sem.at[slot]).wait()

        @pl.when(o < half)
        def _():
            in_s[slot] = jnp.zeros((rows, span), jnp.bfloat16)

        picks = (dot_nt(meta_s[place], pick_ref[...]) == 0.0).astype(jnp.bfloat16)
        flat = (experts * slots, width)
        g = dot_nn(picks, rows_s[:, pl.ds(at, slots), :].reshape(flat))
        out_s[slot, :, :width] = low(g + wide(in_s[slot, :, :width]))
        flat = (experts * slots, extra)
        p = dot_nn(picks, mrow_s[:, pl.ds(at, slots), :].reshape(flat))
        out_s[slot, :, width:full] = low(p + wide(in_s[slot, :, width:full]))
        flat = (experts * slots, width)
        y = dot_nn(picks, crow_s[:, pl.ds(at, slots), :].reshape(flat))
        out_s[slot, :, full:] = low(y + wide(in_s[slot, :, full:]))

        @pl.when(o < half)
        def _():
            local(out_s.at[slot], other_ref.at[j % 2, q], out_sem.at[slot]).start()

        @pl.when(o >= half)
        def _():
            local(out_s.at[slot], both_ref.at[j % 2, q], out_sem.at[slot]).start()

        @pl.when(s == steps - 1)
        def _():
            written(j, o)
            store(experts - 1, (experts - 1) % 2).wait()

        @pl.when((s == steps - 1) & (j + 1 < chunks))
        def _():
            fetch(j + 1, 0)

    @pl.when((s == steps - 1) & (j == chunks - 1))
    def _():
        fold_halves(chunks - 1)
        fold_home(chunks - 1)
        drain_sum(chunks - 1)
        for k in range(chunks - 1):
            last_copy(k).wait_recv()
            together(local(ring_in.at[k], in_s.at[1], fold_sem.at[1]))

            @pl.loop(0, rows // 16)
            def _(i):
                at = pl.ds(pl.multiple_of(i * 16, 16), 16)
                in_s[0, at, :] = low(wide(in_s[0, at, :]) + wide(in_s[1, at, :]))

        together(local(in_s.at[0], final_ref, fold_sem.at[0]))
        for k in range(chunks - 1):
            last_copy(k).wait_send()
            ring_copy(k).wait_send()


def moe(own, cot, picks, wg, wu, wd, outer, chunks, slots, all_experts):
    rows, full = own.shape
    width = cot[0].shape[1]
    extra = full - width
    span = full + width
    experts, _, hidden = wg.shape
    blocks, half, cut = 4 * outer, 2 * outer, rows // 2
    total = blocks * slots
    sizes = (outer, chunks, experts, slots, rows, width, extra, all_experts)

    def expert_at(j, s):
        return (jnp.clip(s - blocks, 0, experts - 1), 0, 0)

    anywhere = pl.BlockSpec(memory_space=pl.ANY)
    in_specs = [
        *[anywhere] * (1 + len(cot)),
        pl.BlockSpec(picks.shape, lambda j, s: (0, 0)),
        pl.BlockSpec((1, width, hidden), expert_at),
        pl.BlockSpec((1, width, hidden), expert_at),
        pl.BlockSpec((1, hidden, width), expert_at),
    ]
    bf16 = jnp.bfloat16
    shapes = [
        ((rows, span), bf16),
        ((experts, 3, hidden, width), jnp.float32),
        ((chunks, rows, full), bf16),
        ((chunks if chunks <= 4 else 3, blocks - 1, rows, full), bf16),
        ((2, half, rows, span), bf16),
        ((2, half, rows, span), bf16),
        ((2, half, rows, span), bf16),
        ((2, outer - 1, cut, span), bf16),
        ((2, outer - 1, cut, span), bf16),
        ((2, rows, span), bf16),
        ((2, outer - 1, rows, span), bf16),
        ((chunks - 1, rows, span), bf16),
        ((chunks - 1, rows, span), bf16),
    ]
    dma = pltpu.SemaphoreType.DMA
    gathers, sums = 5 * outer - 2, 6 * outer - 2
    scratch = [
        pltpu.VMEM((2, rows, span), bf16),
        pltpu.VMEM((2, rows, span), bf16),
        pltpu.VMEM((experts, total, width), bf16),
        pltpu.VMEM((experts, total, width), bf16),
        pltpu.VMEM((experts, total, extra), bf16),
        pltpu.VMEM((blocks, rows, extra), bf16),
        pltpu.VMEM((total, hidden), bf16),
        pltpu.VMEM((total, hidden), bf16),
        pltpu.VMEM((total, hidden), bf16),
        pltpu.VMEM((hidden, total), bf16),
        pltpu.VMEM((2, 3, hidden, width), jnp.float32),
        dma((2,)),
        dma((2,)),
        dma((2,)),
        dma((2,)),
        dma((2,)),
        dma((4,)),
        dma((chunks, gathers)),
        dma((chunks, gathers)),
        dma((chunks, sums)),
        dma((chunks, sums)),
        dma((chunks,)),
        dma((chunks,)),
        dma((chunks,)),
        dma((chunks,)),
    ]
    flops = 2 * chunks * experts * total * width * (hidden * 9 + 4 * rows)
    results = pl.pallas_call(
        functools.partial(moe_kernel, sizes),
        grid=(chunks, 2 * blocks + experts),
        in_specs=in_specs,
        out_specs=[anywhere] * len(shapes),
        out_shape=[jax.ShapeDtypeStruct(*shape) for shape in shapes],
        scratch_shapes=scratch,
        compiler_params=pltpu.CompilerParams(
            dimension_semantics=("arbitrary", "arbitrary"),
            vmem_limit_bytes=66_500_000,
            collective_id=0,
            has_side_effects=True,
        ),
        cost_estimate=pl.CostEstimate(
            flops=flops, bytes_accessed=blocks * chunks * rows * full * 8, transcendentals=0
        ),
        name="moe",
    )(own, *cot, picks, wg, wu, wd)
    return results[:2]


def wide(values):
    return values.astype(jnp.float32)


def low(values):
    return values.astype(jnp.bfloat16)


def tie(*values):
    return lax.optimization_barrier(values)


def ring_sum(values, count):
    total = values
    for step in range(1, count):
        pairs = [(i, (i + step) % count) for i in range(count)]
        total = total + lax.ppermute(values, "tensor", pairs)
    return total


def pick(values, at, axis):
    return lax.dynamic_index_in_dim(values, at, axis, keepdims=False)


class Plane:
    def __init__(self, count):
        self.outer = count // 4
        everyone = range(count)
        self.core = [(i, i ^ 1) for i in everyone]
        self.inner = [(i, i ^ 2) for i in everyone]
        self.count = count

    def pull(self, values, k):
        pairs = [((i + 4 * k) % self.count, i) for i in range(self.count)]
        return lax.ppermute(values, "dp", pairs)

    def swap_inner(self, values):
        return lax.ppermute(values, "dp", self.inner)

    def swap_core(self, values):
        return lax.ppermute(values, "dp", self.core)

    def push(self, values, k):
        pairs = [(i, (i + 4 * k) % self.count) for i in range(self.count)]
        return lax.ppermute(values, "dp", pairs)

    def fold_inner(self, parts, b, axis, kind):
        given = self.swap_inner(pick(parts, 1 - b, axis).astype(kind))
        return wide(pick(parts, b, axis)) + wide(given)

    def fold_outer(self, parts, a, kind):
        total = wide(pick(parts, a, 0))
        for k in range(1, self.outer):
            given = pick(parts, (a + k) % self.outer, 0).astype(kind)
            total = total + wide(self.push(given, k))
        return total

    def scatter(self, values, inner_first):
        kind = values.dtype
        index = lax.axis_index("dp")
        core, b, a = index % 2, index // 2 % 2, index // 4
        parts = values.reshape(self.outer, 2, 2, values.shape[0] // self.count, values.shape[1])
        given = self.swap_core(pick(parts, 1 - core, 2))
        parts = (wide(pick(parts, core, 2)) + wide(given)).astype(kind)
        if inner_first:
            return self.fold_outer(self.fold_inner(parts, b, 1, kind).astype(kind), a, kind)
        return self.fold_inner(self.fold_outer(parts, a, kind).astype(kind), b, 0, kind)

    def first(self, own):
        return self.swap_inner(own), [self.pull(own, k) for k in range(1, self.outer)]

    def second(self, near, fars):
        half = near.shape[0] // 2
        return [
            jnp.concatenate([self.pull(near[:half], k + 1), self.swap_inner(far[half:])], axis=0)
            for k, far in enumerate(fars)
        ]

    def third(self, own, near, fars, diagonals, swapped):
        mine = [own, near]
        for far, diagonal in zip(fars, diagonals):
            mine += [far, diagonal]
        other = swapped[:2]
        for far, diagonal in zip(swapped[2:], diagonals):
            other += [far, self.swap_core(diagonal)]
        return mine + other


def per_device(
    tokens,
    lengths,
    routes,
    attn_gain,
    w_query,
    w_key,
    w_value,
    w_out,
    q_gain,
    k_gain,
    ffn_gain,
    router_weight,
    w_gate,
    w_up,
    w_down,
    cotangent,
):
    tensor_count = lax.axis_size("tensor")
    data_count = lax.axis_size("dp")
    tensor_rank = lax.axis_index("tensor")
    block_rows = tokens.shape[1]
    width = tokens.shape[2]
    full_length = block_rows * tensor_count
    route_count = routes.shape[2]
    local_experts = w_gate.shape[0]
    all_experts = local_experts * data_count
    head_dim = q_gain.shape[0]
    local_width = w_query.shape[1]
    capacity = max(2, (block_rows * route_count * 5 + 4 * all_experts - 1) // (4 * all_experts))
    query_rows = min(512, full_length)
    scale = head_dim ** (-0.5)
    own_start = tensor_rank * block_rows
    token_values = tokens[0].astype(jnp.float32)
    seq_length = lengths[0]
    own_valid = (own_start + jnp.arange(block_rows) < seq_length).astype(jnp.float32)
    key_valid = jnp.arange(full_length) < seq_length
    normed = rms_scale(token_values, attn_gain).astype(jnp.bfloat16)
    gathered = lax.all_gather(normed, "tensor", axis=0, tiled=True)
    plane = Plane(data_count)
    near, fars = plane.first(cotangent[0])
    core = lax.axis_index("dp") % 2
    depth = width // 2
    out_half = lax.dynamic_slice_in_dim(w_out, core * depth, depth, 0)
    gathered, near, fars, out_half = tie(gathered, near, fars, out_half)
    out_mine = lax.all_gather(out_half, "tensor", axis=0)
    query_unrotated = jnp.dot(gathered, w_query, preferred_element_type=jnp.float32)
    key_raw = jnp.dot(gathered, w_key, preferred_element_type=jnp.float32)
    value_raw = jnp.dot(gathered, w_value, preferred_element_type=jnp.float32)
    query_low = prepare(query_unrotated, q_gain).astype(jnp.bfloat16)
    key_low = prepare(key_raw, k_gain).astype(jnp.bfloat16)
    value_low = value_raw.astype(jnp.bfloat16).reshape(full_length, -1, head_dim)

    def block_scores(query_block):
        scores = (
            jnp.einsum("qhd,khd->hqk", query_block, key_low, preferred_element_type=jnp.float32)
            * scale
        )
        return jnp.where(key_valid[None, None, :], scores, NEG)

    mixed_parts = []
    log_totals = []
    for start in range(0, full_length, query_rows):
        scores = block_scores(query_low[start : start + query_rows])
        row_peak = jnp.max(scores, axis=-1, keepdims=True)
        powers = jnp.exp(scores - row_peak)
        total = jnp.sum(powers, axis=-1, keepdims=True)
        weights = (powers / total).astype(jnp.bfloat16)
        mixed_parts.append(
            jnp.einsum("hqk,khd->qhd", weights, value_low, preferred_element_type=jnp.float32)
        )
        log_totals.append(row_peak + jnp.log(total))
    attended = (
        jnp.concatenate(mixed_parts, axis=0).reshape(full_length, local_width).astype(jnp.bfloat16)
    )
    diagonals = plane.second(near, fars)
    swapped = [plane.swap_core(part) for part in (cotangent[0], near, *fars)]
    attended, diagonals, swapped = tie(attended, diagonals, swapped)
    cot_all = plane.third(cotangent[0], near, fars, diagonals, swapped)
    heads_own = lax.all_to_all(
        attended.reshape(tensor_count, block_rows, local_width), "tensor", 0, 0
    )
    heads_own, out_mine = tie(heads_own, out_mine)
    out_other = plane.swap_core(out_mine)
    heads_own = heads_own.reshape(tensor_count, block_rows, local_width)

    def from_heads(out_weight):
        return sum(dot_nt(heads_own[t], out_weight[t]) for t in range(tensor_count))

    attn_mine, attn_other = from_heads(out_mine), from_heads(out_other)
    attn_own = jnp.where(
        core == 0,
        jnp.concatenate([attn_mine, attn_other], axis=1),
        jnp.concatenate([attn_other, attn_mine], axis=1),
    )
    residual = token_values + own_valid[:, None] * attn_own
    moe_own = rms_scale(residual, ffn_gain).astype(jnp.bfloat16)
    router_logits = jnp.dot(moe_own, router_weight, preferred_element_type=jnp.float32)
    own_probs = jax.nn.softmax(router_logits, axis=-1)
    own_routes = lax.dynamic_slice_in_dim(routes[0], own_start, block_rows, 0)
    onehot = own_routes[:, :, None] == jnp.arange(all_experts)[None, None, :]
    named = jnp.any(onehot, axis=1) & (own_valid[:, None] > 0.0)
    named_low = named.astype(jnp.bfloat16)
    before = jnp.arange(block_rows)[:, None] > jnp.arange(block_rows)[None, :]
    order = jnp.dot(before.astype(jnp.bfloat16), named_low, preferred_element_type=jnp.float32)
    place = jnp.where(named, order, -1.0).astype(jnp.bfloat16)
    weight = jnp.where(named, own_probs, 0.0)
    weight_high = weight.astype(jnp.bfloat16)
    weight_low = (weight - weight_high.astype(jnp.float32)).astype(jnp.bfloat16)
    used = 3 * all_experts + 1
    extra = (used + 127) // 128 * 128
    meta = jnp.concatenate(
        [
            weight_high,
            weight_low,
            place,
            jnp.ones((block_rows, 1), jnp.bfloat16),
            jnp.zeros((block_rows, extra - used), jnp.bfloat16),
        ],
        axis=1,
    )
    slots = (capacity + 15) // 16 * 16
    first_expert = lax.axis_index("dp") * local_experts
    slot_row = jnp.arange(local_experts * slots)[:, None]
    slot_column = jnp.arange(extra)[None, :]
    picks = jnp.where(
        slot_column == 2 * all_experts + first_expert + slot_row // slots,
        1.0,
        jnp.where(slot_column == 3 * all_experts, -(slot_row % slots).astype(jnp.float32), 0.0),
    ).astype(jnp.bfloat16)
    packed = jnp.concatenate([moe_own, meta], axis=1)
    combined, sums = moe(
        packed,
        cot_all,
        picks,
        w_gate,
        w_up,
        w_down,
        data_count // 4,
        tensor_count,
        slots,
        all_experts,
    )
    combined = wide(combined)
    grad_moe = combined[:, :width]
    grad_probs = combined[:, width : width + all_experts]
    output = low(residual + combined[:, width + extra :])
    grad_own = lax.dynamic_slice_in_dim(cotangent[0], own_start, block_rows, 0).astype(jnp.float32)
    grad_logits = (
        own_probs * (grad_probs - jnp.sum(own_probs * grad_probs, axis=-1, keepdims=True))
    ).astype(jnp.bfloat16)
    grad_moe = grad_moe + jnp.einsum(
        "re,de->rd", grad_logits, router_weight, preferred_element_type=jnp.float32
    )
    router_part = jnp.einsum("rd,re->de", moe_own, grad_logits, preferred_element_type=jnp.float32)
    ffn_pull = jax.vjp(rms_scale, residual, ffn_gain)[1]
    grad_res_norm, ffn_part = ffn_pull(grad_moe)
    grad_residual = grad_own + grad_res_norm
    grad_attn = (grad_residual * own_valid[:, None]).astype(jnp.bfloat16)
    attn_lower = lax.dynamic_slice_in_dim(grad_attn, core * depth, depth, 1)
    attn_upper = lax.dynamic_slice_in_dim(grad_attn, depth - core * depth, depth, 1)
    grad_heads = jnp.stack(
        [
            low(dot_nn(attn_lower, out_mine[t]) + dot_nn(attn_upper, out_other[t]))
            for t in range(tensor_count)
        ]
    )
    grad_mixed = lax.all_to_all(grad_heads, "tensor", 0, 0)
    grad_mixed, grad_attn = tie(grad_mixed, grad_attn)
    grad_attn_all = lax.all_gather(grad_attn, "tensor", axis=0, tiled=True)
    grad_mixed = grad_mixed.reshape(full_length, -1, head_dim)
    grad_query_parts = []
    grad_keys = jnp.zeros(key_low.shape, jnp.float32)
    grad_values = jnp.zeros(value_low.shape, jnp.float32)
    for order, start in enumerate(range(0, full_length, query_rows)):
        query_block = query_low[start : start + query_rows]
        grad_block = grad_mixed[start : start + query_rows]
        probs_block = jnp.exp(block_scores(query_block) - log_totals[order])
        probs_low = probs_block.astype(jnp.bfloat16)
        grad_values = grad_values + jnp.einsum(
            "hqk,qhd->khd", probs_low, grad_block, preferred_element_type=jnp.float32
        )
        grad_probs_block = jnp.einsum(
            "qhd,khd->hqk", grad_block, value_low, preferred_element_type=jnp.float32
        )
        delta = jnp.sum(probs_block * grad_probs_block, axis=-1, keepdims=True)
        grad_scores = (probs_block * (grad_probs_block - delta)).astype(jnp.bfloat16)
        grad_query_parts.append(
            jnp.einsum("hqk,khd->qhd", grad_scores, key_low, preferred_element_type=jnp.float32)
            * scale
        )
        grad_keys = (
            grad_keys
            + jnp.einsum(
                "hqk,qhd->khd", grad_scores, query_block, preferred_element_type=jnp.float32
            )
            * scale
        )
    grad_queries = jnp.concatenate(grad_query_parts, axis=0)
    query_pull = jax.vjp(prepare, query_unrotated, q_gain)[1]
    grad_query_raw, q_part = query_pull(grad_queries)
    key_pull = jax.vjp(prepare, key_raw, k_gain)[1]
    grad_key_raw, k_part = key_pull(grad_keys)
    grad_q_low = grad_query_raw.astype(jnp.bfloat16)
    grad_k_low = grad_key_raw.astype(jnp.bfloat16)
    grad_v_low = grad_values.reshape(full_length, local_width).astype(jnp.bfloat16)
    query_part = jnp.einsum("ld,lh->dh", gathered, grad_q_low, preferred_element_type=jnp.float32)
    value_part = jnp.einsum("ld,lh->dh", gathered, grad_v_low, preferred_element_type=jnp.float32)
    from_query = jnp.einsum("lh,dh->ld", grad_q_low, w_query, preferred_element_type=jnp.float32)
    from_key = jnp.einsum("lh,dh->ld", grad_k_low, w_key, preferred_element_type=jnp.float32)
    from_value = jnp.einsum("lh,dh->ld", grad_v_low, w_value, preferred_element_type=jnp.float32)
    grad_gathered, grad_attn_all, sums, router_part = tie(
        low(from_query + from_key + from_value), grad_attn_all, sums, router_part
    )
    grad_normed = wide(
        lax.psum_scatter(grad_gathered, "tensor", scatter_dimension=0, tiled=True)
    )
    grad_gate = jnp.swapaxes(sums[:, 0], 1, 2)
    grad_up = jnp.swapaxes(sums[:, 1], 1, 2)
    grad_down = sums[:, 2]
    grad_k_low, grad_gate, grad_up, grad_down = tie(grad_k_low, grad_gate, grad_up, grad_down)
    key_part = jnp.einsum("ld,lh->dh", gathered, grad_k_low, preferred_element_type=jnp.float32)
    out_part = jnp.einsum("ld,lh->dh", grad_attn_all, attended, preferred_element_type=jnp.float32)
    attn_pull = jax.vjp(rms_scale, token_values, attn_gain)[1]
    grad_tok_norm, attn_part = attn_pull(grad_normed)
    grad_tokens = (grad_residual + grad_tok_norm).astype(jnp.bfloat16)
    grad_out = plane.scatter(low(out_part), True)
    grad_value = plane.scatter(low(value_part), False)
    grad_query = plane.scatter(low(query_part), True)
    grad_key = plane.scatter(low(key_part), False)
    routing = plane.scatter(jnp.concatenate([router_part, ffn_part[:, None]], axis=1), False)
    routing = ring_sum(routing, tensor_count)
    parts = [v.reshape(data_count, -1) for v in (attn_part, q_part, k_part)]
    gains = jnp.repeat(jnp.concatenate(parts, axis=1), tensor_count, axis=0)
    gains = jnp.sum(lax.all_to_all(gains, ("dp", "tensor"), 0, 0, tiled=True), axis=0)
    piece = width // data_count
    last = piece + head_dim // data_count
    return (
        output[None],
        grad_tokens[None],
        gains[:piece],
        grad_query,
        grad_key,
        grad_value,
        grad_out,
        gains[piece:last],
        gains[last:],
        routing[:, all_experts],
        routing[:, :all_experts],
        grad_gate,
        grad_up,
        grad_down,
    )


def solution(mesh):
    return jax.shard_map(
        per_device,
        mesh=mesh,
        in_specs=(
            P("dp", "tensor", None),
            P("dp"),
            P("dp", None, None),
            P(),
            P(None, "tensor"),
            P(None, "tensor"),
            P(None, "tensor"),
            P(None, "tensor"),
            P(),
            P(),
            P(),
            P(),
            P("dp", None, "tensor"),
            P("dp", None, "tensor"),
            P("dp", "tensor", None),
            P("dp", None, None),
        ),
        out_specs=(
            P("dp", "tensor", None),
            P("dp", "tensor", None),
            P("dp"),
            P("dp", "tensor"),
            P("dp", "tensor"),
            P("dp", "tensor"),
            P("dp", "tensor"),
            P("dp"),
            P("dp"),
            P("dp"),
            P("dp", None),
            P("dp", None, "tensor"),
            P("dp", None, "tensor"),
            P("dp", "tensor", None),
        ),
        check_vma=False,
    )
```

```python
import functools

import jax
import jax.numpy as jnp
from jax import lax
from jax.experimental import pallas as pl
from jax.experimental.pallas import tpu as pltpu
from jax.sharding import PartitionSpec as P

EPS = 1e-06
THETA = 50000.0
NEG = -1e30


def rms_scale(values, gain):
    return values * lax.rsqrt(jnp.mean(values * values, axis=-1, keepdims=True) + EPS) * gain


def rotate(values):
    length = values.shape[-3]
    half_dim = values.shape[-1] // 2
    positions = jnp.arange(length).astype(jnp.float32)
    rates = THETA ** (-jnp.arange(half_dim).astype(jnp.float32) / half_dim)
    angles = positions[:, None] * rates[None, :]
    cosine = jnp.cos(angles)[:, None, :]
    sine = jnp.sin(angles)[:, None, :]
    first = values[..., :half_dim]
    second = values[..., half_dim:]
    return jnp.concatenate(
        [first * cosine - second * sine, second * cosine + first * sine], axis=-1
    )


def prepare(raw, gain):
    shaped = raw.reshape(raw.shape[0], -1, gain.shape[0])
    return rotate(rms_scale(shaped, gain))


def dot_nt(a, b):
    return lax.dot_general(a, b, (((1,), (1,)), ((), ())), preferred_element_type=jnp.float32)


def dot_nn(a, b):
    return jnp.dot(a, b, preferred_element_type=jnp.float32)


def largest_tile(total, limit, unit):
    best = unit
    for tile in range(unit, limit + 1, unit):
        if total % tile == 0:
            best = tile
    return best


def moe_kernel(
    sizes,
    own_ref,
    *others_refs,
):
    blocks = 4 * sizes[0]
    moe_body(sizes, own_ref, others_refs[:blocks], *others_refs[blocks:])


def moe_body(
    sizes,
    own_ref,
    cot_refs,
    pick_ref,
    wg_ref,
    wu_ref,
    wd_ref,
    final_ref,
    acc_ref,
    late_ref,
    mine_ref,
    gather_ref,
    other_ref,
    both_ref,
    core_in,
    top_in,
    bottom_in,
    near_in,
    far_in,
    ring_out,
    ring_in,
    in_s,
    out_s,
    rows_s,
    crow_s,
    mrow_s,
    meta_s,
    aw_s,
    gg_s,
    gu_s,
    turn_s,
    acc_s,
    load_sem,
    store_sem,
    x_sem,
    c_sem,
    out_sem,
    fold_sem,
    plane_send,
    plane_recv,
    sum_send,
    sum_recv,
    ring_send,
    ring_recv,
    last_send,
    last_recv,
    late_sem,
):
    outer, chunks, experts, slots, rows, width, extra, all_experts = sizes
    blocks, half, cut = 4 * outer, 2 * outer, rows // 2
    full = width + extra
    span = full + width
    total = blocks * slots
    ring = gather_ref.shape[0]
    j = pl.program_id(0)
    s = pl.program_id(1)
    steps = 2 * blocks + experts
    me = lax.axis_index("dp")
    z = lax.axis_index("tensor")
    a, rest = me // 4, me % 4
    inner_id = me + 2 - 4 * ((me // 2) % 2)
    core_id = me + 1 - 2 * (me % 2)
    upper, lower = pl.ds(0, cut), pl.ds(cut, cut)
    x_part, y_part = pl.ds(0, full), pl.ds(full, width)

    def outer_id(k):
        return ((a + k + outer) % outer) * 4 + rest

    def remote(src, dst, send, recv, where, axis="dp"):
        return pltpu.make_async_remote_copy(
            src_ref=src,
            dst_ref=dst,
            send_sem=send,
            recv_sem=recv,
            device_id={axis: where},
            device_id_type=pl.DeviceIdType.MESH,
        )

    def plane_copy(c, src, dst, rows_at, ident, where):
        first = isinstance(src, int) and src == 0
        near = src if isinstance(src, int) else dst
        source = mine_ref.at[c] if first else gather_ref.at[c % ring, near - 1]
        target = gather_ref.at[c % ring, dst - 1]
        if rows_at is not None:
            source, target = source.at[rows_at], target.at[rows_at]
        return remote(source, target, plane_send.at[c, ident], plane_recv.at[c, ident], where)

    def near_copy(c):
        return plane_copy(c, 0, 1, None, 0, inner_id)

    def far_copy(c, k):
        return plane_copy(c, 0, 2 * k, None, k, outer_id(-k))

    def top_copy(c, k):
        return plane_copy(c, 1, 2 * k + 1, upper, outer - 1 + k, outer_id(-k))

    def bottom_copy(c, k):
        return plane_copy(c, 2 * k, 2 * k + 1, lower, 2 * outer - 2 + k, inner_id)

    def core_copy(c, q):
        return plane_copy(c, q, half + q, None, 3 * outer - 2 + q, core_id)

    def column(c):
        return (z + c + 1) % chunks

    def ring_copy(k):
        where = (z - k - 1 + chunks) % chunks
        return remote(own_ref, mine_ref.at[k], ring_send.at[k], ring_recv.at[k], where, "tensor")

    others = range(1, outer)

    def first_hop(c):
        near_copy(c).start()
        for k in others:
            far_copy(c, k).start()
        core_copy(c, 0).start()

    def second_hop(c):
        near_copy(c).wait_recv()
        for k in others:
            top_copy(c, k).start()
        for k in others:
            far_copy(c, k).wait_recv()
            bottom_copy(c, k).start()
        for q in [1] + [2 * k for k in others]:
            core_copy(c, q).start()

    def third_hop(c):
        for k in others:
            top_copy(c, k).wait_recv()
            bottom_copy(c, k).wait_recv()
            core_copy(c, 2 * k + 1).start()

    def drain_gather(c):
        near_copy(c).wait_send()
        for k in others:
            far_copy(c, k).wait_send()
            top_copy(c, k).wait_send()
            bottom_copy(c, k).wait_send()
        for q in range(half):
            core_copy(c, q).wait_send()

    def sum_copy(c, src, dst, ident, where):
        def each(act):
            def columns(size):
                part = pl.ds(0, size)
                source, target = src.at[:, part], dst.at[:, part]
                act(remote(source, target, sum_send.at[c, ident], sum_recv.at[c, ident], where))

            if isinstance(c, int):
                columns(full if c == chunks - 1 else span)
                return

            @pl.when(c < chunks - 1)
            def _():
                columns(span)

            @pl.when(c == chunks - 1)
            def _():
                columns(full)

        class Copy:
            def start(self):
                each(lambda copy: copy.start())

            def wait_recv(self):
                each(lambda copy: copy.wait_recv())

            def wait_send(self):
                each(lambda copy: copy.wait_send())

        return Copy()

    def late_copy(q, side, slot):
        owner = ((a + q // 2) % outer) * 4 + ((me // 2 + q) % 2) * 2 + (me + side) % 2
        return local(out_s.at[slot, :, y_part], late_ref.at[owner], late_sem.at[slot])

    def swap_copy(c, q):
        return sum_copy(c, other_ref.at[c % 2, q], core_in.at[c % 2, q], q, core_id)

    def both_at(c, q, rows_at):
        return both_ref.at[c % 2, q, rows_at]

    def up_copy(c, k):
        ident = half + k - 1
        return sum_copy(c, both_at(c, 2 * k + 1, upper), top_in.at[c % 2, k - 1], ident, outer_id(k))

    def down_copy(c, k):
        ident = half + outer - 1 + k - 1
        source = both_at(c, 2 * k + 1, lower)
        return sum_copy(c, source, bottom_in.at[c % 2, k - 1], ident, inner_id)

    def home_near(c, part):
        rows_at = (upper, lower)[part]
        ident = half + 2 * outer - 2 + part
        return sum_copy(c, both_at(c, 1, rows_at), near_in.at[c % 2, rows_at], ident, inner_id)

    def home_far(c, k, part):
        rows_at = (upper, lower)[part]
        ident = half + 2 * outer + 2 * (k - 1) + part
        target = far_in.at[c % 2, k - 1, rows_at]
        return sum_copy(c, both_at(c, 2 * k, rows_at), target, ident, outer_id(k))

    def last_copy(c):
        source, target = ring_out.at[c], ring_in.at[c]
        return remote(source, target, last_send.at[c], last_recv.at[c], column(c), "tensor")

    def local(src, dst, sem):
        return pltpu.make_async_copy(src, dst, sem)

    def together(*copies):
        for copy in copies:
            copy.start()
        for copy in copies:
            copy.wait()

    def fold_halves(c):
        for k in others:
            up_copy(c, k).wait_recv()
            down_copy(c, k).wait_recv()
            copies = [
                local(both_at(c, 2 * k, lower), in_s.at[0, lower], fold_sem.at[0]),
                local(top_in.at[c % 2, k - 1], in_s.at[1, upper], fold_sem.at[1]),
                local(bottom_in.at[c % 2, k - 1], in_s.at[1, lower], fold_sem.at[2]),
            ]
            if k == 1:
                copies.append(local(both_at(c, 1, upper), in_s.at[0, upper], fold_sem.at[3]))
            together(*copies)

            @pl.loop(0, rows // 16)
            def _(i):
                at = pl.ds(pl.multiple_of(i * 16, 16), 16)
                in_s[0, at, :] = low(wide(in_s[0, at, :]) + wide(in_s[1, at, :]))

            together(local(in_s.at[0, lower], both_at(c, 2 * k, lower), fold_sem.at[0]))
        together(local(in_s.at[0, upper], both_at(c, 1, upper), fold_sem.at[0]))
        for k in others:
            home_far(c, k, 1).start()
        home_near(c, 0).start()

    def fold_home(c):
        for part in (0, 1):
            home_near(c, part).wait_recv()
        together(
            local(both_ref.at[c % 2, 0], in_s.at[0], fold_sem.at[0]),
            local(near_in.at[c % 2], in_s.at[1], fold_sem.at[1]),
        )

        @pl.loop(0, rows // 16)
        def _(i):
            at = pl.ds(pl.multiple_of(i * 16, 16), 16)
            in_s[0, at, :] = low(wide(in_s[0, at, :]) + wide(in_s[1, at, :]))

        for k in others:
            for part in (0, 1):
                home_far(c, k, part).wait_recv()
            together(local(far_in.at[c % 2, k - 1], in_s.at[1], fold_sem.at[1]))

            @pl.loop(0, rows // 16)
            def _(i):
                at = pl.ds(pl.multiple_of(i * 16, 16), 16)
                in_s[0, at, :] = low(wide(in_s[0, at, :]) + wide(in_s[1, at, :]))


    def drain_sum(c):
        for q in range(half):
            swap_copy(c, q).wait_send()
        for k in others:
            up_copy(c, k).wait_send()
            down_copy(c, k).wait_send()
            for part in (0, 1):
                home_far(c, k, part).wait_send()
        for part in (0, 1):
            home_near(c, part).wait_send()

    def fetch(c, at):
        q, side, slot = at // 2, at % 2, at % 2
        r = side * half + q

        @pl.when(side == 1)
        def _():
            core_copy(c, q).wait_recv()

        rows_at = pl.ds(pl.multiple_of(column(c) * rows, rows), rows)
        @pl.when(r == 0)
        def _():
            local(mine_ref.at[c], in_s.at[slot, :, x_part], x_sem.at[slot]).start()

        @pl.when(r > 0)
        def _():
            source = gather_ref.at[c % ring, jnp.maximum(r - 1, 0)]
            local(source, in_s.at[slot, :, x_part], x_sem.at[slot]).start()

        for place, cot_ref in enumerate(cot_refs):

            @pl.when(r == place)
            def _():
                local(cot_ref.at[rows_at], in_s.at[slot, :, y_part], c_sem.at[slot]).start()


    def fetched(slot):
        local(mine_ref.at[0], in_s.at[slot, :, x_part], x_sem.at[slot]).wait()
        local(cot_refs[0].at[pl.ds(0, rows)], in_s.at[slot, :, y_part], c_sem.at[slot]).wait()

    def load(e, slot):
        return local(acc_ref.at[e], acc_s.at[slot], load_sem.at[slot])

    def store(e, slot):
        return local(acc_s.at[slot], acc_ref.at[e], store_sem.at[slot])

    @pl.when((j == 0) & (s == 0))
    def _():
        barrier = pltpu.get_barrier_semaphore()
        peers = [("dp", core_id), ("dp", inner_id)] + [("dp", outer_id(k)) for k in others]
        peers += [("tensor", (z + k) % chunks) for k in range(1, chunks)]
        for axis, where in peers:
            pl.semaphore_signal(
                barrier, inc=1, device_id={axis: where}, device_id_type=pl.DeviceIdType.MESH
            )
        pl.semaphore_wait(barrier, len(peers))
        ring_copy(0).start()
        together(local(own_ref, in_s.at[0, :, x_part], fold_sem.at[0]))
        together(local(in_s.at[0, :, x_part], mine_ref.at[chunks - 1], fold_sem.at[0]))
        ring_copy(0).wait_recv()
        for k in range(1, chunks - 1):
            ring_copy(k).start()
        first_hop(0)
        fetch(0, 0)
        second_hop(0)

    @pl.when((s == 0) & (j > 0))
    def _():
        load(0, 0).start()

    @pl.when((j == 0) & (s == 4))
    def _():
        third_hop(0)
        if chunks > 2:
            ring_copy(1).wait_recv()
        first_hop(1)

    @pl.when((s == blocks + experts) & (j + 1 < chunks))
    def _():
        third_hop(j + 1)

    @pl.when((s == blocks + 2) & (j >= 1))
    def _():
        fold_halves(j - 1)

    @pl.when((s == blocks + 2) & (j + 1 < chunks))
    def _():
        second_hop(j + 1)

    @pl.when((s == blocks + 2) & (j + 3 < chunks))
    def _():
        ring_copy(j + 2).wait_recv()

    @pl.when((s == blocks + 2) & (j + 2 < chunks))
    def _():
        first_hop(j + 2)

    @pl.when(s == blocks + 3)
    def _():
        drain_gather(j)

    @pl.when((s == blocks + experts + half - 1) & (j >= 1))
    def _():
        fold_home(j - 1)
        together(local(in_s.at[0], ring_out.at[j - 1], fold_sem.at[0]))
        last_copy(j - 1).start()
        drain_sum(j - 1)

    @pl.when(s < blocks)
    def _():
        slot = s % 2

        @pl.when(s + 1 < blocks)
        def _():
            fetch(j, s + 1)

        fetched(slot)
        meta = in_s[slot, :, width:full]
        picks = (dot_nt(pick_ref[...], meta) == 0.0).astype(jnp.bfloat16)
        at = pl.multiple_of(s * slots, slots)
        got = low(dot_nn(picks, in_s[slot, :, :full]))
        cot = low(dot_nn(picks, in_s[slot, :, full:]))
        for e in range(experts):
            part = slice(e * slots, (e + 1) * slots)
            rows_s[e, pl.ds(at, slots), :] = got[part, :width]
            mrow_s[e, pl.ds(at, slots), :] = got[part, width:]
            crow_s[e, pl.ds(at, slots), :] = cot[part]
        meta_s[s] = meta

    @pl.when((s >= blocks) & (s < blocks + experts))
    def _():
        e = s - blocks
        slot = e % 2
        tile = largest_tile(total, 320, 16)
        expert = me * experts + e
        wg = wg_ref[0]
        wu = wu_ref[0]
        wd = wd_ref[0]

        @pl.loop(0, total // tile)
        def _(m):
            ds = pl.ds(pl.multiple_of(m * tile, tile), tile)
            picked_rows = rows_s[e, ds, :]
            gate = dot_nn(picked_rows, wg)
            up = dot_nn(picked_rows, wu)
            grad_act = dot_nt(crow_s[e, ds, :], wd)
            meta = wide(mrow_s[e, ds, :])
            column = lax.broadcasted_iota(jnp.int32, meta.shape, 1)
            wanted = (column == expert) | (column == expert + all_experts)
            weight = jnp.sum(jnp.where(wanted, meta, 0.0), axis=1, keepdims=True)
            sig = jax.nn.sigmoid(gate)
            silu = gate * sig
            act = silu * up
            g_pick = jnp.sum(act * grad_act, axis=1, keepdims=True)
            scaled = weight * grad_act
            aw_s[ds, :] = low(weight * act)
            gg_s[ds, :] = low(scaled * up * sig * (1.0 + gate * (1.0 - sig)))
            gu_s[ds, :] = low(scaled * silu)
            mrow_s[e, ds, :] = low(jnp.where(column == expert, g_pick, 0.0))

        @pl.when(e >= 1)
        def _():
            store(e - 1, 1 - slot).wait()

        @pl.when(j == 0)
        def _():
            acc_s[slot] = jnp.zeros(acc_s.shape[1:], jnp.float32)

        @pl.when(j > 0)
        def _():
            load(e, slot).wait()

            @pl.when(e + 1 < experts)
            def _():
                load(e + 1, 1 - slot).start()

        cols = largest_tile(width, 512, 128)
        for which, (left, right) in enumerate(((gg_s, rows_s), (gu_s, rows_s), (aw_s, crow_s))):
            turn_s[...] = left[...].T

            @pl.loop(0, width // cols)
            def _(n):
                ds = pl.ds(pl.multiple_of(n * cols, cols), cols)
                add = dot_nn(turn_s[...], right[e, :, ds])
                acc_s[slot, which, :, ds] = acc_s[slot, which, :, ds] + add

        store(e, slot).start()

        @pl.loop(0, total // tile)
        def _(m):
            ds = pl.ds(pl.multiple_of(m * tile, tile), tile)
            crow_s[e, ds, :] = low(dot_nn(aw_s[ds, :], wd))
            rows_s[e, ds, :] = low(dot_nt(gg_s[ds, :], wg) + dot_nt(gu_s[ds, :], wu))

    first = blocks + experts

    def written(c, o):
        q, slot = half - 1 - o % half, o % 2

        @pl.when(c == chunks - 1)
        def _():
            late_copy(q, 1 - o // half, slot).wait()

        @pl.when(o < half)
        def _():
            local(out_s.at[slot], other_ref.at[c % 2, q], out_sem.at[slot]).wait()
            swap_copy(c, q).start()

        @pl.when(o >= half)
        def _():
            local(out_s.at[slot], both_ref.at[c % 2, q], out_sem.at[slot]).wait()

        for k in others:

            @pl.when((o >= half) & (q == 2 * k + 1))
            def _():
                up_copy(c, k).start()
                down_copy(c, k).start()

            @pl.when((o >= half) & (q == 2 * k))
            def _():
                home_far(c, k, 0).start()

        @pl.when((o >= half) & (q == 1))
        def _():
            home_near(c, 1).start()

    @pl.when(s >= first)
    def _():
        o = s - first
        slot = o % 2
        q = half - 1 - o % half
        side = 1 - o // half
        place = 2 * q + side
        at = pl.multiple_of(place * slots, slots)

        @pl.when(o >= 1)
        def _():
            written(j, o - 1)

        @pl.when((o >= half - 1) & (o < 2 * half - 1))
        def _():
            coming = half - 1 - (o + 1) % half
            swap_copy(j, coming).wait_recv()
            local(core_in.at[j % 2, coming], in_s.at[1 - slot], x_sem.at[1 - slot]).start()

        @pl.when(o >= half)
        def _():
            local(core_in.at[j % 2, q], in_s.at[slot], x_sem.at[slot]).wait()

        @pl.when((o >= half) & (j == chunks - 1))
        def _():
            in_s[slot, :, full:] = jnp.zeros((rows, width), jnp.bfloat16)

        @pl.when(o < half)
        def _():
            in_s[slot] = jnp.zeros((rows, span), jnp.bfloat16)

        picks = (dot_nt(meta_s[place], pick_ref[...]) == 0.0).astype(jnp.bfloat16)
        flat = (experts * slots, width)
        g = dot_nn(picks, rows_s[:, pl.ds(at, slots), :].reshape(flat))
        out_s[slot, :, :width] = low(g + wide(in_s[slot, :, :width]))
        flat = (experts * slots, extra)
        p = dot_nn(picks, mrow_s[:, pl.ds(at, slots), :].reshape(flat))
        out_s[slot, :, width:full] = low(p + wide(in_s[slot, :, width:full]))
        flat = (experts * slots, width)
        y = dot_nn(picks, crow_s[:, pl.ds(at, slots), :].reshape(flat))
        out_s[slot, :, full:] = low(y + wide(in_s[slot, :, full:]))

        @pl.when(j == chunks - 1)
        def _():
            late_copy(q, side, slot).start()

        @pl.when(o < half)
        def _():
            local(out_s.at[slot], other_ref.at[j % 2, q], out_sem.at[slot]).start()

        @pl.when(o >= half)
        def _():
            local(out_s.at[slot], both_ref.at[j % 2, q], out_sem.at[slot]).start()

        @pl.when(s == steps - 1)
        def _():
            written(j, o)
            store(experts - 1, (experts - 1) % 2).wait()

        @pl.when((s == steps - 1) & (j + 1 < chunks))
        def _():
            fetch(j + 1, 0)

    @pl.when((s == steps - 1) & (j == chunks - 1))
    def _():
        fold_halves(chunks - 1)
        fold_home(chunks - 1)
        drain_sum(chunks - 1)
        in_s[0, :, full:] = jnp.zeros((rows, width), jnp.bfloat16)
        for k in range(chunks - 1):
            last_copy(k).wait_recv()
            together(local(ring_in.at[k], in_s.at[1], fold_sem.at[1]))

            @pl.loop(0, rows // 16)
            def _(i):
                at = pl.ds(pl.multiple_of(i * 16, 16), 16)
                in_s[0, at, :] = low(wide(in_s[0, at, :]) + wide(in_s[1, at, :]))

        together(local(in_s.at[0], final_ref, fold_sem.at[0]))
        for k in range(chunks - 1):
            last_copy(k).wait_send()
            ring_copy(k).wait_send()


def moe(own, cot, picks, wg, wu, wd, outer, chunks, slots, all_experts):
    rows, full = own.shape
    width = cot[0].shape[1]
    extra = full - width
    span = full + width
    experts, _, hidden = wg.shape
    blocks, half, cut = 4 * outer, 2 * outer, rows // 2
    total = blocks * slots
    sizes = (outer, chunks, experts, slots, rows, width, extra, all_experts)

    def expert_at(j, s):
        return (jnp.clip(s - blocks, 0, experts - 1), 0, 0)

    anywhere = pl.BlockSpec(memory_space=pl.ANY)
    in_specs = [
        *[anywhere] * (1 + len(cot)),
        pl.BlockSpec(picks.shape, lambda j, s: (0, 0)),
        pl.BlockSpec((1, width, hidden), expert_at),
        pl.BlockSpec((1, width, hidden), expert_at),
        pl.BlockSpec((1, hidden, width), expert_at),
    ]
    bf16 = jnp.bfloat16
    shapes = [
        ((rows, span), bf16),
        ((experts, 3, hidden, width), jnp.float32),
        ((blocks, rows, width), bf16),
        ((chunks, rows, full), bf16),
        ((chunks if chunks <= 4 else 3, blocks - 1, rows, full), bf16),
        ((2, half, rows, span), bf16),
        ((2, half, rows, span), bf16),
        ((2, half, rows, span), bf16),
        ((2, outer - 1, cut, span), bf16),
        ((2, outer - 1, cut, span), bf16),
        ((2, rows, span), bf16),
        ((2, outer - 1, rows, span), bf16),
        ((chunks - 1, rows, span), bf16),
        ((chunks - 1, rows, span), bf16),
    ]
    dma = pltpu.SemaphoreType.DMA
    gathers, sums = 5 * outer - 2, 6 * outer - 2
    scratch = [
        pltpu.VMEM((2, rows, span), bf16),
        pltpu.VMEM((2, rows, span), bf16),
        pltpu.VMEM((experts, total, width), bf16),
        pltpu.VMEM((experts, total, width), bf16),
        pltpu.VMEM((experts, total, extra), bf16),
        pltpu.VMEM((blocks, rows, extra), bf16),
        pltpu.VMEM((total, hidden), bf16),
        pltpu.VMEM((total, hidden), bf16),
        pltpu.VMEM((total, hidden), bf16),
        pltpu.VMEM((hidden, total), bf16),
        pltpu.VMEM((2, 3, hidden, width), jnp.float32),
        dma((2,)),
        dma((2,)),
        dma((2,)),
        dma((2,)),
        dma((2,)),
        dma((4,)),
        dma((chunks, gathers)),
        dma((chunks, gathers)),
        dma((chunks, sums)),
        dma((chunks, sums)),
        dma((chunks,)),
        dma((chunks,)),
        dma((chunks,)),
        dma((chunks,)),
        dma((2,)),
    ]
    flops = 2 * chunks * experts * total * width * (hidden * 9 + 4 * rows)
    results = pl.pallas_call(
        functools.partial(moe_kernel, sizes),
        grid=(chunks, 2 * blocks + experts),
        in_specs=in_specs,
        out_specs=[anywhere] * len(shapes),
        out_shape=[jax.ShapeDtypeStruct(*shape) for shape in shapes],
        scratch_shapes=scratch,
        compiler_params=pltpu.CompilerParams(
            dimension_semantics=("arbitrary", "arbitrary"),
            vmem_limit_bytes=66_500_000,
            collective_id=0,
            has_side_effects=True,
        ),
        cost_estimate=pl.CostEstimate(
            flops=flops, bytes_accessed=blocks * chunks * rows * full * 8, transcendentals=0
        ),
        name="moe",
    )(own, *cot, picks, wg, wu, wd)
    return results[:3]


def wide(values):
    return values.astype(jnp.float32)


def low(values):
    return values.astype(jnp.bfloat16)


def tie(*values):
    return lax.optimization_barrier(values)


def ring_sum(values, count):
    total = values
    for step in range(1, count):
        pairs = [(i, (i + step) % count) for i in range(count)]
        total = total + lax.ppermute(values, "tensor", pairs)
    return total


def pick(values, at, axis):
    return lax.dynamic_index_in_dim(values, at, axis, keepdims=False)


class Plane:
    def __init__(self, count):
        self.outer = count // 4
        everyone = range(count)
        self.core = [(i, i ^ 1) for i in everyone]
        self.inner = [(i, i ^ 2) for i in everyone]
        self.count = count

    def pull(self, values, k):
        pairs = [((i + 4 * k) % self.count, i) for i in range(self.count)]
        return lax.ppermute(values, "dp", pairs)

    def swap_inner(self, values):
        return lax.ppermute(values, "dp", self.inner)

    def swap_core(self, values):
        return lax.ppermute(values, "dp", self.core)

    def push(self, values, k):
        pairs = [(i, (i + 4 * k) % self.count) for i in range(self.count)]
        return lax.ppermute(values, "dp", pairs)

    def fold_inner(self, parts, b, axis, kind):
        given = self.swap_inner(pick(parts, 1 - b, axis).astype(kind))
        return wide(pick(parts, b, axis)) + wide(given)

    def fold_outer(self, parts, a, kind):
        total = wide(pick(parts, a, 0))
        for k in range(1, self.outer):
            given = pick(parts, (a + k) % self.outer, 0).astype(kind)
            total = total + wide(self.push(given, k))
        return total

    def scatter(self, values, inner_first):
        kind = values.dtype
        return self.scatter_rest(self.fold_core(values), kind, inner_first)

    def fold_core(self, values):
        core = lax.axis_index("dp") % 2
        parts = values.reshape(self.outer, 2, 2, values.shape[0] // self.count, values.shape[1])
        given = self.swap_core(pick(parts, 1 - core, 2))
        return (wide(pick(parts, core, 2)) + wide(given)).astype(values.dtype)

    def scatter_rest(self, parts, kind, inner_first):
        index = lax.axis_index("dp")
        b, a = index // 2 % 2, index // 4
        if inner_first:
            return self.fold_outer(self.fold_inner(parts, b, 1, kind).astype(kind), a, kind)
        return self.fold_inner(self.fold_outer(parts, a, kind).astype(kind), b, 0, kind)

    def first(self, own):
        return self.swap_inner(own), [self.pull(own, k) for k in range(1, self.outer)]

    def second(self, near, fars):
        half = near.shape[0] // 2
        return [
            jnp.concatenate([self.pull(near[:half], k + 1), self.swap_inner(far[half:])], axis=0)
            for k, far in enumerate(fars)
        ]

    def third(self, own, near, fars, diagonals, swapped):
        mine = [own, near]
        for far, diagonal in zip(fars, diagonals):
            mine += [far, diagonal]
        other = swapped[:2]
        for far, diagonal in zip(swapped[2:], diagonals):
            other += [far, self.swap_core(diagonal)]
        return mine + other


def per_device(
    tokens,
    lengths,
    routes,
    attn_gain,
    w_query,
    w_key,
    w_value,
    w_out,
    q_gain,
    k_gain,
    ffn_gain,
    router_weight,
    w_gate,
    w_up,
    w_down,
    cotangent,
):
    tensor_count = lax.axis_size("tensor")
    data_count = lax.axis_size("dp")
    tensor_rank = lax.axis_index("tensor")
    block_rows = tokens.shape[1]
    width = tokens.shape[2]
    full_length = block_rows * tensor_count
    route_count = routes.shape[2]
    local_experts = w_gate.shape[0]
    all_experts = local_experts * data_count
    head_dim = q_gain.shape[0]
    local_width = w_query.shape[1]
    capacity = max(2, (block_rows * route_count * 5 + 4 * all_experts - 1) // (4 * all_experts))
    query_rows = min(512, full_length)
    scale = head_dim ** (-0.5)
    own_start = tensor_rank * block_rows
    token_values = tokens[0].astype(jnp.float32)
    seq_length = lengths[0]
    own_valid = (own_start + jnp.arange(block_rows) < seq_length).astype(jnp.float32)
    key_valid = jnp.arange(full_length) < seq_length
    normed = rms_scale(token_values, attn_gain).astype(jnp.bfloat16)
    gathered = lax.all_gather(normed, "tensor", axis=0, tiled=True)
    plane = Plane(data_count)
    near, fars = plane.first(cotangent[0])
    core = lax.axis_index("dp") % 2
    depth = width // 2
    out_half = lax.dynamic_slice_in_dim(w_out, core * depth, depth, 0)
    gathered, near, fars, out_half = tie(gathered, near, fars, out_half)
    out_mine = lax.all_gather(out_half, "tensor", axis=0)
    query_unrotated = jnp.dot(gathered, w_query, preferred_element_type=jnp.float32)
    key_raw = jnp.dot(gathered, w_key, preferred_element_type=jnp.float32)
    value_raw = jnp.dot(gathered, w_value, preferred_element_type=jnp.float32)
    query_low = prepare(query_unrotated, q_gain).astype(jnp.bfloat16)
    key_low = prepare(key_raw, k_gain).astype(jnp.bfloat16)
    value_low = value_raw.astype(jnp.bfloat16).reshape(full_length, -1, head_dim)

    def block_scores(query_block):
        scores = (
            jnp.einsum("qhd,khd->hqk", query_block, key_low, preferred_element_type=jnp.float32)
            * scale
        )
        return jnp.where(key_valid[None, None, :], scores, NEG)

    mixed_parts = []
    log_totals = []
    for start in range(0, full_length, query_rows):
        scores = block_scores(query_low[start : start + query_rows])
        row_peak = jnp.max(scores, axis=-1, keepdims=True)
        powers = jnp.exp(scores - row_peak)
        total = jnp.sum(powers, axis=-1, keepdims=True)
        weights = (powers / total).astype(jnp.bfloat16)
        mixed_parts.append(
            jnp.einsum("hqk,khd->qhd", weights, value_low, preferred_element_type=jnp.float32)
        )
        log_totals.append(row_peak + jnp.log(total))
    attended = (
        jnp.concatenate(mixed_parts, axis=0).reshape(full_length, local_width).astype(jnp.bfloat16)
    )
    diagonals = plane.second(near, fars)
    swapped = [plane.swap_core(part) for part in (cotangent[0], near, *fars)]
    attended, diagonals, swapped = tie(attended, diagonals, swapped)
    cot_all = plane.third(cotangent[0], near, fars, diagonals, swapped)
    heads_own = lax.all_to_all(
        attended.reshape(tensor_count, block_rows, local_width), "tensor", 0, 0
    )
    heads_own, out_mine = tie(heads_own, out_mine)
    out_other = plane.swap_core(out_mine)
    heads_own = heads_own.reshape(tensor_count, block_rows, local_width)

    def from_heads(out_weight):
        return sum(dot_nt(heads_own[t], out_weight[t]) for t in range(tensor_count))

    attn_mine, attn_other = from_heads(out_mine), from_heads(out_other)
    attn_own = jnp.where(
        core == 0,
        jnp.concatenate([attn_mine, attn_other], axis=1),
        jnp.concatenate([attn_other, attn_mine], axis=1),
    )
    residual = token_values + own_valid[:, None] * attn_own
    moe_own = rms_scale(residual, ffn_gain).astype(jnp.bfloat16)
    router_logits = jnp.dot(moe_own, router_weight, preferred_element_type=jnp.float32)
    own_probs = jax.nn.softmax(router_logits, axis=-1)
    own_routes = lax.dynamic_slice_in_dim(routes[0], own_start, block_rows, 0)
    onehot = own_routes[:, :, None] == jnp.arange(all_experts)[None, None, :]
    named = jnp.any(onehot, axis=1) & (own_valid[:, None] > 0.0)
    named_low = named.astype(jnp.bfloat16)
    before = jnp.arange(block_rows)[:, None] > jnp.arange(block_rows)[None, :]
    order = jnp.dot(before.astype(jnp.bfloat16), named_low, preferred_element_type=jnp.float32)
    place = jnp.where(named, order, -1.0).astype(jnp.bfloat16)
    weight = jnp.where(named, own_probs, 0.0)
    weight_high = weight.astype(jnp.bfloat16)
    weight_low = (weight - weight_high.astype(jnp.float32)).astype(jnp.bfloat16)
    used = 3 * all_experts + 1
    extra = (used + 127) // 128 * 128
    meta = jnp.concatenate(
        [
            weight_high,
            weight_low,
            place,
            jnp.ones((block_rows, 1), jnp.bfloat16),
            jnp.zeros((block_rows, extra - used), jnp.bfloat16),
        ],
        axis=1,
    )
    slots = (capacity + 15) // 16 * 16
    first_expert = lax.axis_index("dp") * local_experts
    slot_row = jnp.arange(local_experts * slots)[:, None]
    slot_column = jnp.arange(extra)[None, :]
    picks = jnp.where(
        slot_column == 2 * all_experts + first_expert + slot_row // slots,
        1.0,
        jnp.where(slot_column == 3 * all_experts, -(slot_row % slots).astype(jnp.float32), 0.0),
    ).astype(jnp.bfloat16)
    packed = jnp.concatenate([moe_own, meta], axis=1)
    combined, sums, late = moe(
        packed,
        cot_all,
        picks,
        w_gate,
        w_up,
        w_down,
        data_count // 4,
        tensor_count,
        slots,
        all_experts,
    )
    combined = wide(combined)
    grad_moe = combined[:, :width]
    grad_probs = combined[:, width : width + all_experts]
    grad_own = lax.dynamic_slice_in_dim(cotangent[0], own_start, block_rows, 0).astype(jnp.float32)
    grad_logits = (
        own_probs * (grad_probs - jnp.sum(own_probs * grad_probs, axis=-1, keepdims=True))
    ).astype(jnp.bfloat16)
    grad_moe = grad_moe + jnp.einsum(
        "re,de->rd", grad_logits, router_weight, preferred_element_type=jnp.float32
    )
    router_part = jnp.einsum("rd,re->de", moe_own, grad_logits, preferred_element_type=jnp.float32)
    ffn_pull = jax.vjp(rms_scale, residual, ffn_gain)[1]
    grad_res_norm, ffn_part = ffn_pull(grad_moe)
    grad_residual = grad_own + grad_res_norm
    grad_attn = (grad_residual * own_valid[:, None]).astype(jnp.bfloat16)
    attn_lower = lax.dynamic_slice_in_dim(grad_attn, core * depth, depth, 1)
    attn_upper = lax.dynamic_slice_in_dim(grad_attn, depth - core * depth, depth, 1)
    grad_heads = jnp.stack(
        [
            low(dot_nn(attn_lower, out_mine[t]) + dot_nn(attn_upper, out_other[t]))
            for t in range(tensor_count)
        ]
    )
    grad_mixed = lax.all_to_all(grad_heads, "tensor", 0, 0)
    grad_mixed, grad_attn = tie(grad_mixed, grad_attn)
    grad_attn_all = lax.all_gather(grad_attn, "tensor", axis=0, tiled=True)
    grad_mixed = grad_mixed.reshape(full_length, -1, head_dim)
    grad_query_parts = []
    grad_keys = jnp.zeros(key_low.shape, jnp.float32)
    grad_values = jnp.zeros(value_low.shape, jnp.float32)
    for order, start in enumerate(range(0, full_length, query_rows)):
        query_block = query_low[start : start + query_rows]
        grad_block = grad_mixed[start : start + query_rows]
        probs_block = jnp.exp(block_scores(query_block) - log_totals[order])
        probs_low = probs_block.astype(jnp.bfloat16)
        grad_values = grad_values + jnp.einsum(
            "hqk,qhd->khd", probs_low, grad_block, preferred_element_type=jnp.float32
        )
        grad_probs_block = jnp.einsum(
            "qhd,khd->hqk", grad_block, value_low, preferred_element_type=jnp.float32
        )
        delta = jnp.sum(probs_block * grad_probs_block, axis=-1, keepdims=True)
        grad_scores = (probs_block * (grad_probs_block - delta)).astype(jnp.bfloat16)
        grad_query_parts.append(
            jnp.einsum("hqk,khd->qhd", grad_scores, key_low, preferred_element_type=jnp.float32)
            * scale
        )
        grad_keys = (
            grad_keys
            + jnp.einsum(
                "hqk,qhd->khd", grad_scores, query_block, preferred_element_type=jnp.float32
            )
            * scale
        )
    grad_queries = jnp.concatenate(grad_query_parts, axis=0)
    query_pull = jax.vjp(prepare, query_unrotated, q_gain)[1]
    grad_query_raw, q_part = query_pull(grad_queries)
    key_pull = jax.vjp(prepare, key_raw, k_gain)[1]
    grad_key_raw, k_part = key_pull(grad_keys)
    grad_q_low = grad_query_raw.astype(jnp.bfloat16)
    grad_k_low = grad_key_raw.astype(jnp.bfloat16)
    grad_v_low = grad_values.reshape(full_length, local_width).astype(jnp.bfloat16)
    query_part = jnp.einsum("ld,lh->dh", gathered, grad_q_low, preferred_element_type=jnp.float32)
    value_part = jnp.einsum("ld,lh->dh", gathered, grad_v_low, preferred_element_type=jnp.float32)
    from_query = jnp.einsum("lh,dh->ld", grad_q_low, w_query, preferred_element_type=jnp.float32)
    from_key = jnp.einsum("lh,dh->ld", grad_k_low, w_key, preferred_element_type=jnp.float32)
    from_value = jnp.einsum("lh,dh->ld", grad_v_low, w_value, preferred_element_type=jnp.float32)
    query_part = plane.fold_core(low(query_part))
    value_part = plane.fold_core(low(value_part))
    grad_gathered = low(from_query + from_key + from_value)
    grad_gathered, grad_attn_all, sums, router_part, late, grad_k_late, query_part, value_part = tie(
        grad_gathered, grad_attn_all, sums, router_part, late, grad_k_low, query_part, value_part
    )
    cut = width // 2
    late = plane.fold_core(late.reshape(-1, width))
    late = [
        plane.scatter_rest(late[..., :cut], late.dtype, True),
        plane.scatter_rest(late[..., cut:], late.dtype, False),
    ]
    output = low(residual + combined[:, width + extra :] + jnp.concatenate(late, axis=1))
    grad_normed = wide(
        lax.psum_scatter(grad_gathered, "tensor", scatter_dimension=0, tiled=True)
    )
    grad_gate = jnp.swapaxes(sums[:, 0], 1, 2)
    grad_up = jnp.swapaxes(sums[:, 1], 1, 2)
    grad_down = sums[:, 2]
    key_part = jnp.einsum("ld,lh->dh", gathered, grad_k_late, preferred_element_type=jnp.float32)
    key_part = plane.fold_core(low(key_part))
    key_part, grad_gate, grad_up, grad_down = tie(key_part, grad_gate, grad_up, grad_down)
    out_part = jnp.einsum("ld,lh->dh", grad_attn_all, attended, preferred_element_type=jnp.float32)
    attn_pull = jax.vjp(rms_scale, token_values, attn_gain)[1]
    grad_tok_norm, attn_part = attn_pull(grad_normed)
    grad_tokens = (grad_residual + grad_tok_norm).astype(jnp.bfloat16)
    grad_out = plane.scatter(low(out_part), True)
    grad_value = plane.scatter_rest(value_part, value_part.dtype, False)
    grad_query = plane.scatter_rest(query_part, query_part.dtype, True)
    grad_key = plane.scatter_rest(key_part, key_part.dtype, False)
    routing = plane.scatter(jnp.concatenate([router_part, ffn_part[:, None]], axis=1), False)
    routing = ring_sum(routing, tensor_count)
    parts = [v.reshape(data_count, -1) for v in (attn_part, q_part, k_part)]
    gains = jnp.repeat(jnp.concatenate(parts, axis=1), tensor_count, axis=0)
    gains = jnp.sum(lax.all_to_all(gains, ("dp", "tensor"), 0, 0, tiled=True), axis=0)
    piece = width // data_count
    last = piece + head_dim // data_count
    return (
        output[None],
        grad_tokens[None],
        gains[:piece],
        grad_query,
        grad_key,
        grad_value,
        grad_out,
        gains[piece:last],
        gains[last:],
        routing[:, all_experts],
        routing[:, :all_experts],
        grad_gate,
        grad_up,
        grad_down,
    )


def solution(mesh):
    return jax.shard_map(
        per_device,
        mesh=mesh,
        in_specs=(
            P("dp", "tensor", None),
            P("dp"),
            P("dp", None, None),
            P(),
            P(None, "tensor"),
            P(None, "tensor"),
            P(None, "tensor"),
            P(None, "tensor"),
            P(),
            P(),
            P(),
            P(),
            P("dp", None, "tensor"),
            P("dp", None, "tensor"),
            P("dp", "tensor", None),
            P("dp", None, None),
        ),
        out_specs=(
            P("dp", "tensor", None),
            P("dp", "tensor", None),
            P("dp"),
            P("dp", "tensor"),
            P("dp", "tensor"),
            P("dp", "tensor"),
            P("dp", "tensor"),
            P("dp"),
            P("dp"),
            P("dp"),
            P("dp", None),
            P("dp", None, "tensor"),
            P("dp", None, "tensor"),
            P("dp", "tensor", None),
        ),
        check_vma=False,
    )
```

```python
import functools

import jax
import jax.numpy as jnp
from jax import lax
from jax.experimental import pallas as pl
from jax.experimental.pallas import tpu as pltpu
from jax.sharding import PartitionSpec as P

EPS = 1e-06
THETA = 50000.0
NEG = -1e30


def rms_scale(values, gain):
    return values * lax.rsqrt(jnp.mean(values * values, axis=-1, keepdims=True) + EPS) * gain


def rotate(values):
    length = values.shape[-3]
    half_dim = values.shape[-1] // 2
    positions = jnp.arange(length).astype(jnp.float32)
    rates = THETA ** (-jnp.arange(half_dim).astype(jnp.float32) / half_dim)
    angles = positions[:, None] * rates[None, :]
    cosine = jnp.cos(angles)[:, None, :]
    sine = jnp.sin(angles)[:, None, :]
    first = values[..., :half_dim]
    second = values[..., half_dim:]
    return jnp.concatenate(
        [first * cosine - second * sine, second * cosine + first * sine], axis=-1
    )


def prepare(raw, gain):
    shaped = raw.reshape(raw.shape[0], -1, gain.shape[0])
    return rotate(rms_scale(shaped, gain))


def dot_nt(a, b):
    return lax.dot_general(a, b, (((1,), (1,)), ((), ())), preferred_element_type=jnp.float32)


def dot_nn(a, b):
    return jnp.dot(a, b, preferred_element_type=jnp.float32)


def largest_tile(total, limit, unit):
    best = unit
    for tile in range(unit, limit + 1, unit):
        if total % tile == 0:
            best = tile
    return best


def moe_kernel(
    sizes,
    own_ref,
    *others_refs,
):
    blocks = 4 * sizes[0]
    moe_body(sizes, own_ref, others_refs[:blocks], *others_refs[blocks:])


def moe_body(
    sizes,
    own_ref,
    cot_refs,
    pick_ref,
    wg_ref,
    wu_ref,
    wd_ref,
    final_ref,
    acc_ref,
    late_ref,
    mine_ref,
    gather_ref,
    other_ref,
    both_ref,
    core_in,
    top_in,
    bottom_in,
    near_in,
    far_in,
    ring_out,
    ring_in,
    in_s,
    out_s,
    rows_s,
    crow_s,
    mrow_s,
    meta_s,
    aw_s,
    gg_s,
    gu_s,
    turn_s,
    acc_s,
    load_sem,
    store_sem,
    x_sem,
    c_sem,
    out_sem,
    fold_sem,
    plane_send,
    plane_recv,
    sum_send,
    sum_recv,
    ring_send,
    ring_recv,
    last_send,
    last_recv,
    late_sem,
):
    outer, chunks, experts, slots, rows, width, extra, all_experts = sizes
    blocks, half, cut = 4 * outer, 2 * outer, rows // 2
    full = width + extra
    span = full + width
    total = blocks * slots
    ring = gather_ref.shape[0]
    j = pl.program_id(0)
    s = pl.program_id(1)
    steps = 2 * blocks + experts
    me = lax.axis_index("dp")
    z = lax.axis_index("tensor")
    a, rest = me // 4, me % 4
    inner_id = me + 2 - 4 * ((me // 2) % 2)
    core_id = me + 1 - 2 * (me % 2)
    upper, lower = pl.ds(0, cut), pl.ds(cut, cut)
    x_part, y_part = pl.ds(0, full), pl.ds(full, width)

    def outer_id(k):
        return ((a + k + outer) % outer) * 4 + rest

    def remote(src, dst, send, recv, where, axis="dp"):
        return pltpu.make_async_remote_copy(
            src_ref=src,
            dst_ref=dst,
            send_sem=send,
            recv_sem=recv,
            device_id={axis: where},
            device_id_type=pl.DeviceIdType.MESH,
        )

    def plane_copy(c, src, dst, rows_at, ident, where):
        first = isinstance(src, int) and src == 0
        near = src if isinstance(src, int) else dst
        source = mine_ref.at[c] if first else gather_ref.at[c % ring, near - 1]
        target = gather_ref.at[c % ring, dst - 1]
        if rows_at is not None:
            source, target = source.at[rows_at], target.at[rows_at]
        return remote(source, target, plane_send.at[c, ident], plane_recv.at[c, ident], where)

    def near_copy(c):
        return plane_copy(c, 0, 1, None, 0, inner_id)

    def far_copy(c, k):
        return plane_copy(c, 0, 2 * k, None, k, outer_id(-k))

    def top_copy(c, k):
        return plane_copy(c, 1, 2 * k + 1, upper, outer - 1 + k, outer_id(-k))

    def bottom_copy(c, k):
        return plane_copy(c, 2 * k, 2 * k + 1, lower, 2 * outer - 2 + k, inner_id)

    def core_copy(c, q):
        return plane_copy(c, q, half + q, None, 3 * outer - 2 + q, core_id)

    def column(c):
        return (z + c + 1) % chunks

    def ring_copy(k):
        where = (z - k - 1 + chunks) % chunks
        return remote(own_ref, mine_ref.at[k], ring_send.at[k], ring_recv.at[k], where, "tensor")

    others = range(1, outer)

    def first_hop(c):
        near_copy(c).start()
        for k in others:
            far_copy(c, k).start()
        core_copy(c, 0).start()

    def second_hop(c):
        near_copy(c).wait_recv()
        for k in others:
            top_copy(c, k).start()
        for k in others:
            far_copy(c, k).wait_recv()
            bottom_copy(c, k).start()
        for q in [1] + [2 * k for k in others]:
            core_copy(c, q).start()

    def third_hop(c):
        for k in others:
            top_copy(c, k).wait_recv()
            bottom_copy(c, k).wait_recv()
            core_copy(c, 2 * k + 1).start()

    def drain_gather(c):
        near_copy(c).wait_send()
        for k in others:
            far_copy(c, k).wait_send()
            top_copy(c, k).wait_send()
            bottom_copy(c, k).wait_send()
        for q in range(half):
            core_copy(c, q).wait_send()

    def sum_copy(c, src, dst, ident, where):
        def each(act):
            def columns(size):
                part = pl.ds(0, size)
                source, target = src.at[:, part], dst.at[:, part]
                act(remote(source, target, sum_send.at[c, ident], sum_recv.at[c, ident], where))

            if isinstance(c, int):
                columns(full if c == chunks - 1 else span)
                return

            @pl.when(c < chunks - 1)
            def _():
                columns(span)

            @pl.when(c == chunks - 1)
            def _():
                columns(full)

        class Copy:
            def start(self):
                each(lambda copy: copy.start())

            def wait_recv(self):
                each(lambda copy: copy.wait_recv())

            def wait_send(self):
                each(lambda copy: copy.wait_send())

        return Copy()

    def late_copy(q, side, slot):
        owner = ((a + q // 2) % outer) * 4 + ((me // 2 + q) % 2) * 2 + (me + side) % 2
        return local(out_s.at[slot, :, y_part], late_ref.at[owner], late_sem.at[slot])

    def swap_copy(c, q):
        return sum_copy(c, other_ref.at[c % 2, q], core_in.at[c % 2, q], q, core_id)

    def both_at(c, q, rows_at):
        return both_ref.at[c % 2, q, rows_at]

    def up_copy(c, k):
        ident = half + k - 1
        return sum_copy(c, both_at(c, 2 * k + 1, upper), top_in.at[c % 2, k - 1], ident, outer_id(k))

    def down_copy(c, k):
        ident = half + outer - 1 + k - 1
        source = both_at(c, 2 * k + 1, lower)
        return sum_copy(c, source, bottom_in.at[c % 2, k - 1], ident, inner_id)

    def home_near(c, part):
        rows_at = (upper, lower)[part]
        ident = half + 2 * outer - 2 + part
        return sum_copy(c, both_at(c, 1, rows_at), near_in.at[c % 2, rows_at], ident, inner_id)

    def home_far(c, k, part):
        rows_at = (upper, lower)[part]
        ident = half + 2 * outer + 2 * (k - 1) + part
        target = far_in.at[c % 2, k - 1, rows_at]
        return sum_copy(c, both_at(c, 2 * k, rows_at), target, ident, outer_id(k))

    def last_copy(c):
        source, target = ring_out.at[c], ring_in.at[c]
        return remote(source, target, last_send.at[c], last_recv.at[c], column(c), "tensor")

    def local(src, dst, sem):
        return pltpu.make_async_copy(src, dst, sem)

    def together(*copies):
        for copy in copies:
            copy.start()
        for copy in copies:
            copy.wait()

    def fold_halves(c):
        for k in others:
            up_copy(c, k).wait_recv()
            down_copy(c, k).wait_recv()
            copies = [
                local(both_at(c, 2 * k, lower), in_s.at[0, lower], fold_sem.at[0]),
                local(top_in.at[c % 2, k - 1], in_s.at[1, upper], fold_sem.at[1]),
                local(bottom_in.at[c % 2, k - 1], in_s.at[1, lower], fold_sem.at[2]),
            ]
            if k == 1:
                copies.append(local(both_at(c, 1, upper), in_s.at[0, upper], fold_sem.at[3]))
            together(*copies)

            @pl.loop(0, rows // 16)
            def _(i):
                at = pl.ds(pl.multiple_of(i * 16, 16), 16)
                in_s[0, at, :] = low(wide(in_s[0, at, :]) + wide(in_s[1, at, :]))

            together(local(in_s.at[0, lower], both_at(c, 2 * k, lower), fold_sem.at[0]))
        together(local(in_s.at[0, upper], both_at(c, 1, upper), fold_sem.at[0]))
        for k in others:
            home_far(c, k, 1).start()
        home_near(c, 0).start()

    def fold_home(c):
        for part in (0, 1):
            home_near(c, part).wait_recv()
        together(
            local(both_ref.at[c % 2, 0], in_s.at[0], fold_sem.at[0]),
            local(near_in.at[c % 2], in_s.at[1], fold_sem.at[1]),
        )

        @pl.loop(0, rows // 16)
        def _(i):
            at = pl.ds(pl.multiple_of(i * 16, 16), 16)
            in_s[0, at, :] = low(wide(in_s[0, at, :]) + wide(in_s[1, at, :]))

        for k in others:
            for part in (0, 1):
                home_far(c, k, part).wait_recv()
            together(local(far_in.at[c % 2, k - 1], in_s.at[1], fold_sem.at[1]))

            @pl.loop(0, rows // 16)
            def _(i):
                at = pl.ds(pl.multiple_of(i * 16, 16), 16)
                in_s[0, at, :] = low(wide(in_s[0, at, :]) + wide(in_s[1, at, :]))


    def drain_sum(c):
        for q in range(half):
            swap_copy(c, q).wait_send()
        for k in others:
            up_copy(c, k).wait_send()
            down_copy(c, k).wait_send()
            for part in (0, 1):
                home_far(c, k, part).wait_send()
        for part in (0, 1):
            home_near(c, part).wait_send()

    def fetch(c, at):
        q, side, slot = at // 2, at % 2, at % 2
        r = side * half + q

        @pl.when(side == 1)
        def _():
            core_copy(c, q).wait_recv()

        rows_at = pl.ds(pl.multiple_of(column(c) * rows, rows), rows)
        @pl.when(r == 0)
        def _():
            local(mine_ref.at[c], in_s.at[slot, :, x_part], x_sem.at[slot]).start()

        @pl.when(r > 0)
        def _():
            source = gather_ref.at[c % ring, jnp.maximum(r - 1, 0)]
            local(source, in_s.at[slot, :, x_part], x_sem.at[slot]).start()

        for place, cot_ref in enumerate(cot_refs):

            @pl.when(r == place)
            def _():
                local(cot_ref.at[rows_at], in_s.at[slot, :, y_part], c_sem.at[slot]).start()


    def fetched(slot):
        local(mine_ref.at[0], in_s.at[slot, :, x_part], x_sem.at[slot]).wait()
        local(cot_refs[0].at[pl.ds(0, rows)], in_s.at[slot, :, y_part], c_sem.at[slot]).wait()

    def load(e, slot):
        return local(acc_ref.at[e], acc_s.at[slot], load_sem.at[slot])

    def store(e, slot):
        return local(acc_s.at[slot], acc_ref.at[e], store_sem.at[slot])

    @pl.when((j == 0) & (s == 0))
    def _():
        barrier = pltpu.get_barrier_semaphore()
        peers = [("dp", core_id), ("dp", inner_id)] + [("dp", outer_id(k)) for k in others]
        peers += [("tensor", (z + k) % chunks) for k in range(1, chunks)]
        for axis, where in peers:
            pl.semaphore_signal(
                barrier, inc=1, device_id={axis: where}, device_id_type=pl.DeviceIdType.MESH
            )
        pl.semaphore_wait(barrier, len(peers))
        ring_copy(0).start()
        together(local(own_ref, in_s.at[0, :, x_part], fold_sem.at[0]))
        together(local(in_s.at[0, :, x_part], mine_ref.at[chunks - 1], fold_sem.at[0]))
        ring_copy(0).wait_recv()
        for k in range(1, chunks - 1):
            ring_copy(k).start()
        first_hop(0)
        fetch(0, 0)
        second_hop(0)

    @pl.when((s == 0) & (j > 0))
    def _():
        load(0, 0).start()

    @pl.when((j == 0) & (s == 4))
    def _():
        third_hop(0)
        if chunks > 2:
            ring_copy(1).wait_recv()
        first_hop(1)

    @pl.when((s == blocks + experts) & (j + 1 < chunks))
    def _():
        third_hop(j + 1)

    @pl.when((s == blocks + 2) & (j >= 1))
    def _():
        fold_halves(j - 1)

    @pl.when((s == blocks + 2) & (j + 1 < chunks))
    def _():
        second_hop(j + 1)

    @pl.when((s == blocks + 2) & (j + 3 < chunks))
    def _():
        ring_copy(j + 2).wait_recv()

    @pl.when((s == blocks + 2) & (j + 2 < chunks))
    def _():
        first_hop(j + 2)

    @pl.when(s == blocks + 3)
    def _():
        drain_gather(j)

    @pl.when((s == blocks + experts + half - 1) & (j >= 1))
    def _():
        fold_home(j - 1)
        together(local(in_s.at[0], ring_out.at[j - 1], fold_sem.at[0]))
        last_copy(j - 1).start()
        drain_sum(j - 1)

    @pl.when(s < blocks)
    def _():
        slot = s % 2

        @pl.when(s + 1 < blocks)
        def _():
            fetch(j, s + 1)

        fetched(slot)
        meta = in_s[slot, :, width:full]
        picks = (dot_nt(pick_ref[...], meta) == 0.0).astype(jnp.bfloat16)
        at = pl.multiple_of(s * slots, slots)
        got = low(dot_nn(picks, in_s[slot, :, :full]))
        cot = low(dot_nn(picks, in_s[slot, :, full:]))
        for e in range(experts):
            part = slice(e * slots, (e + 1) * slots)
            rows_s[e, pl.ds(at, slots), :] = got[part, :width]
            mrow_s[e, pl.ds(at, slots), :] = got[part, width:]
            crow_s[e, pl.ds(at, slots), :] = cot[part]
        meta_s[s] = meta

    @pl.when((s >= blocks) & (s < blocks + experts))
    def _():
        e = s - blocks
        slot = e % 2
        tile = largest_tile(total, 320, 16)
        expert = me * experts + e
        wg = wg_ref[0]
        wu = wu_ref[0]
        wd = wd_ref[0]

        @pl.loop(0, total // tile)
        def _(m):
            ds = pl.ds(pl.multiple_of(m * tile, tile), tile)
            picked_rows = rows_s[e, ds, :]
            gate = dot_nn(picked_rows, wg)
            up = dot_nn(picked_rows, wu)
            grad_act = dot_nt(crow_s[e, ds, :], wd)
            meta = wide(mrow_s[e, ds, :])
            column = lax.broadcasted_iota(jnp.int32, meta.shape, 1)
            wanted = (column == expert) | (column == expert + all_experts)
            weight = jnp.sum(jnp.where(wanted, meta, 0.0), axis=1, keepdims=True)
            sig = jax.nn.sigmoid(gate)
            silu = gate * sig
            act = silu * up
            g_pick = jnp.sum(act * grad_act, axis=1, keepdims=True)
            scaled = weight * grad_act
            aw_s[ds, :] = low(weight * act)
            gg_s[ds, :] = low(scaled * up * sig * (1.0 + gate * (1.0 - sig)))
            gu_s[ds, :] = low(scaled * silu)
            mrow_s[e, ds, :] = low(jnp.where(column == expert, g_pick, 0.0))

        @pl.when(e >= 1)
        def _():
            store(e - 1, 1 - slot).wait()

        @pl.when(j == 0)
        def _():
            acc_s[slot] = jnp.zeros(acc_s.shape[1:], jnp.float32)

        @pl.when(j > 0)
        def _():
            load(e, slot).wait()

            @pl.when(e + 1 < experts)
            def _():
                load(e + 1, 1 - slot).start()

        cols = largest_tile(width, 512, 128)
        for which, (left, right) in enumerate(((gg_s, rows_s), (gu_s, rows_s), (aw_s, crow_s))):
            turn_s[...] = left[...].T

            @pl.loop(0, width // cols)
            def _(n):
                ds = pl.ds(pl.multiple_of(n * cols, cols), cols)
                add = dot_nn(turn_s[...], right[e, :, ds])
                acc_s[slot, which, :, ds] = acc_s[slot, which, :, ds] + add

        store(e, slot).start()

        @pl.loop(0, total // tile)
        def _(m):
            ds = pl.ds(pl.multiple_of(m * tile, tile), tile)
            crow_s[e, ds, :] = low(dot_nn(aw_s[ds, :], wd))
            rows_s[e, ds, :] = low(dot_nt(gg_s[ds, :], wg) + dot_nt(gu_s[ds, :], wu))

    first = blocks + experts

    def written(c, o):
        q, slot = half - 1 - o % half, o % 2

        @pl.when(c == chunks - 1)
        def _():
            late_copy(q, 1 - o // half, slot).wait()

        @pl.when(o < half)
        def _():
            local(out_s.at[slot], other_ref.at[c % 2, q], out_sem.at[slot]).wait()
            swap_copy(c, q).start()

        @pl.when(o >= half)
        def _():
            local(out_s.at[slot], both_ref.at[c % 2, q], out_sem.at[slot]).wait()

        for k in others:

            @pl.when((o >= half) & (q == 2 * k + 1))
            def _():
                up_copy(c, k).start()
                down_copy(c, k).start()

            @pl.when((o >= half) & (q == 2 * k))
            def _():
                home_far(c, k, 0).start()

        @pl.when((o >= half) & (q == 1))
        def _():
            home_near(c, 1).start()

    @pl.when(s >= first)
    def _():
        o = s - first
        slot = o % 2
        q = half - 1 - o % half
        side = 1 - o // half
        place = 2 * q + side
        at = pl.multiple_of(place * slots, slots)

        @pl.when(o >= 1)
        def _():
            written(j, o - 1)

        @pl.when((o >= half - 1) & (o < 2 * half - 1))
        def _():
            coming = half - 1 - (o + 1) % half
            swap_copy(j, coming).wait_recv()
            local(core_in.at[j % 2, coming], in_s.at[1 - slot], x_sem.at[1 - slot]).start()

        @pl.when(o >= half)
        def _():
            local(core_in.at[j % 2, q], in_s.at[slot], x_sem.at[slot]).wait()

        @pl.when((o >= half) & (j == chunks - 1))
        def _():
            in_s[slot, :, full:] = jnp.zeros((rows, width), jnp.bfloat16)

        @pl.when(o < half)
        def _():
            in_s[slot] = jnp.zeros((rows, span), jnp.bfloat16)

        picks = (dot_nt(meta_s[place], pick_ref[...]) == 0.0).astype(jnp.bfloat16)
        flat = (experts * slots, width)
        g = dot_nn(picks, rows_s[:, pl.ds(at, slots), :].reshape(flat))
        out_s[slot, :, :width] = low(g + wide(in_s[slot, :, :width]))
        flat = (experts * slots, extra)
        p = dot_nn(picks, mrow_s[:, pl.ds(at, slots), :].reshape(flat))
        out_s[slot, :, width:full] = low(p + wide(in_s[slot, :, width:full]))
        flat = (experts * slots, width)
        y = dot_nn(picks, crow_s[:, pl.ds(at, slots), :].reshape(flat))
        out_s[slot, :, full:] = low(y + wide(in_s[slot, :, full:]))

        @pl.when(j == chunks - 1)
        def _():
            late_copy(q, side, slot).start()

        @pl.when(o < half)
        def _():
            local(out_s.at[slot], other_ref.at[j % 2, q], out_sem.at[slot]).start()

        @pl.when(o >= half)
        def _():
            local(out_s.at[slot], both_ref.at[j % 2, q], out_sem.at[slot]).start()

        @pl.when(s == steps - 1)
        def _():
            written(j, o)
            store(experts - 1, (experts - 1) % 2).wait()

        @pl.when((s == steps - 1) & (j + 1 < chunks))
        def _():
            fetch(j + 1, 0)

    @pl.when((s == steps - 1) & (j == chunks - 1))
    def _():
        fold_halves(chunks - 1)
        fold_home(chunks - 1)
        drain_sum(chunks - 1)
        in_s[0, :, full:] = jnp.zeros((rows, width), jnp.bfloat16)
        for k in range(chunks - 1):
            last_copy(k).wait_recv()
            together(local(ring_in.at[k], in_s.at[1], fold_sem.at[1]))

            @pl.loop(0, rows // 16)
            def _(i):
                at = pl.ds(pl.multiple_of(i * 16, 16), 16)
                in_s[0, at, :] = low(wide(in_s[0, at, :]) + wide(in_s[1, at, :]))

        together(local(in_s.at[0], final_ref, fold_sem.at[0]))
        for k in range(chunks - 1):
            last_copy(k).wait_send()
            ring_copy(k).wait_send()


def moe(own, cot, picks, wg, wu, wd, outer, chunks, slots, all_experts):
    rows, full = own.shape
    width = cot[0].shape[1]
    extra = full - width
    span = full + width
    experts, _, hidden = wg.shape
    blocks, half, cut = 4 * outer, 2 * outer, rows // 2
    total = blocks * slots
    sizes = (outer, chunks, experts, slots, rows, width, extra, all_experts)

    def expert_at(j, s):
        return (jnp.clip(s - blocks, 0, experts - 1), 0, 0)

    anywhere = pl.BlockSpec(memory_space=pl.ANY)
    in_specs = [
        *[anywhere] * (1 + len(cot)),
        pl.BlockSpec(picks.shape, lambda j, s: (0, 0)),
        pl.BlockSpec((1, width, hidden), expert_at),
        pl.BlockSpec((1, width, hidden), expert_at),
        pl.BlockSpec((1, hidden, width), expert_at),
    ]
    bf16 = jnp.bfloat16
    shapes = [
        ((rows, span), bf16),
        ((experts, 3, hidden, width), jnp.float32),
        ((blocks, rows, width), bf16),
        ((chunks, rows, full), bf16),
        ((chunks if chunks <= 4 else 3, blocks - 1, rows, full), bf16),
        ((2, half, rows, span), bf16),
        ((2, half, rows, span), bf16),
        ((2, half, rows, span), bf16),
        ((2, outer - 1, cut, span), bf16),
        ((2, outer - 1, cut, span), bf16),
        ((2, rows, span), bf16),
        ((2, outer - 1, rows, span), bf16),
        ((chunks - 1, rows, span), bf16),
        ((chunks - 1, rows, span), bf16),
    ]
    dma = pltpu.SemaphoreType.DMA
    gathers, sums = 5 * outer - 2, 6 * outer - 2
    scratch = [
        pltpu.VMEM((2, rows, span), bf16),
        pltpu.VMEM((2, rows, span), bf16),
        pltpu.VMEM((experts, total, width), bf16),
        pltpu.VMEM((experts, total, width), bf16),
        pltpu.VMEM((experts, total, extra), bf16),
        pltpu.VMEM((blocks, rows, extra), bf16),
        pltpu.VMEM((total, hidden), bf16),
        pltpu.VMEM((total, hidden), bf16),
        pltpu.VMEM((total, hidden), bf16),
        pltpu.VMEM((hidden, total), bf16),
        pltpu.VMEM((2, 3, hidden, width), jnp.float32),
        dma((2,)),
        dma((2,)),
        dma((2,)),
        dma((2,)),
        dma((2,)),
        dma((4,)),
        dma((chunks, gathers)),
        dma((chunks, gathers)),
        dma((chunks, sums)),
        dma((chunks, sums)),
        dma((chunks,)),
        dma((chunks,)),
        dma((chunks,)),
        dma((chunks,)),
        dma((2,)),
    ]
    flops = 2 * chunks * experts * total * width * (hidden * 9 + 4 * rows)
    results = pl.pallas_call(
        functools.partial(moe_kernel, sizes),
        grid=(chunks, 2 * blocks + experts),
        in_specs=in_specs,
        out_specs=[anywhere] * len(shapes),
        out_shape=[jax.ShapeDtypeStruct(*shape) for shape in shapes],
        scratch_shapes=scratch,
        compiler_params=pltpu.CompilerParams(
            dimension_semantics=("arbitrary", "arbitrary"),
            vmem_limit_bytes=66_500_000,
            collective_id=0,
            has_side_effects=True,
        ),
        cost_estimate=pl.CostEstimate(
            flops=flops, bytes_accessed=blocks * chunks * rows * full * 8, transcendentals=0
        ),
        name="moe",
    )(own, *cot, picks, wg, wu, wd)
    return results[:3]


def wide(values):
    return values.astype(jnp.float32)


def low(values):
    return values.astype(jnp.bfloat16)


def tie(*values):
    return lax.optimization_barrier(values)


def ring_sum(values, count):
    total = values
    for step in range(1, count):
        pairs = [(i, (i + step) % count) for i in range(count)]
        total = total + lax.ppermute(values, "tensor", pairs)
    return total


def pick(values, at, axis):
    return lax.dynamic_index_in_dim(values, at, axis, keepdims=False)


class Plane:
    def __init__(self, count):
        self.outer = count // 4
        everyone = range(count)
        self.core = [(i, i ^ 1) for i in everyone]
        self.inner = [(i, i ^ 2) for i in everyone]
        self.count = count

    def pull(self, values, k):
        pairs = [((i + 4 * k) % self.count, i) for i in range(self.count)]
        return lax.ppermute(values, "dp", pairs)

    def swap_inner(self, values):
        return lax.ppermute(values, "dp", self.inner)

    def swap_core(self, values):
        return lax.ppermute(values, "dp", self.core)

    def push(self, values, k):
        pairs = [(i, (i + 4 * k) % self.count) for i in range(self.count)]
        return lax.ppermute(values, "dp", pairs)

    def fold_inner(self, parts, b, axis, kind):
        given = self.swap_inner(pick(parts, 1 - b, axis).astype(kind))
        return wide(pick(parts, b, axis)) + wide(given)

    def fold_outer(self, parts, a, kind):
        total = wide(pick(parts, a, 0))
        for k in range(1, self.outer):
            given = pick(parts, (a + k) % self.outer, 0).astype(kind)
            total = total + wide(self.push(given, k))
        return total

    def scatter(self, values, inner_first):
        kind = values.dtype
        return self.scatter_rest(self.fold_core(values), kind, inner_first)

    def fold_core(self, values):
        core = lax.axis_index("dp") % 2
        parts = values.reshape(self.outer, 2, 2, values.shape[0] // self.count, values.shape[1])
        given = self.swap_core(pick(parts, 1 - core, 2))
        return (wide(pick(parts, core, 2)) + wide(given)).astype(values.dtype)

    def scatter_rest(self, parts, kind, inner_first):
        index = lax.axis_index("dp")
        b, a = index // 2 % 2, index // 4
        if inner_first:
            return self.fold_outer(self.fold_inner(parts, b, 1, kind).astype(kind), a, kind)
        return self.fold_inner(self.fold_outer(parts, a, kind).astype(kind), b, 0, kind)

    def first(self, own):
        return self.swap_inner(own), [self.pull(own, k) for k in range(1, self.outer)]

    def second(self, near, fars):
        half = near.shape[0] // 2
        return [
            jnp.concatenate([self.pull(near[:half], k + 1), self.swap_inner(far[half:])], axis=0)
            for k, far in enumerate(fars)
        ]

    def third(self, own, near, fars, diagonals, swapped):
        mine = [own, near]
        for far, diagonal in zip(fars, diagonals):
            mine += [far, diagonal]
        other = swapped[:2]
        for far, diagonal in zip(swapped[2:], diagonals):
            other += [far, self.swap_core(diagonal)]
        return mine + other


def per_device(
    tokens,
    lengths,
    routes,
    attn_gain,
    w_query,
    w_key,
    w_value,
    w_out,
    q_gain,
    k_gain,
    ffn_gain,
    router_weight,
    w_gate,
    w_up,
    w_down,
    cotangent,
):
    tensor_count = lax.axis_size("tensor")
    data_count = lax.axis_size("dp")
    tensor_rank = lax.axis_index("tensor")
    block_rows = tokens.shape[1]
    width = tokens.shape[2]
    full_length = block_rows * tensor_count
    route_count = routes.shape[2]
    local_experts = w_gate.shape[0]
    all_experts = local_experts * data_count
    head_dim = q_gain.shape[0]
    local_width = w_query.shape[1]
    capacity = max(2, (block_rows * route_count * 5 + 4 * all_experts - 1) // (4 * all_experts))
    query_rows = min(512, full_length)
    scale = head_dim ** (-0.5)
    own_start = tensor_rank * block_rows
    token_values = tokens[0].astype(jnp.float32)
    seq_length = lengths[0]
    own_valid = (own_start + jnp.arange(block_rows) < seq_length).astype(jnp.float32)
    key_valid = jnp.arange(full_length) < seq_length
    normed = rms_scale(token_values, attn_gain).astype(jnp.bfloat16)
    gathered = lax.all_gather(normed, "tensor", axis=0, tiled=True)
    plane = Plane(data_count)
    near, fars = plane.first(cotangent[0])
    core = lax.axis_index("dp") % 2
    depth = width // 2
    out_half = lax.dynamic_slice_in_dim(w_out, core * depth, depth, 0)
    gathered, near, fars, out_half = tie(gathered, near, fars, out_half)
    out_mine = lax.all_gather(out_half, "tensor", axis=0)
    query_unrotated = jnp.dot(gathered, w_query, preferred_element_type=jnp.float32)
    key_raw = jnp.dot(gathered, w_key, preferred_element_type=jnp.float32)
    value_raw = jnp.dot(gathered, w_value, preferred_element_type=jnp.float32)
    query_low = prepare(query_unrotated, q_gain).astype(jnp.bfloat16)
    key_low = prepare(key_raw, k_gain).astype(jnp.bfloat16)
    value_low = value_raw.astype(jnp.bfloat16).reshape(full_length, -1, head_dim)

    def block_scores(query_block):
        scores = (
            jnp.einsum("qhd,khd->hqk", query_block, key_low, preferred_element_type=jnp.float32)
            * scale
        )
        return jnp.where(key_valid[None, None, :], scores, NEG)

    mixed_parts = []
    log_totals = []
    for start in range(0, full_length, query_rows):
        scores = block_scores(query_low[start : start + query_rows])
        row_peak = jnp.max(scores, axis=-1, keepdims=True)
        powers = jnp.exp(scores - row_peak)
        total = jnp.sum(powers, axis=-1, keepdims=True)
        weights = (powers / total).astype(jnp.bfloat16)
        mixed_parts.append(
            jnp.einsum("hqk,khd->qhd", weights, value_low, preferred_element_type=jnp.float32)
        )
        log_totals.append(row_peak + jnp.log(total))
    attended = (
        jnp.concatenate(mixed_parts, axis=0).reshape(full_length, local_width).astype(jnp.bfloat16)
    )
    diagonals = plane.second(near, fars)
    swapped = [plane.swap_core(part) for part in (cotangent[0], near, *fars)]
    attended, diagonals, swapped = tie(attended, diagonals, swapped)
    cot_all = plane.third(cotangent[0], near, fars, diagonals, swapped)
    heads_own = lax.all_to_all(
        attended.reshape(tensor_count, block_rows, local_width), "tensor", 0, 0
    )
    heads_own, out_mine = tie(heads_own, out_mine)
    out_other = plane.swap_core(out_mine)
    heads_own = heads_own.reshape(tensor_count, block_rows, local_width)

    def from_heads(out_weight):
        return sum(dot_nt(heads_own[t], out_weight[t]) for t in range(tensor_count))

    attn_mine, attn_other = from_heads(out_mine), from_heads(out_other)
    attn_own = jnp.where(
        core == 0,
        jnp.concatenate([attn_mine, attn_other], axis=1),
        jnp.concatenate([attn_other, attn_mine], axis=1),
    )
    residual = token_values + own_valid[:, None] * attn_own
    moe_own = rms_scale(residual, ffn_gain).astype(jnp.bfloat16)
    router_logits = jnp.dot(moe_own, router_weight, preferred_element_type=jnp.float32)
    own_probs = jax.nn.softmax(router_logits, axis=-1)
    own_routes = lax.dynamic_slice_in_dim(routes[0], own_start, block_rows, 0)
    onehot = own_routes[:, :, None] == jnp.arange(all_experts)[None, None, :]
    named = jnp.any(onehot, axis=1) & (own_valid[:, None] > 0.0)
    named_low = named.astype(jnp.bfloat16)
    before = jnp.arange(block_rows)[:, None] > jnp.arange(block_rows)[None, :]
    order = jnp.dot(before.astype(jnp.bfloat16), named_low, preferred_element_type=jnp.float32)
    place = jnp.where(named, order, -1.0).astype(jnp.bfloat16)
    weight = jnp.where(named, own_probs, 0.0)
    weight_high = weight.astype(jnp.bfloat16)
    weight_low = (weight - weight_high.astype(jnp.float32)).astype(jnp.bfloat16)
    used = 3 * all_experts + 1
    extra = (used + 127) // 128 * 128
    meta = jnp.concatenate(
        [
            weight_high,
            weight_low,
            place,
            jnp.ones((block_rows, 1), jnp.bfloat16),
            jnp.zeros((block_rows, extra - used), jnp.bfloat16),
        ],
        axis=1,
    )
    slots = (capacity + 15) // 16 * 16
    first_expert = lax.axis_index("dp") * local_experts
    slot_row = jnp.arange(local_experts * slots)[:, None]
    slot_column = jnp.arange(extra)[None, :]
    picks = jnp.where(
        slot_column == 2 * all_experts + first_expert + slot_row // slots,
        1.0,
        jnp.where(slot_column == 3 * all_experts, -(slot_row % slots).astype(jnp.float32), 0.0),
    ).astype(jnp.bfloat16)
    packed = jnp.concatenate([moe_own, meta], axis=1)
    combined, sums, late = moe(
        packed,
        cot_all,
        picks,
        w_gate,
        w_up,
        w_down,
        data_count // 4,
        tensor_count,
        slots,
        all_experts,
    )
    combined = wide(combined)
    grad_moe = combined[:, :width]
    grad_probs = combined[:, width : width + all_experts]
    late = plane.fold_core(late.reshape(-1, width))
    grad_own = lax.dynamic_slice_in_dim(cotangent[0], own_start, block_rows, 0).astype(jnp.float32)
    grad_logits = (
        own_probs * (grad_probs - jnp.sum(own_probs * grad_probs, axis=-1, keepdims=True))
    ).astype(jnp.bfloat16)
    grad_moe = grad_moe + jnp.einsum(
        "re,de->rd", grad_logits, router_weight, preferred_element_type=jnp.float32
    )
    router_part = jnp.einsum("rd,re->de", moe_own, grad_logits, preferred_element_type=jnp.float32)
    ffn_pull = jax.vjp(rms_scale, residual, ffn_gain)[1]
    grad_res_norm, ffn_part = ffn_pull(grad_moe)
    grad_residual = grad_own + grad_res_norm
    grad_attn = (grad_residual * own_valid[:, None]).astype(jnp.bfloat16)
    attn_lower = lax.dynamic_slice_in_dim(grad_attn, core * depth, depth, 1)
    attn_upper = lax.dynamic_slice_in_dim(grad_attn, depth - core * depth, depth, 1)
    grad_heads = jnp.stack(
        [
            low(dot_nn(attn_lower, out_mine[t]) + dot_nn(attn_upper, out_other[t]))
            for t in range(tensor_count)
        ]
    )
    grad_mixed = lax.all_to_all(grad_heads, "tensor", 0, 0)
    grad_attn_all = lax.all_gather(grad_attn, "tensor", axis=0, tiled=True)
    grad_mixed = grad_mixed.reshape(full_length, -1, head_dim)
    grad_query_parts = []
    grad_keys = jnp.zeros(key_low.shape, jnp.float32)
    grad_values = jnp.zeros(value_low.shape, jnp.float32)
    for order, start in enumerate(range(0, full_length, query_rows)):
        query_block = query_low[start : start + query_rows]
        grad_block = grad_mixed[start : start + query_rows]
        probs_block = jnp.exp(block_scores(query_block) - log_totals[order])
        probs_low = probs_block.astype(jnp.bfloat16)
        grad_values = grad_values + jnp.einsum(
            "hqk,qhd->khd", probs_low, grad_block, preferred_element_type=jnp.float32
        )
        grad_probs_block = jnp.einsum(
            "qhd,khd->hqk", grad_block, value_low, preferred_element_type=jnp.float32
        )
        delta = jnp.sum(probs_block * grad_probs_block, axis=-1, keepdims=True)
        grad_scores = (probs_block * (grad_probs_block - delta)).astype(jnp.bfloat16)
        grad_query_parts.append(
            jnp.einsum("hqk,khd->qhd", grad_scores, key_low, preferred_element_type=jnp.float32)
            * scale
        )
        grad_keys = (
            grad_keys
            + jnp.einsum(
                "hqk,qhd->khd", grad_scores, query_block, preferred_element_type=jnp.float32
            )
            * scale
        )
    grad_queries = jnp.concatenate(grad_query_parts, axis=0)
    query_pull = jax.vjp(prepare, query_unrotated, q_gain)[1]
    grad_query_raw, q_part = query_pull(grad_queries)
    key_pull = jax.vjp(prepare, key_raw, k_gain)[1]
    grad_key_raw, k_part = key_pull(grad_keys)
    grad_q_low = grad_query_raw.astype(jnp.bfloat16)
    grad_k_low = grad_key_raw.astype(jnp.bfloat16)
    grad_v_low = grad_values.reshape(full_length, local_width).astype(jnp.bfloat16)
    query_part = jnp.einsum("ld,lh->dh", gathered, grad_q_low, preferred_element_type=jnp.float32)
    value_part = jnp.einsum("ld,lh->dh", gathered, grad_v_low, preferred_element_type=jnp.float32)
    from_query = jnp.einsum("lh,dh->ld", grad_q_low, w_query, preferred_element_type=jnp.float32)
    from_key = jnp.einsum("lh,dh->ld", grad_k_low, w_key, preferred_element_type=jnp.float32)
    from_value = jnp.einsum("lh,dh->ld", grad_v_low, w_value, preferred_element_type=jnp.float32)
    grad_gathered, grad_attn_all, sums = tie(
        low(from_query + from_key + from_value), grad_attn_all, sums
    )
    cut = width // 2
    late = [
        plane.scatter_rest(late[..., :cut], late.dtype, True),
        plane.scatter_rest(late[..., cut:], late.dtype, False),
    ]
    output = low(residual + combined[:, width + extra :] + jnp.concatenate(late, axis=1))
    grad_normed = wide(
        lax.psum_scatter(grad_gathered, "tensor", scatter_dimension=0, tiled=True)
    )
    grad_gate = jnp.swapaxes(sums[:, 0], 1, 2)
    grad_up = jnp.swapaxes(sums[:, 1], 1, 2)
    grad_down = sums[:, 2]
    grad_k_low, grad_gate, grad_up, grad_down = tie(grad_k_low, grad_gate, grad_up, grad_down)
    key_part = jnp.einsum("ld,lh->dh", gathered, grad_k_low, preferred_element_type=jnp.float32)
    out_part = jnp.einsum("ld,lh->dh", grad_attn_all, attended, preferred_element_type=jnp.float32)
    attn_pull = jax.vjp(rms_scale, token_values, attn_gain)[1]
    grad_tok_norm, attn_part = attn_pull(grad_normed)
    grad_tokens = (grad_residual + grad_tok_norm).astype(jnp.bfloat16)
    grad_out = plane.scatter(low(out_part), True)
    grad_value = plane.scatter(low(value_part), False)
    grad_query = plane.scatter(low(query_part), True)
    grad_key = plane.scatter(low(key_part), False)
    routing = plane.scatter(jnp.concatenate([router_part, ffn_part[:, None]], axis=1), False)
    routing = ring_sum(routing, tensor_count)
    parts = [v.reshape(data_count, -1) for v in (attn_part, q_part, k_part)]
    gains = jnp.repeat(jnp.concatenate(parts, axis=1), tensor_count, axis=0)
    gains = jnp.sum(lax.all_to_all(gains, ("dp", "tensor"), 0, 0, tiled=True), axis=0)
    piece = width // data_count
    last = piece + head_dim // data_count
    return (
        output[None],
        grad_tokens[None],
        gains[:piece],
        grad_query,
        grad_key,
        grad_value,
        grad_out,
        gains[piece:last],
        gains[last:],
        routing[:, all_experts],
        routing[:, :all_experts],
        grad_gate,
        grad_up,
        grad_down,
    )


def solution(mesh):
    return jax.shard_map(
        per_device,
        mesh=mesh,
        in_specs=(
            P("dp", "tensor", None),
            P("dp"),
            P("dp", None, None),
            P(),
            P(None, "tensor"),
            P(None, "tensor"),
            P(None, "tensor"),
            P(None, "tensor"),
            P(),
            P(),
            P(),
            P(),
            P("dp", None, "tensor"),
            P("dp", None, "tensor"),
            P("dp", "tensor", None),
            P("dp", None, None),
        ),
        out_specs=(
            P("dp", "tensor", None),
            P("dp", "tensor", None),
            P("dp"),
            P("dp", "tensor"),
            P("dp", "tensor"),
            P("dp", "tensor"),
            P("dp", "tensor"),
            P("dp"),
            P("dp"),
            P("dp"),
            P("dp", None),
            P("dp", None, "tensor"),
            P("dp", None, "tensor"),
            P("dp", "tensor", None),
        ),
        check_vma=False,
    )
```

```python
import functools

import jax
import jax.numpy as jnp
from jax import lax
from jax.experimental import pallas as pl
from jax.experimental.pallas import tpu as pltpu
from jax.sharding import PartitionSpec as P

EPS = 1e-06
THETA = 50000.0
NEG = -1e30


def rms_scale(values, gain):
    return values * lax.rsqrt(jnp.mean(values * values, axis=-1, keepdims=True) + EPS) * gain


def rotate(values):
    length = values.shape[-3]
    half_dim = values.shape[-1] // 2
    positions = jnp.arange(length).astype(jnp.float32)
    rates = THETA ** (-jnp.arange(half_dim).astype(jnp.float32) / half_dim)
    angles = positions[:, None] * rates[None, :]
    cosine = jnp.cos(angles)[:, None, :]
    sine = jnp.sin(angles)[:, None, :]
    first = values[..., :half_dim]
    second = values[..., half_dim:]
    return jnp.concatenate(
        [first * cosine - second * sine, second * cosine + first * sine], axis=-1
    )


def prepare(raw, gain):
    shaped = raw.reshape(raw.shape[0], -1, gain.shape[0])
    return rotate(rms_scale(shaped, gain))


def dot_nt(a, b):
    return lax.dot_general(a, b, (((1,), (1,)), ((), ())), preferred_element_type=jnp.float32)


def dot_nn(a, b):
    return jnp.dot(a, b, preferred_element_type=jnp.float32)


def largest_tile(total, limit, unit):
    best = unit
    for tile in range(unit, limit + 1, unit):
        if total % tile == 0:
            best = tile
    return best


def moe_kernel(
    sizes,
    own_ref,
    *others_refs,
):
    blocks = 4 * sizes[0]
    moe_body(sizes, own_ref, others_refs[:blocks], *others_refs[blocks:])


def moe_body(
    sizes,
    own_ref,
    cot_refs,
    pick_ref,
    wg_ref,
    wu_ref,
    wd_ref,
    final_ref,
    acc_ref,
    mine_ref,
    gather_ref,
    other_ref,
    both_ref,
    core_in,
    top_in,
    bottom_in,
    near_in,
    far_in,
    ring_out,
    ring_in,
    in_s,
    out_s,
    rows_s,
    crow_s,
    mrow_s,
    meta_s,
    aw_s,
    gg_s,
    gu_s,
    turn_s,
    acc_s,
    load_sem,
    store_sem,
    x_sem,
    c_sem,
    out_sem,
    fold_sem,
    plane_send,
    plane_recv,
    sum_send,
    sum_recv,
    ring_send,
    ring_recv,
    last_send,
    last_recv,
):
    outer, chunks, experts, slots, rows, width, extra, all_experts = sizes
    blocks, half, cut = 4 * outer, 2 * outer, rows // 2
    full = width + extra
    span = full + width
    total = blocks * slots
    ring = gather_ref.shape[0]
    j = pl.program_id(0)
    s = pl.program_id(1)
    steps = 2 * blocks + experts
    me = lax.axis_index("dp")
    z = lax.axis_index("tensor")
    a, rest = me // 4, me % 4
    inner_id = me + 2 - 4 * ((me // 2) % 2)
    core_id = me + 1 - 2 * (me % 2)
    upper, lower = pl.ds(0, cut), pl.ds(cut, cut)
    x_part, y_part = pl.ds(0, full), pl.ds(full, width)

    def outer_id(k):
        return ((a + k + outer) % outer) * 4 + rest

    def remote(src, dst, send, recv, where, axis="dp"):
        return pltpu.make_async_remote_copy(
            src_ref=src,
            dst_ref=dst,
            send_sem=send,
            recv_sem=recv,
            device_id={axis: where},
            device_id_type=pl.DeviceIdType.MESH,
        )

    def plane_copy(c, src, dst, rows_at, ident, where):
        first = isinstance(src, int) and src == 0
        near = src if isinstance(src, int) else dst
        source = mine_ref.at[c] if first else gather_ref.at[c % ring, near - 1]
        target = gather_ref.at[c % ring, dst - 1]
        if rows_at is not None:
            source, target = source.at[rows_at], target.at[rows_at]
        return remote(source, target, plane_send.at[c, ident], plane_recv.at[c, ident], where)

    def near_copy(c):
        return plane_copy(c, 0, 1, None, 0, inner_id)

    def far_copy(c, k):
        return plane_copy(c, 0, 2 * k, None, k, outer_id(-k))

    def top_copy(c, k):
        return plane_copy(c, 1, 2 * k + 1, upper, outer - 1 + k, outer_id(-k))

    def bottom_copy(c, k):
        return plane_copy(c, 2 * k, 2 * k + 1, lower, 2 * outer - 2 + k, inner_id)

    def core_copy(c, q):
        return plane_copy(c, q, half + q, None, 3 * outer - 2 + q, core_id)

    def column(c):
        return (z + c + 1) % chunks

    def ring_copy(k):
        where = (z - k - 1 + chunks) % chunks
        return remote(own_ref, mine_ref.at[k], ring_send.at[k], ring_recv.at[k], where, "tensor")

    others = range(1, outer)

    def first_hop(c):
        near_copy(c).start()
        for k in others:
            far_copy(c, k).start()
        core_copy(c, 0).start()

    def second_hop(c):
        near_copy(c).wait_recv()
        for k in others:
            top_copy(c, k).start()
        for k in others:
            far_copy(c, k).wait_recv()
            bottom_copy(c, k).start()
        for q in [1] + [2 * k for k in others]:
            core_copy(c, q).start()

    def third_hop(c):
        for k in others:
            top_copy(c, k).wait_recv()
            bottom_copy(c, k).wait_recv()
            core_copy(c, 2 * k + 1).start()

    def drain_gather(c):
        near_copy(c).wait_send()
        for k in others:
            far_copy(c, k).wait_send()
            top_copy(c, k).wait_send()
            bottom_copy(c, k).wait_send()
        for q in range(half):
            core_copy(c, q).wait_send()

    def sum_copy(c, src, dst, ident, where):
        return remote(src, dst, sum_send.at[c, ident], sum_recv.at[c, ident], where)

    def swap_copy(c, q):
        return sum_copy(c, other_ref.at[c % 2, q], core_in.at[c % 2, q], q, core_id)

    def both_at(c, q, rows_at):
        return both_ref.at[c % 2, q, rows_at]

    def up_copy(c, k):
        ident = half + k - 1
        return sum_copy(c, both_at(c, 2 * k + 1, upper), top_in.at[c % 2, k - 1], ident, outer_id(k))

    def down_copy(c, k):
        ident = half + outer - 1 + k - 1
        source = both_at(c, 2 * k + 1, lower)
        return sum_copy(c, source, bottom_in.at[c % 2, k - 1], ident, inner_id)

    def home_near(c, part):
        rows_at = (upper, lower)[part]
        ident = half + 2 * outer - 2 + part
        return sum_copy(c, both_at(c, 1, rows_at), near_in.at[c % 2, rows_at], ident, inner_id)

    def home_far(c, k, part):
        rows_at = (upper, lower)[part]
        ident = half + 2 * outer + 2 * (k - 1) + part
        target = far_in.at[c % 2, k - 1, rows_at]
        return sum_copy(c, both_at(c, 2 * k, rows_at), target, ident, outer_id(k))

    def last_copy(c):
        source, target = ring_out.at[c], ring_in.at[c]
        return remote(source, target, last_send.at[c], last_recv.at[c], column(c), "tensor")

    def local(src, dst, sem):
        return pltpu.make_async_copy(src, dst, sem)

    def together(*copies):
        for copy in copies:
            copy.start()
        for copy in copies:
            copy.wait()

    def fold_halves(c):
        for k in others:
            up_copy(c, k).wait_recv()
            down_copy(c, k).wait_recv()
            copies = [
                local(both_at(c, 2 * k, lower), in_s.at[0, lower], fold_sem.at[0]),
                local(top_in.at[c % 2, k - 1], in_s.at[1, upper], fold_sem.at[1]),
                local(bottom_in.at[c % 2, k - 1], in_s.at[1, lower], fold_sem.at[2]),
            ]
            if k == 1:
                copies.append(local(both_at(c, 1, upper), in_s.at[0, upper], fold_sem.at[3]))
            together(*copies)

            @pl.loop(0, rows // 16)
            def _(i):
                at = pl.ds(pl.multiple_of(i * 16, 16), 16)
                in_s[0, at, :] = low(wide(in_s[0, at, :]) + wide(in_s[1, at, :]))

            together(local(in_s.at[0, lower], both_at(c, 2 * k, lower), fold_sem.at[0]))
        together(local(in_s.at[0, upper], both_at(c, 1, upper), fold_sem.at[0]))
        for k in others:
            home_far(c, k, 1).start()
        home_near(c, 0).start()

    def fold_home(c):
        for part in (0, 1):
            home_near(c, part).wait_recv()
        together(
            local(both_ref.at[c % 2, 0], in_s.at[0], fold_sem.at[0]),
            local(near_in.at[c % 2], in_s.at[1], fold_sem.at[1]),
        )

        @pl.loop(0, rows // 16)
        def _(i):
            at = pl.ds(pl.multiple_of(i * 16, 16), 16)
            in_s[0, at, :] = low(wide(in_s[0, at, :]) + wide(in_s[1, at, :]))

        for k in others:
            for part in (0, 1):
                home_far(c, k, part).wait_recv()
            together(local(far_in.at[c % 2, k - 1], in_s.at[1], fold_sem.at[1]))

            @pl.loop(0, rows // 16)
            def _(i):
                at = pl.ds(pl.multiple_of(i * 16, 16), 16)
                in_s[0, at, :] = low(wide(in_s[0, at, :]) + wide(in_s[1, at, :]))


    def drain_sum(c):
        for q in range(half):
            swap_copy(c, q).wait_send()
        for k in others:
            up_copy(c, k).wait_send()
            down_copy(c, k).wait_send()
            for part in (0, 1):
                home_far(c, k, part).wait_send()
        for part in (0, 1):
            home_near(c, part).wait_send()

    def fetch(c, at):
        q, side, slot = at // 2, at % 2, at % 2
        r = side * half + q

        @pl.when(side == 1)
        def _():
            core_copy(c, q).wait_recv()

        rows_at = pl.ds(pl.multiple_of(column(c) * rows, rows), rows)
        @pl.when(r == 0)
        def _():
            local(mine_ref.at[c], in_s.at[slot, :, x_part], x_sem.at[slot]).start()

        @pl.when(r > 0)
        def _():
            source = gather_ref.at[c % ring, jnp.maximum(r - 1, 0)]
            local(source, in_s.at[slot, :, x_part], x_sem.at[slot]).start()

        for place, cot_ref in enumerate(cot_refs):

            @pl.when(r == place)
            def _():
                local(cot_ref.at[rows_at], in_s.at[slot, :, y_part], c_sem.at[slot]).start()


    def fetched(slot):
        local(mine_ref.at[0], in_s.at[slot, :, x_part], x_sem.at[slot]).wait()
        local(cot_refs[0].at[pl.ds(0, rows)], in_s.at[slot, :, y_part], c_sem.at[slot]).wait()

    def load(e, slot):
        return local(acc_ref.at[e], acc_s.at[slot], load_sem.at[slot])

    def store(e, slot):
        return local(acc_s.at[slot], acc_ref.at[e], store_sem.at[slot])

    @pl.when((j == 0) & (s == 0))
    def _():
        barrier = pltpu.get_barrier_semaphore()
        peers = [("dp", core_id), ("dp", inner_id)] + [("dp", outer_id(k)) for k in others]
        peers += [("tensor", (z + k) % chunks) for k in range(1, chunks)]
        for axis, where in peers:
            pl.semaphore_signal(
                barrier, inc=1, device_id={axis: where}, device_id_type=pl.DeviceIdType.MESH
            )
        pl.semaphore_wait(barrier, len(peers))
        ring_copy(0).start()
        together(local(own_ref, in_s.at[0, :, x_part], fold_sem.at[0]))
        together(local(in_s.at[0, :, x_part], mine_ref.at[chunks - 1], fold_sem.at[0]))
        ring_copy(0).wait_recv()
        for k in range(1, chunks - 1):
            ring_copy(k).start()
        first_hop(0)
        fetch(0, 0)
        second_hop(0)

    @pl.when((s == 0) & (j > 0))
    def _():
        load(0, 0).start()

    @pl.when((j == 0) & (s == 4))
    def _():
        third_hop(0)
        if chunks > 2:
            ring_copy(1).wait_recv()
        first_hop(1)

    @pl.when((s == blocks + experts) & (j + 1 < chunks))
    def _():
        third_hop(j + 1)

    @pl.when((s == blocks + 2) & (j >= 1))
    def _():
        fold_halves(j - 1)

    @pl.when((s == blocks + 2) & (j + 1 < chunks))
    def _():
        second_hop(j + 1)

    @pl.when((s == blocks + 2) & (j + 3 < chunks))
    def _():
        ring_copy(j + 2).wait_recv()

    @pl.when((s == blocks + 2) & (j + 2 < chunks))
    def _():
        first_hop(j + 2)

    @pl.when(s == blocks + 3)
    def _():
        drain_gather(j)

    @pl.when((s == blocks + experts + half - 1) & (j >= 1))
    def _():
        fold_home(j - 1)
        together(local(in_s.at[0], ring_out.at[j - 1], fold_sem.at[0]))
        last_copy(j - 1).start()
        drain_sum(j - 1)

    @pl.when(s < blocks)
    def _():
        slot = s % 2

        @pl.when(s + 1 < blocks)
        def _():
            fetch(j, s + 1)

        fetched(slot)
        meta = in_s[slot, :, width:full]
        picks = (dot_nt(pick_ref[...], meta) == 0.0).astype(jnp.bfloat16)
        at = pl.multiple_of(s * slots, slots)
        got = low(dot_nn(picks, in_s[slot, :, :full]))
        cot = low(dot_nn(picks, in_s[slot, :, full:]))
        for e in range(experts):
            part = slice(e * slots, (e + 1) * slots)
            rows_s[e, pl.ds(at, slots), :] = got[part, :width]
            mrow_s[e, pl.ds(at, slots), :] = got[part, width:]
            crow_s[e, pl.ds(at, slots), :] = cot[part]
        meta_s[s] = meta

    @pl.when((s >= blocks) & (s < blocks + experts))
    def _():
        e = s - blocks
        slot = e % 2
        tile = largest_tile(total, 320, 16)
        expert = me * experts + e
        wg = wg_ref[0]
        wu = wu_ref[0]
        wd = wd_ref[0]

        @pl.loop(0, total // tile)
        def _(m):
            ds = pl.ds(pl.multiple_of(m * tile, tile), tile)
            picked_rows = rows_s[e, ds, :]
            gate = dot_nn(picked_rows, wg)
            up = dot_nn(picked_rows, wu)
            grad_act = dot_nt(crow_s[e, ds, :], wd)
            meta = wide(mrow_s[e, ds, :])
            column = lax.broadcasted_iota(jnp.int32, meta.shape, 1)
            wanted = (column == expert) | (column == expert + all_experts)
            weight = jnp.sum(jnp.where(wanted, meta, 0.0), axis=1, keepdims=True)
            sig = jax.nn.sigmoid(gate)
            silu = gate * sig
            act = silu * up
            g_pick = jnp.sum(act * grad_act, axis=1, keepdims=True)
            scaled = weight * grad_act
            aw_s[ds, :] = low(weight * act)
            gg_s[ds, :] = low(scaled * up * sig * (1.0 + gate * (1.0 - sig)))
            gu_s[ds, :] = low(scaled * silu)
            mrow_s[e, ds, :] = low(jnp.where(column == expert, g_pick, 0.0))

        @pl.when(e >= 1)
        def _():
            store(e - 1, 1 - slot).wait()

        @pl.when(j == 0)
        def _():
            acc_s[slot] = jnp.zeros(acc_s.shape[1:], jnp.float32)

        @pl.when(j > 0)
        def _():
            load(e, slot).wait()

            @pl.when(e + 1 < experts)
            def _():
                load(e + 1, 1 - slot).start()

        cols = largest_tile(width, 512, 128)
        for which, (left, right) in enumerate(((gg_s, rows_s), (gu_s, rows_s), (aw_s, crow_s))):
            turn_s[...] = left[...].T

            @pl.loop(0, width // cols)
            def _(n):
                ds = pl.ds(pl.multiple_of(n * cols, cols), cols)
                add = dot_nn(turn_s[...], right[e, :, ds])
                acc_s[slot, which, :, ds] = acc_s[slot, which, :, ds] + add

        store(e, slot).start()

        @pl.loop(0, total // tile)
        def _(m):
            ds = pl.ds(pl.multiple_of(m * tile, tile), tile)
            crow_s[e, ds, :] = low(dot_nn(aw_s[ds, :], wd))
            rows_s[e, ds, :] = low(dot_nt(gg_s[ds, :], wg) + dot_nt(gu_s[ds, :], wu))

    first = blocks + experts

    def written(c, o):
        q, slot = half - 1 - o % half, o % 2

        @pl.when(o < half)
        def _():
            local(out_s.at[slot], other_ref.at[c % 2, q], out_sem.at[slot]).wait()
            swap_copy(c, q).start()

        @pl.when(o >= half)
        def _():
            local(out_s.at[slot], both_ref.at[c % 2, q], out_sem.at[slot]).wait()

        for k in others:

            @pl.when((o >= half) & (q == 2 * k + 1))
            def _():
                up_copy(c, k).start()
                down_copy(c, k).start()

            @pl.when((o >= half) & (q == 2 * k))
            def _():
                home_far(c, k, 0).start()

        @pl.when((o >= half) & (q == 1))
        def _():
            home_near(c, 1).start()

    @pl.when(s >= first)
    def _():
        o = s - first
        slot = o % 2
        q = half - 1 - o % half
        side = 1 - o // half
        place = 2 * q + side
        at = pl.multiple_of(place * slots, slots)

        @pl.when(o >= 1)
        def _():
            written(j, o - 1)

        @pl.when((o >= half - 1) & (o < 2 * half - 1))
        def _():
            coming = half - 1 - (o + 1) % half
            swap_copy(j, coming).wait_recv()
            local(core_in.at[j % 2, coming], in_s.at[1 - slot], x_sem.at[1 - slot]).start()

        @pl.when(o >= half)
        def _():
            local(core_in.at[j % 2, q], in_s.at[slot], x_sem.at[slot]).wait()

        @pl.when(o < half)
        def _():
            in_s[slot] = jnp.zeros((rows, span), jnp.bfloat16)

        picks = (dot_nt(meta_s[place], pick_ref[...]) == 0.0).astype(jnp.bfloat16)
        flat = (experts * slots, width)
        g = dot_nn(picks, rows_s[:, pl.ds(at, slots), :].reshape(flat))
        out_s[slot, :, :width] = low(g + wide(in_s[slot, :, :width]))
        flat = (experts * slots, extra)
        p = dot_nn(picks, mrow_s[:, pl.ds(at, slots), :].reshape(flat))
        out_s[slot, :, width:full] = low(p + wide(in_s[slot, :, width:full]))
        flat = (experts * slots, width)
        y = dot_nn(picks, crow_s[:, pl.ds(at, slots), :].reshape(flat))
        out_s[slot, :, full:] = low(y + wide(in_s[slot, :, full:]))

        @pl.when(o < half)
        def _():
            local(out_s.at[slot], other_ref.at[j % 2, q], out_sem.at[slot]).start()

        @pl.when(o >= half)
        def _():
            local(out_s.at[slot], both_ref.at[j % 2, q], out_sem.at[slot]).start()

        @pl.when(s == steps - 1)
        def _():
            written(j, o)
            store(experts - 1, (experts - 1) % 2).wait()

        @pl.when((s == steps - 1) & (j + 1 < chunks))
        def _():
            fetch(j + 1, 0)

    @pl.when((s == steps - 1) & (j == chunks - 1))
    def _():
        fold_halves(chunks - 1)
        fold_home(chunks - 1)
        drain_sum(chunks - 1)
        for k in range(chunks - 1):
            last_copy(k).wait_recv()
            together(local(ring_in.at[k], in_s.at[1], fold_sem.at[1]))

            @pl.loop(0, rows // 16)
            def _(i):
                at = pl.ds(pl.multiple_of(i * 16, 16), 16)
                in_s[0, at, :] = low(wide(in_s[0, at, :]) + wide(in_s[1, at, :]))

        together(local(in_s.at[0], final_ref, fold_sem.at[0]))
        for k in range(chunks - 1):
            last_copy(k).wait_send()
            ring_copy(k).wait_send()


def moe(own, cot, picks, wg, wu, wd, outer, chunks, slots, all_experts):
    rows, full = own.shape
    width = cot[0].shape[1]
    extra = full - width
    span = full + width
    experts, _, hidden = wg.shape
    blocks, half, cut = 4 * outer, 2 * outer, rows // 2
    total = blocks * slots
    sizes = (outer, chunks, experts, slots, rows, width, extra, all_experts)

    def expert_at(j, s):
        return (jnp.clip(s - blocks, 0, experts - 1), 0, 0)

    anywhere = pl.BlockSpec(memory_space=pl.ANY)
    in_specs = [
        *[anywhere] * (1 + len(cot)),
        pl.BlockSpec(picks.shape, lambda j, s: (0, 0)),
        pl.BlockSpec((1, width, hidden), expert_at),
        pl.BlockSpec((1, width, hidden), expert_at),
        pl.BlockSpec((1, hidden, width), expert_at),
    ]
    bf16 = jnp.bfloat16
    shapes = [
        ((rows, span), bf16),
        ((experts, 3, hidden, width), jnp.float32),
        ((chunks, rows, full), bf16),
        ((chunks if chunks <= 4 else 3, blocks - 1, rows, full), bf16),
        ((2, half, rows, span), bf16),
        ((2, half, rows, span), bf16),
        ((2, half, rows, span), bf16),
        ((2, outer - 1, cut, span), bf16),
        ((2, outer - 1, cut, span), bf16),
        ((2, rows, span), bf16),
        ((2, outer - 1, rows, span), bf16),
        ((chunks - 1, rows, span), bf16),
        ((chunks - 1, rows, span), bf16),
    ]
    dma = pltpu.SemaphoreType.DMA
    gathers, sums = 5 * outer - 2, 6 * outer - 2
    scratch = [
        pltpu.VMEM((2, rows, span), bf16),
        pltpu.VMEM((2, rows, span), bf16),
        pltpu.VMEM((experts, total, width), bf16),
        pltpu.VMEM((experts, total, width), bf16),
        pltpu.VMEM((experts, total, extra), bf16),
        pltpu.VMEM((blocks, rows, extra), bf16),
        pltpu.VMEM((total, hidden), bf16),
        pltpu.VMEM((total, hidden), bf16),
        pltpu.VMEM((total, hidden), bf16),
        pltpu.VMEM((hidden, total), bf16),
        pltpu.VMEM((2, 3, hidden, width), jnp.float32),
        dma((2,)),
        dma((2,)),
        dma((2,)),
        dma((2,)),
        dma((2,)),
        dma((4,)),
        dma((chunks, gathers)),
        dma((chunks, gathers)),
        dma((chunks, sums)),
        dma((chunks, sums)),
        dma((chunks,)),
        dma((chunks,)),
        dma((chunks,)),
        dma((chunks,)),
    ]
    flops = 2 * chunks * experts * total * width * (hidden * 9 + 4 * rows)
    results = pl.pallas_call(
        functools.partial(moe_kernel, sizes),
        grid=(chunks, 2 * blocks + experts),
        in_specs=in_specs,
        out_specs=[anywhere] * len(shapes),
        out_shape=[jax.ShapeDtypeStruct(*shape) for shape in shapes],
        scratch_shapes=scratch,
        compiler_params=pltpu.CompilerParams(
            dimension_semantics=("arbitrary", "arbitrary"),
            vmem_limit_bytes=66_500_000,
            collective_id=0,
            has_side_effects=True,
        ),
        cost_estimate=pl.CostEstimate(
            flops=flops, bytes_accessed=blocks * chunks * rows * full * 8, transcendentals=0
        ),
        name="moe",
    )(own, *cot, picks, wg, wu, wd)
    return results[:2]


def wide(values):
    return values.astype(jnp.float32)


def low(values):
    return values.astype(jnp.bfloat16)


def tie(*values):
    return lax.optimization_barrier(values)


def ring_sum(values, count):
    total = values
    for step in range(1, count):
        pairs = [(i, (i + step) % count) for i in range(count)]
        total = total + lax.ppermute(values, "tensor", pairs)
    return total


def pick(values, at, axis):
    return lax.dynamic_index_in_dim(values, at, axis, keepdims=False)


class Plane:
    def __init__(self, count):
        self.outer = count // 4
        everyone = range(count)
        self.core = [(i, i ^ 1) for i in everyone]
        self.inner = [(i, i ^ 2) for i in everyone]
        self.count = count

    def pull(self, values, k):
        pairs = [((i + 4 * k) % self.count, i) for i in range(self.count)]
        return lax.ppermute(values, "dp", pairs)

    def swap_inner(self, values):
        return lax.ppermute(values, "dp", self.inner)

    def swap_core(self, values):
        return lax.ppermute(values, "dp", self.core)

    def push(self, values, k):
        pairs = [(i, (i + 4 * k) % self.count) for i in range(self.count)]
        return lax.ppermute(values, "dp", pairs)

    def fold_inner(self, parts, b, axis, kind):
        given = self.swap_inner(pick(parts, 1 - b, axis).astype(kind))
        return wide(pick(parts, b, axis)) + wide(given)

    def fold_outer(self, parts, a, kind):
        total = wide(pick(parts, a, 0))
        for k in range(1, self.outer):
            given = pick(parts, (a + k) % self.outer, 0).astype(kind)
            total = total + wide(self.push(given, k))
        return total

    def scatter(self, values, inner_first):
        kind = values.dtype
        return self.scatter_rest(self.fold_core(values), kind, inner_first)

    def fold_core(self, values):
        core = lax.axis_index("dp") % 2
        parts = values.reshape(self.outer, 2, 2, values.shape[0] // self.count, values.shape[1])
        given = self.swap_core(pick(parts, 1 - core, 2))
        return (wide(pick(parts, core, 2)) + wide(given)).astype(values.dtype)

    def scatter_rest(self, parts, kind, inner_first):
        index = lax.axis_index("dp")
        b, a = index // 2 % 2, index // 4
        if inner_first:
            return self.fold_outer(self.fold_inner(parts, b, 1, kind).astype(kind), a, kind)
        return self.fold_inner(self.fold_outer(parts, a, kind).astype(kind), b, 0, kind)

    def first(self, own):
        return self.swap_inner(own), [self.pull(own, k) for k in range(1, self.outer)]

    def second(self, near, fars):
        half = near.shape[0] // 2
        return [
            jnp.concatenate([self.pull(near[:half], k + 1), self.swap_inner(far[half:])], axis=0)
            for k, far in enumerate(fars)
        ]

    def third(self, own, near, fars, diagonals, swapped):
        mine = [own, near]
        for far, diagonal in zip(fars, diagonals):
            mine += [far, diagonal]
        other = swapped[:2]
        for far, diagonal in zip(swapped[2:], diagonals):
            other += [far, self.swap_core(diagonal)]
        return mine + other


def per_device(
    tokens,
    lengths,
    routes,
    attn_gain,
    w_query,
    w_key,
    w_value,
    w_out,
    q_gain,
    k_gain,
    ffn_gain,
    router_weight,
    w_gate,
    w_up,
    w_down,
    cotangent,
):
    tensor_count = lax.axis_size("tensor")
    data_count = lax.axis_size("dp")
    tensor_rank = lax.axis_index("tensor")
    block_rows = tokens.shape[1]
    width = tokens.shape[2]
    full_length = block_rows * tensor_count
    route_count = routes.shape[2]
    local_experts = w_gate.shape[0]
    all_experts = local_experts * data_count
    head_dim = q_gain.shape[0]
    local_width = w_query.shape[1]
    capacity = max(2, (block_rows * route_count * 5 + 4 * all_experts - 1) // (4 * all_experts))
    query_rows = min(512, full_length)
    scale = head_dim ** (-0.5)
    own_start = tensor_rank * block_rows
    token_values = tokens[0].astype(jnp.float32)
    seq_length = lengths[0]
    own_valid = (own_start + jnp.arange(block_rows) < seq_length).astype(jnp.float32)
    key_valid = jnp.arange(full_length) < seq_length
    normed = rms_scale(token_values, attn_gain).astype(jnp.bfloat16)
    gathered = lax.all_gather(normed, "tensor", axis=0, tiled=True)
    plane = Plane(data_count)
    near, fars = plane.first(cotangent[0])
    core = lax.axis_index("dp") % 2
    depth = width // 2
    out_half = lax.dynamic_slice_in_dim(w_out, core * depth, depth, 0)
    gathered, near, fars, out_half = tie(gathered, near, fars, out_half)
    out_mine = lax.all_gather(out_half, "tensor", axis=0)
    query_unrotated = jnp.dot(gathered, w_query, preferred_element_type=jnp.float32)
    key_raw = jnp.dot(gathered, w_key, preferred_element_type=jnp.float32)
    value_raw = jnp.dot(gathered, w_value, preferred_element_type=jnp.float32)
    query_low = prepare(query_unrotated, q_gain).astype(jnp.bfloat16)
    key_low = prepare(key_raw, k_gain).astype(jnp.bfloat16)
    value_low = value_raw.astype(jnp.bfloat16).reshape(full_length, -1, head_dim)

    def block_scores(query_block):
        scores = (
            jnp.einsum("qhd,khd->hqk", query_block, key_low, preferred_element_type=jnp.float32)
            * scale
        )
        return jnp.where(key_valid[None, None, :], scores, NEG)

    mixed_parts = []
    log_totals = []
    for start in range(0, full_length, query_rows):
        scores = block_scores(query_low[start : start + query_rows])
        row_peak = jnp.max(scores, axis=-1, keepdims=True)
        powers = jnp.exp(scores - row_peak)
        total = jnp.sum(powers, axis=-1, keepdims=True)
        weights = (powers / total).astype(jnp.bfloat16)
        mixed_parts.append(
            jnp.einsum("hqk,khd->qhd", weights, value_low, preferred_element_type=jnp.float32)
        )
        log_totals.append(row_peak + jnp.log(total))
    attended = (
        jnp.concatenate(mixed_parts, axis=0).reshape(full_length, local_width).astype(jnp.bfloat16)
    )
    diagonals = plane.second(near, fars)
    swapped = [plane.swap_core(part) for part in (cotangent[0], near, *fars)]
    attended, diagonals, swapped = tie(attended, diagonals, swapped)
    cot_all = plane.third(cotangent[0], near, fars, diagonals, swapped)
    heads_own = lax.all_to_all(
        attended.reshape(tensor_count, block_rows, local_width), "tensor", 0, 0
    )
    heads_own, out_mine = tie(heads_own, out_mine)
    out_other = plane.swap_core(out_mine)
    heads_own = heads_own.reshape(tensor_count, block_rows, local_width)

    def from_heads(out_weight):
        return sum(dot_nt(heads_own[t], out_weight[t]) for t in range(tensor_count))

    attn_mine, attn_other = from_heads(out_mine), from_heads(out_other)
    attn_own = jnp.where(
        core == 0,
        jnp.concatenate([attn_mine, attn_other], axis=1),
        jnp.concatenate([attn_other, attn_mine], axis=1),
    )
    residual = token_values + own_valid[:, None] * attn_own
    moe_own = rms_scale(residual, ffn_gain).astype(jnp.bfloat16)
    router_logits = jnp.dot(moe_own, router_weight, preferred_element_type=jnp.float32)
    own_probs = jax.nn.softmax(router_logits, axis=-1)
    own_routes = lax.dynamic_slice_in_dim(routes[0], own_start, block_rows, 0)
    onehot = own_routes[:, :, None] == jnp.arange(all_experts)[None, None, :]
    named = jnp.any(onehot, axis=1) & (own_valid[:, None] > 0.0)
    named_low = named.astype(jnp.bfloat16)
    before = jnp.arange(block_rows)[:, None] > jnp.arange(block_rows)[None, :]
    order = jnp.dot(before.astype(jnp.bfloat16), named_low, preferred_element_type=jnp.float32)
    place = jnp.where(named, order, -1.0).astype(jnp.bfloat16)
    weight = jnp.where(named, own_probs, 0.0)
    weight_high = weight.astype(jnp.bfloat16)
    weight_low = (weight - weight_high.astype(jnp.float32)).astype(jnp.bfloat16)
    used = 3 * all_experts + 1
    extra = (used + 127) // 128 * 128
    meta = jnp.concatenate(
        [
            weight_high,
            weight_low,
            place,
            jnp.ones((block_rows, 1), jnp.bfloat16),
            jnp.zeros((block_rows, extra - used), jnp.bfloat16),
        ],
        axis=1,
    )
    slots = (capacity + 15) // 16 * 16
    first_expert = lax.axis_index("dp") * local_experts
    slot_row = jnp.arange(local_experts * slots)[:, None]
    slot_column = jnp.arange(extra)[None, :]
    picks = jnp.where(
        slot_column == 2 * all_experts + first_expert + slot_row // slots,
        1.0,
        jnp.where(slot_column == 3 * all_experts, -(slot_row % slots).astype(jnp.float32), 0.0),
    ).astype(jnp.bfloat16)
    packed = jnp.concatenate([moe_own, meta], axis=1)
    combined, sums = moe(
        packed,
        cot_all,
        picks,
        w_gate,
        w_up,
        w_down,
        data_count // 4,
        tensor_count,
        slots,
        all_experts,
    )
    combined = wide(combined)
    grad_moe = combined[:, :width]
    grad_probs = combined[:, width : width + all_experts]
    output = low(residual + combined[:, width + extra :])
    grad_own = lax.dynamic_slice_in_dim(cotangent[0], own_start, block_rows, 0).astype(jnp.float32)
    grad_logits = (
        own_probs * (grad_probs - jnp.sum(own_probs * grad_probs, axis=-1, keepdims=True))
    ).astype(jnp.bfloat16)
    grad_moe = grad_moe + jnp.einsum(
        "re,de->rd", grad_logits, router_weight, preferred_element_type=jnp.float32
    )
    router_part = jnp.einsum("rd,re->de", moe_own, grad_logits, preferred_element_type=jnp.float32)
    ffn_pull = jax.vjp(rms_scale, residual, ffn_gain)[1]
    grad_res_norm, ffn_part = ffn_pull(grad_moe)
    grad_residual = grad_own + grad_res_norm
    grad_attn = (grad_residual * own_valid[:, None]).astype(jnp.bfloat16)
    attn_lower = lax.dynamic_slice_in_dim(grad_attn, core * depth, depth, 1)
    attn_upper = lax.dynamic_slice_in_dim(grad_attn, depth - core * depth, depth, 1)
    grad_heads = jnp.stack(
        [
            low(dot_nn(attn_lower, out_mine[t]) + dot_nn(attn_upper, out_other[t]))
            for t in range(tensor_count)
        ]
    )
    grad_mixed = lax.all_to_all(grad_heads, "tensor", 0, 0)
    grad_mixed, grad_attn = tie(grad_mixed, grad_attn)
    grad_attn_all = lax.all_gather(grad_attn, "tensor", axis=0, tiled=True)
    grad_mixed = grad_mixed.reshape(full_length, -1, head_dim)
    grad_query_parts = []
    grad_keys = jnp.zeros(key_low.shape, jnp.float32)
    grad_values = jnp.zeros(value_low.shape, jnp.float32)
    for order, start in enumerate(range(0, full_length, query_rows)):
        query_block = query_low[start : start + query_rows]
        grad_block = grad_mixed[start : start + query_rows]
        probs_block = jnp.exp(block_scores(query_block) - log_totals[order])
        probs_low = probs_block.astype(jnp.bfloat16)
        grad_values = grad_values + jnp.einsum(
            "hqk,qhd->khd", probs_low, grad_block, preferred_element_type=jnp.float32
        )
        grad_probs_block = jnp.einsum(
            "qhd,khd->hqk", grad_block, value_low, preferred_element_type=jnp.float32
        )
        delta = jnp.sum(probs_block * grad_probs_block, axis=-1, keepdims=True)
        grad_scores = (probs_block * (grad_probs_block - delta)).astype(jnp.bfloat16)
        grad_query_parts.append(
            jnp.einsum("hqk,khd->qhd", grad_scores, key_low, preferred_element_type=jnp.float32)
            * scale
        )
        grad_keys = (
            grad_keys
            + jnp.einsum(
                "hqk,qhd->khd", grad_scores, query_block, preferred_element_type=jnp.float32
            )
            * scale
        )
    grad_queries = jnp.concatenate(grad_query_parts, axis=0)
    query_pull = jax.vjp(prepare, query_unrotated, q_gain)[1]
    grad_query_raw, q_part = query_pull(grad_queries)
    key_pull = jax.vjp(prepare, key_raw, k_gain)[1]
    grad_key_raw, k_part = key_pull(grad_keys)
    grad_q_low = grad_query_raw.astype(jnp.bfloat16)
    grad_k_low = grad_key_raw.astype(jnp.bfloat16)
    grad_v_low = grad_values.reshape(full_length, local_width).astype(jnp.bfloat16)
    query_part = jnp.einsum("ld,lh->dh", gathered, grad_q_low, preferred_element_type=jnp.float32)
    value_part = jnp.einsum("ld,lh->dh", gathered, grad_v_low, preferred_element_type=jnp.float32)
    from_query = jnp.einsum("lh,dh->ld", grad_q_low, w_query, preferred_element_type=jnp.float32)
    from_key = jnp.einsum("lh,dh->ld", grad_k_low, w_key, preferred_element_type=jnp.float32)
    from_value = jnp.einsum("lh,dh->ld", grad_v_low, w_value, preferred_element_type=jnp.float32)
    grad_gathered, grad_attn_all, sums, router_part, grad_k_late = tie(
        low(from_query + from_key + from_value), grad_attn_all, sums, router_part, grad_k_low
    )
    grad_normed = wide(
        lax.psum_scatter(grad_gathered, "tensor", scatter_dimension=0, tiled=True)
    )
    grad_gate = jnp.swapaxes(sums[:, 0], 1, 2)
    grad_up = jnp.swapaxes(sums[:, 1], 1, 2)
    grad_down = sums[:, 2]
    key_part = jnp.einsum("ld,lh->dh", gathered, grad_k_late, preferred_element_type=jnp.float32)
    key_part = plane.fold_core(low(key_part))
    key_part, grad_gate, grad_up, grad_down = tie(key_part, grad_gate, grad_up, grad_down)
    out_part = jnp.einsum("ld,lh->dh", grad_attn_all, attended, preferred_element_type=jnp.float32)
    attn_pull = jax.vjp(rms_scale, token_values, attn_gain)[1]
    grad_tok_norm, attn_part = attn_pull(grad_normed)
    grad_tokens = (grad_residual + grad_tok_norm).astype(jnp.bfloat16)
    grad_out = plane.scatter(low(out_part), True)
    grad_value = plane.scatter(low(value_part), False)
    grad_query = plane.scatter(low(query_part), True)
    grad_key = plane.scatter_rest(key_part, key_part.dtype, False)
    routing = plane.scatter(jnp.concatenate([router_part, ffn_part[:, None]], axis=1), False)
    routing = ring_sum(routing, tensor_count)
    parts = [v.reshape(data_count, -1) for v in (attn_part, q_part, k_part)]
    gains = jnp.repeat(jnp.concatenate(parts, axis=1), tensor_count, axis=0)
    gains = jnp.sum(lax.all_to_all(gains, ("dp", "tensor"), 0, 0, tiled=True), axis=0)
    piece = width // data_count
    last = piece + head_dim // data_count
    return (
        output[None],
        grad_tokens[None],
        gains[:piece],
        grad_query,
        grad_key,
        grad_value,
        grad_out,
        gains[piece:last],
        gains[last:],
        routing[:, all_experts],
        routing[:, :all_experts],
        grad_gate,
        grad_up,
        grad_down,
    )


def solution(mesh):
    return jax.shard_map(
        per_device,
        mesh=mesh,
        in_specs=(
            P("dp", "tensor", None),
            P("dp"),
            P("dp", None, None),
            P(),
            P(None, "tensor"),
            P(None, "tensor"),
            P(None, "tensor"),
            P(None, "tensor"),
            P(),
            P(),
            P(),
            P(),
            P("dp", None, "tensor"),
            P("dp", None, "tensor"),
            P("dp", "tensor", None),
            P("dp", None, None),
        ),
        out_specs=(
            P("dp", "tensor", None),
            P("dp", "tensor", None),
            P("dp"),
            P("dp", "tensor"),
            P("dp", "tensor"),
            P("dp", "tensor"),
            P("dp", "tensor"),
            P("dp"),
            P("dp"),
            P("dp"),
            P("dp", None),
            P("dp", None, "tensor"),
            P("dp", None, "tensor"),
            P("dp", "tensor", None),
        ),
        check_vma=False,
    )
```
